32 devices in a mesh: space: 2 (over y), filt: 4 (over x, core), rep: 4 (over z).
Axes of the slice: x: 2, y: 2, z: 4, core: 2. Of those that a mesh axis runs over, the one named last changes fastest.
Arguments:
- volume: bfloat16 [4, 64, 8, 8, 128], P('rep', 'filt', 'space'), may hold values from -6 to 6
- weight1: bfloat16 [64, 64, 3, 3, 3], P('filt'), may hold values from -0.15625 to 0.15625
- bias1: float32 [64], P('filt'), may hold values from -3 to 3
- weight2: bfloat16 [64, 64, 3, 3, 3], P('filt'), may hold values from -0.15625 to 0.15625
- bias2: float32 [64], P('filt'), may hold values from -3 to 3
- upstream: bfloat16 [4, 64, 8, 8, 128], P('rep', 'filt', 'space'), may hold values from -6 to 6
Outputs:
- output: bfloat16 [4, 64, 8, 8, 128], P('rep', 'filt', 'space')
- volume_grad: bfloat16 [4, 64, 8, 8, 128], P('rep', 'filt', 'space')
- weight_grad1: float32 [64, 64, 3, 3, 3], P('filt')
- bias_grad1: float32 [64], P('filt')
- weight_grad2: float32 [64, 64, 3, 3, 3], P('filt')
- bias_grad2: float32 [64], P('filt')
The draws below stay inside these ranges and needn't reach their ends.
All inputs are finite; a program needn't handle non-finite values.
Results may differ from the reference program's by a relative error of at most 0.0058.
Values may be sent and summed in bfloat16 or wider, within the bound.
No kernel may reach another device: no remote copies, remote signals or barrier semaphores. Data moves between devices by JAX's collectives and lax.ppermute only.
A program may use at most 64 MiB of HBM per device.

```python
import math
import jax
import jax.numpy as jnp
from jax import lax

C = 64
NY = 8
NZ = 128
NX = 8
SAMPLES = 4


def block_levels(own_key, dims, split, smallest, high):
    def one(dim, parts):
        heights = jax.random.uniform(jax.random.fold_in(jax.random.fold_in(own_key, 6), dim), (parts,), jnp.float32, smallest / len(split), high / len(split))
        return jnp.repeat(jnp.exp(heights), dims[dim] // parts).reshape((-1,) + (1,) * (len(dims) - dim - 1))

    gain = one(*split[0])
    for cut in split[1:]:
        gain = gain * one(*cut)
    return gain


def noise(key, shape, deviation, most, pieces=(), kind=jnp.bfloat16):
    result = jax.random.normal(key, shape, jnp.float32) * deviation
    if len(pieces) > 0:
        result = block_levels(key, shape, pieces, -0.22, 0.18) * result
    return jnp.clip(result, min=-most, max=most).astype(kind)


def setup_inputs(seed: int = 0) -> dict:
    seeds = jax.random.split(jax.random.key(seed), 7)
    return {
        "volume": noise(seeds[0], (SAMPLES, C, NX, NY, NZ), 1.0, 6.0, ((0, 4), (1, 4), (2, 2))),
        "weight1": noise(seeds[1], (C, C, 3, 3, 3), (27 * C) ** -0.5, 0.15625, ((0, 4),)),
        "bias1": noise(seeds[2], (C,), 0.5, 3.0, ((0, 4),), jnp.float32),
        "weight2": noise(seeds[3], (C, C, 3, 3, 3), (27 * C) ** -0.5, 0.15625, ((0, 4),)),
        "bias2": noise(seeds[4], (C,), 0.5, 3.0, ((0, 4),), jnp.float32),
        "upstream": noise(seeds[5], (SAMPLES, C, NX, NY, NZ), 1.0, 6.0, ((0, 4), (1, 4), (2, 2))),
    }


SLOPE = 0.3
NUMBERS = ('NCDHW', 'OIDHW', 'NCDHW')

def smooth(values):
    return SLOPE * values + (1.0 - SLOPE) * jax.nn.softplus(values)

def smooth_slope(values):
    return SLOPE + (1.0 - SLOPE) * jax.nn.sigmoid(values)

def conv_same(field, kernel):
    return lax.conv_general_dilated(field, kernel, (1, 1, 1), ((1, 1), (1, 1), (1, 1)), dimension_numbers=NUMBERS, precision=lax.Precision.HIGHEST, preferred_element_type=jnp.float32)

def flipped_kernel(kernel):
    return jnp.transpose(jnp.flip(kernel, (2, 3, 4)), (1, 0, 2, 3, 4))

def layer_grads(field, delta, scale):
    padded = jnp.pad(field.astype(jnp.float32), ((0, 0), (0, 0), (1, 1), (1, 1), (1, 1)))
    left = jnp.transpose(padded, (1, 0, 2, 3, 4))
    right = jnp.transpose(delta.astype(jnp.float32), (1, 0, 2, 3, 4))
    product = lax.conv_general_dilated(left, right, (1, 1, 1), ((0, 0), (0, 0), (0, 0)), dimension_numbers=NUMBERS, precision=lax.Precision.HIGHEST, preferred_element_type=jnp.float32)
    weight_part = jnp.transpose(product, (1, 0, 2, 3, 4)) * scale
    bias_part = lax.optimization_barrier(jnp.sum(delta.astype(jnp.float32), axis=(0, 2, 3, 4))) * scale
    return (weight_part, bias_part)

def reference(volume, weight1, bias1, weight2, bias2, upstream):
    first_kernel = weight1.astype(jnp.float32)
    second_kernel = weight2.astype(jnp.float32)
    scale = 1.0 / math.sqrt(SAMPLES * NX * NY * NZ)
    first_pre = conv_same(volume.astype(jnp.float32), first_kernel) + bias1[None, :, None, None, None]
    hidden = smooth(first_pre).astype(jnp.bfloat16)
    second_pre = conv_same(hidden.astype(jnp.float32), second_kernel) + bias2[None, :, None, None, None]
    output = smooth(second_pre).astype(jnp.bfloat16)
    second_delta = (upstream.astype(jnp.float32) * smooth_slope(second_pre)).astype(jnp.bfloat16)
    weight_grad2, bias_grad2 = layer_grads(hidden, second_delta, scale)
    hidden_grad = conv_same(second_delta.astype(jnp.float32), flipped_kernel(second_kernel))
    first_delta = (hidden_grad * smooth_slope(first_pre)).astype(jnp.bfloat16)
    weight_grad1, bias_grad1 = layer_grads(volume, first_delta, scale)
    volume_grad = conv_same(first_delta.astype(jnp.float32), flipped_kernel(first_kernel)).astype(jnp.bfloat16)
    return (output, volume_grad, weight_grad1, bias_grad1, weight_grad2, bias_grad2)
```

```python
import functools
import math

import jax
import jax.numpy as jnp
from jax import lax
from jax.experimental import pallas as pl
from jax.experimental.pallas import tpu as pltpu
from jax.sharding import PartitionSpec as P

SLOPE = 0.3
BF = jnp.bfloat16
F32 = jnp.float32
VM = pltpu.VMEM
ANY = pl.BlockSpec(memory_space=pl.ANY)
WHOLE = pl.BlockSpec(memory_space=pltpu.VMEM)


def call(kernel, outs, n_any, n_vmem, scratch=(), flops=0, moved=0, name=None):
    return pl.pallas_call(
        kernel,
        out_shape=outs,
        in_specs=[ANY] * n_any + [WHOLE] * n_vmem,
        out_specs=jax.tree.map(lambda _: WHOLE, outs),
        scratch_shapes=list(scratch),
        compiler_params=pltpu.CompilerParams(vmem_limit_bytes=40 << 20),
        cost_estimate=pl.CostEstimate(flops=flops, bytes_accessed=moved, transcendentals=0),
        name=name,
    )


def shape(dims, kind):
    return jax.ShapeDtypeStruct(tuple(dims), kind)


def parts(values):
    e = jnp.exp(-jnp.abs(values))
    one = 1.0 + e
    soft = jnp.maximum(values, 0.0) + jnp.log(one)
    sig = jnp.where(values >= 0.0, 1.0, e) / one
    return SLOPE * values + (1.0 - SLOPE) * soft, SLOPE + (1.0 - SLOPE) * sig


def slope_of(values):
    e = jnp.exp(-jnp.abs(values))
    return SLOPE + (1.0 - SLOPE) * (jnp.where(values >= 0.0, 1.0, e) / (1.0 + e))


def smooth(values):
    e = jnp.exp(-jnp.abs(values))
    soft = jnp.maximum(values, 0.0) + jnp.log(1.0 + e)
    return SLOPE * values + (1.0 - SLOPE) * soft


def swap(block):
    return jnp.transpose(block.astype(F32), (1, 0, 2))


def pack_field(f_ref, o_ref):
    for x in range(f_ref.shape[1]):
        o_ref[x] = swap(f_ref[:, x]).astype(BF)


def pack_weight(w_ref, b_ref, o_ref):
    group, chan = w_ref.shape[1], w_ref.shape[2]
    for pair in range(5):
        for kz in range(3):
            low = w_ref[6 * pair + kz]
            if pair < 4:
                high = w_ref[6 * pair + 3 + kz]
            else:
                high = jnp.zeros_like(low)
            o_ref[3 * pair + kz] = jnp.concatenate([low, high], axis=1)
    eye = lax.broadcasted_iota(jnp.int32, (group, group), 0) == lax.broadcasted_iota(
        jnp.int32, (group, group), 1
    )
    col = jnp.sum(jnp.where(eye, jnp.broadcast_to(b_ref[...], (group, group)), 0.0), axis=1, keepdims=True)
    col = jnp.broadcast_to(col, (group, 2 * chan))
    first = col.astype(BF)
    rest = col - first.astype(F32)
    second = rest.astype(BF)
    third = (rest - second.astype(F32)).astype(BF)
    lane = lax.broadcasted_iota(jnp.int32, (group, 2 * chan), 1)
    picked = jnp.where(lane == 0, first.astype(F32), jnp.where(lane == 1, second.astype(F32), third.astype(F32)))
    o_ref[15] = picked.astype(BF)


def pack_kernel(f_ref, w_ref, b_ref, of_ref, ow_ref):
    pack_weight(w_ref, b_ref, ow_ref)
    pack_field(f_ref, of_ref)


def pack(field, weight, bias):
    group, layers, ny, nz = field.shape
    chan = weight.shape[1]
    taps = jnp.transpose(weight, (2, 3, 4, 0, 1)).reshape(27, group, chan)
    return call(
        pack_kernel,
        (shape((layers, ny, group, nz), BF), shape((16, group, 2 * chan), BF)),
        0,
        3,
        moved=2 * field.size * 2,
        name="pack",
    )(field, taps, bias.reshape(1, group))


class Plan:
    def __init__(self, layers, ny, nz, chan, groups, spaces):
        self.layers, self.ny, self.nz, self.chan = layers, ny, nz, chan
        self.groups, self.spaces = groups, spaces
        self.group = chan // groups
        self.pair = spaces == 2
        self.window = (2 if self.pair else 3) * layers
        self.sides = 1 if self.pair else 2

    def start(self, reach):
        if self.pair:
            return lax.axis_index("space") * (self.layers - reach)
        return self.layers - reach

    def count(self, reach):
        return self.layers + self.sides * reach

    def own(self):
        return self.start(0)

    def inside(self, layer):
        if self.pair:
            return None
        at = (lax.axis_index("space") - 1) * self.layers + layer
        return jnp.logical_and(at >= 0, at < self.spaces * self.layers)

    def chan_at(self, flip):
        return pl.multiple_of((lax.axis_index("filt") ^ flip) * self.group, self.group)

    def padded(self):
        return (self.window + 2, self.ny + 2, self.chan, self.nz)


def flip_perm(value, flip):
    n = lax.axis_size("filt")
    return lax.ppermute(value, "filt", [(i, i ^ flip) for i in range(n)])


def over(value):
    return lax.ppermute(value, "space", [(0, 1), (1, 0)])


def up(value):
    n = lax.axis_size("space")
    return lax.ppermute(value, "space", [(i, i + 1) for i in range(n - 1)])


def down(value):
    n = lax.axis_size("space")
    return lax.ppermute(value, "space", [(i + 1, i) for i in range(n - 1)])


def gather_all(field, plan):
    if plan.pair and plan.groups == 4:
        half = plan.layers // 2
        x = flip_perm(field, 2)
        y = over(field)
        c = flip_perm(field, 1)
        d0 = over(x[:half])
        d1 = flip_perm(y[half:], 2)
        xc = flip_perm(x, 1)
        yc = flip_perm(y, 1)
        e0 = flip_perm(d0, 1)
        e1 = flip_perm(d1, 1)
        return [
            (field, "own", 0, 0),
            (c, "own", 0, 1),
            (x, "own", 0, 2),
            (xc, "own", 0, 3),
            (y, "other", 0, 0),
            (yc, "other", 0, 1),
            (d0, "other", 0, 2),
            (d1, "other", half, 2),
            (e0, "other", 0, 3),
            (e1, "other", half, 3),
        ]
    out = []
    for flip in range(plan.groups):
        mine = flip_perm(field, flip) if flip else field
        out.append((mine, "own", 0, flip))
        if plan.pair:
            out.append((over(mine), "other", 0, flip))
        else:
            out.append((up(mine), "low", 0, flip))
            out.append((down(mine), "high", 0, flip))
    return out


def gather_halo(field, plan):
    out = []
    if plan.pair:
        s = lax.axis_index("space")
        edge = lax.dynamic_slice_in_dim(field, (1 - s) * (plan.layers - 2), 2, axis=0)
        halos = [(over(edge), "halo")]
    else:
        halos = [(up(field[plan.layers - 2 :]), "low"), (down(field[:2]), "high")]
    for value, place in [(field, "own")] + halos:
        if plan.groups == 4:
            x = flip_perm(value, 2)
            c = flip_perm(value, 1)
            xc = flip_perm(x, 1)
            flips = [value, c, x, xc]
        else:
            flips = [flip_perm(value, k) if k else value for k in range(plan.groups)]
        out += [(v, place, 0, k) for k, v in enumerate(flips)]
    return out


def gather_weight(packed, plan):
    if plan.groups == 4:
        x = flip_perm(packed, 2)
        c = flip_perm(packed, 1)
        xc = flip_perm(x, 1)
        return [packed, c, x, xc]
    return [flip_perm(packed, k) if k else packed for k in range(plan.groups)]


def field_place(plan, place, k):
    if plan.pair:
        s = lax.axis_index("space")
        return 1 + k + (s if place == "own" else 1 - s) * plan.layers
    return 1 + k + {"low": 0, "own": 1, "high": 2}[place] * plan.layers


def halo_place(plan, place):
    if plan.pair:
        s = lax.axis_index("space")
        return 2 * s if place == "own" else (1 - s) * plan.layers
    return {"low": 0, "own": 2, "high": plan.layers + 2}[place]


def load_weight(plan, refs, dst, sem, start):
    for flip, ref in enumerate(refs):
        copy = pltpu.make_async_copy(ref, dst.at[:, pl.ds(plan.chan_at(flip), plan.group), :], sem.at[flip])
        copy.start() if start else copy.wait()


def load_pieces(plan, refs, places, dst, sem, start, halo=False):
    for n, (ref, (place, k, flip)) in enumerate(zip(refs, places)):
        rows = pl.ds(plan.chan_at(flip), plan.group)
        if halo:
            target = dst.at[pl.ds(halo_place(plan, place), ref.shape[0]), :, rows, :]
        else:
            target = dst.at[pl.ds(field_place(plan, place, k), ref.shape[0]), pl.ds(1, plan.ny), rows, :]
        copy = pltpu.make_async_copy(ref, target, sem.at[n])
        copy.start() if start else copy.wait()


def zero_edges(plan, ref):
    zero = jnp.zeros(ref.shape[2:], ref.dtype)
    for x in (0, ref.shape[0] - 1):
        for y in range(ref.shape[1]):
            ref[x, y] = zero
    for x in range(1, ref.shape[0] - 1):
        ref[x, 0] = zero
        ref[x, ref.shape[1] - 1] = zero


def weight_matrix(w_ref, chan):
    cols = []
    for pair in range(5):
        block = w_ref[3 * pair : 3 * pair + 3].reshape(3 * chan, 2 * chan)
        cols.append(block if pair < 4 else block[:, :chan])
    return jnp.concatenate(cols, axis=1)


def bias_column(w_ref):
    rows = w_ref[15].astype(F32)
    return rows[:, 0:1] + rows[:, 1:2] + rows[:, 2:3]


def taps(field_ref, x, y):
    c, nz = field_ref.shape[2], field_ref.shape[3]
    rows = []
    for kx in range(3):
        first = field_ref[x + kx, y : y + 3].reshape(3 * c, nz)
        second = field_ref[x + kx, y + 1 : y + 4].reshape(3 * c, nz)
        rows.append(jnp.concatenate([first, second], axis=1))
    return jnp.concatenate(rows, axis=0)


def z_shift(values, by):
    nz = values.shape[1]
    lane = lax.broadcasted_iota(jnp.int32, values.shape, 1)
    if by > 0:
        return jnp.where(lane == 0, 0.0, pltpu.roll(values, 1, 1))
    return jnp.where(lane == nz - 1, 0.0, pltpu.roll(values, nz - 1, 1))


def z_sum(product, rows, half, nz):
    part = product[:, half * nz : (half + 1) * nz]
    return part[rows : 2 * rows] + z_shift(part[:rows], 1) + z_shift(part[2 * rows :], -1)


def conv_rows(weight, field_ref, x, each):
    ny, nz = field_ref.shape[1] - 2, field_ref.shape[3]
    rows = weight.shape[0] // 3
    for y in range(0, ny, 2):
        product = jnp.dot(weight, taps(field_ref, x, y), preferred_element_type=F32)
        for half in range(2):
            each(y + half, z_sum(product, rows, half, nz))


def first_kernel(plan, places, *refs):
    n = len(places)
    pieces, weights = refs[:n], refs[n : n + plan.groups]
    h_ref, s_ref, a_ref, w_ref, sem, wsem = refs[n + plan.groups :]
    load_weight(plan, weights, w_ref, wsem, True)
    load_pieces(plan, pieces, places, a_ref, sem, True)
    zero_edges(plan, a_ref)
    zero_edges(plan, h_ref)
    load_weight(plan, weights, w_ref, wsem, False)
    load_pieces(plan, pieces, places, a_ref, sem, False)
    start = plan.start(3)
    m_ref = weight_matrix(w_ref, plan.chan)
    bias = bias_column(w_ref)

    def body(t, carry):
        x = start + t
        inside = plan.inside(x)

        def each(y, value):
            act, slope = parts(value + bias)
            if inside is not None:
                act = jnp.where(inside, act, 0.0)
                slope = jnp.where(inside, slope, 0.0)
            h_ref[x + 1, y + 1] = act.astype(BF)
            s_ref[t, y] = slope

        conv_rows(m_ref, a_ref, x, each)
        return carry

    lax.fori_loop(0, plan.count(3), body, 0)


def grads(plan, d_ref, f_ref, sh_ref, acc_ref, g_ref):
    group, nz, ny, chan = plan.group, plan.nz, plan.ny, plan.chan
    rows = pl.ds(plan.chan_at(0), group)
    own = plan.own()
    zero = jnp.zeros((3 * group, nz), BF)

    def shift(t, total):
        sh_ref[t, 0] = zero
        sh_ref[t, ny + 1] = zero
        for y in range(ny):
            value = d_ref[own + t + 1, y + 1, rows, :].astype(F32)
            total = total + value
            sh_ref[t, y + 1] = jnp.concatenate([z_shift(value, -1), value, z_shift(value, 1)], axis=0).astype(BF)
        return total

    total = lax.fori_loop(0, plan.layers, shift, jnp.zeros((group, nz), F32))
    acc_ref[...] = jnp.zeros_like(acc_ref)

    def body(t, carry):
        x = own + t
        for y in range(0, ny, 2):
            left = jnp.concatenate(
                [
                    jnp.concatenate([sh_ref[t, y + 2 - ky], sh_ref[t, y + 3 - ky]], axis=1)
                    for ky in range(3)
                ],
                axis=0,
            )
            right = jnp.concatenate(
                [jnp.concatenate([f_ref[x + kx, y + 1], f_ref[x + kx, y + 2]], axis=1) for kx in range(3)],
                axis=0,
            )
            acc_ref[...] += lax.dot_general(
                left, right, (((1,), (1,)), ((), ())), preferred_element_type=F32
            )
        return carry

    lax.fori_loop(0, plan.layers, body, 0)
    n = 9 * group
    g_ref[0:n] = acc_ref[:, 0 : 2 * chan]
    last = acc_ref[:, 2 * chan :]
    g_ref[n : n + n // 2] = jnp.concatenate([last[: n // 2], last[n // 2 :]], axis=1)
    g_ref[n + n // 2 :] = jnp.broadcast_to(jnp.sum(total, axis=1, keepdims=True), (group, 2 * chan))


def second_kernel(plan, places, *refs):
    n = len(places)
    pieces, weights = refs[:n], refs[n : n + plan.groups]
    h_ref, d_ref, o_ref, g_ref, u_ref, w_ref, p_ref, sh_ref, acc_ref, sem, wsem = refs[n + plan.groups :]
    load_weight(plan, weights, w_ref, wsem, True)
    load_pieces(plan, pieces, places, u_ref, sem, True, halo=True)
    zero_edges(plan, d_ref)
    load_weight(plan, weights, w_ref, wsem, False)
    load_pieces(plan, pieces, places, u_ref, sem, False, halo=True)
    start = plan.start(2)
    m_ref = weight_matrix(w_ref, plan.chan)
    bias = bias_column(w_ref)

    def body(t, carry):
        x = start + t

        def each(y, value):
            pre = value + bias
            p_ref[t, y] = pre
            d_ref[x + 1, y + 1] = (u_ref[t, y].astype(F32) * slope_of(pre)).astype(BF)

        conv_rows(m_ref, h_ref, x, each)
        return carry

    lax.fori_loop(0, plan.count(2), body, 0)
    rows = pl.ds(plan.chan_at(0), plan.group)
    first = plan.own() - start
    for t in range(plan.layers):
        o_ref[:, t] = jnp.transpose(smooth(p_ref[first + t, :, rows, :]), (1, 0, 2)).astype(BF)
    grads(plan, d_ref, h_ref, sh_ref, acc_ref, g_ref)


def flipped_kernel(plan, *refs):
    chan = plan.chan
    weights = refs[: 2 * plan.groups]
    outs = refs[2 * plan.groups : 2 * plan.groups + 2]
    w_refs, sem = refs[2 * plan.groups + 2 : 2 * plan.groups + 4], refs[2 * plan.groups + 4]
    for go in (True, False):
        for k in range(2):
            load_weight(plan, weights[k * plan.groups : (k + 1) * plan.groups], w_refs[k], sem.at[k], go)
    for w_ref, out in zip(w_refs, outs):
        for kz in range(3):
            turned = [jnp.transpose(w_ref[3 * pair + 2 - kz].astype(F32), (1, 0)) for pair in range(5)]
            for pair in range(5):
                low = turned[4 - pair][:chan]
                if pair < 4:
                    block = jnp.concatenate([low, turned[3 - pair][chan:]], axis=1)
                    out[kz, :, 2 * chan * pair : 2 * chan * (pair + 1)] = block.astype(BF)
                else:
                    out[kz, :, 2 * chan * pair :] = low.astype(BF)


def third_kernel(plan, places, *refs):
    n = len(places)
    pieces = refs[:n]
    s_ref, d2_ref, t_ref, d_ref, g_ref, a_ref, sh_ref, acc_ref, sem = refs[n:]
    load_pieces(plan, pieces, places, a_ref, sem, True)
    zero_edges(plan, d_ref)
    zero_edges(plan, a_ref)
    start = plan.start(1)
    skip = start - plan.start(3)
    m_ref = t_ref[...].reshape(3 * plan.chan, 9 * plan.chan)

    def body(t, carry):
        x = start + t

        def each(y, value):
            d_ref[x + 1, y + 1] = (value * s_ref[skip + t, y]).astype(BF)

        conv_rows(m_ref, d2_ref, x, each)
        return carry

    lax.fori_loop(0, plan.count(1), body, 0)
    load_pieces(plan, pieces, places, a_ref, sem, False)
    grads(plan, d_ref, a_ref, sh_ref, acc_ref, g_ref)


def fourth_kernel(plan, d_ref, t_ref, o_ref, r_ref):
    own = plan.own()
    rows = pl.ds(plan.chan_at(0), plan.group)
    m_ref = t_ref[:, rows, :].reshape(3 * plan.group, 9 * plan.chan)

    def body(t, carry):
        def each(y, value):
            r_ref[t, y] = value

        conv_rows(m_ref, d_ref, own + t, each)
        return carry

    lax.fori_loop(0, plan.layers, body, 0)
    for t in range(plan.layers):
        o_ref[:, t] = jnp.transpose(r_ref[t], (1, 0, 2)).astype(BF)


def to_wire(values, rows):
    row = lax.broadcasted_iota(jnp.int32, values.shape, 0)
    lane = lax.broadcasted_iota(jnp.int32, values.shape, 1)
    high = values.astype(BF).astype(F32)
    second = jnp.logical_and(row >= rows, lane >= values.shape[1] // 2)
    return jnp.where(second, values - high, high).astype(BF)


def add_wire(values, wire, rows):
    got = wire.astype(F32)
    row = lax.broadcasted_iota(jnp.int32, values.shape, 0)
    return values + got + jnp.where(row >= rows, pltpu.roll(got, values.shape[1] // 2, 1), 0.0)


def wire_kernel(rows, a_ref, w_ref):
    w_ref[...] = to_wire(a_ref[...], rows)


def step_kernel(rows, a_ref, got_ref, o_ref, w_ref):
    total = add_wire(a_ref[...], got_ref[...], rows)
    o_ref[...] = total
    w_ref[...] = to_wire(total, rows)


def last_kernel(rows, group, scale, a_ref, got_ref, w_ref, b_ref):
    total = add_wire(a_ref[...], got_ref[...], rows) * scale
    n = 9 * group
    chan = total.shape[1] // 2
    w_ref[0:9] = total[:n, :chan].reshape(9, group, chan)
    w_ref[9:18] = total[:n, chan:].reshape(9, group, chan)
    tail = total[n : n + n // 2]
    w_ref[18:27] = jnp.concatenate([tail[:, :chan], tail[:, chan:]], axis=0).reshape(9, group, chan)
    col = total[rows:, :group]
    eye = lax.broadcasted_iota(jnp.int32, (group, group), 0) == lax.broadcasted_iota(
        jnp.int32, (group, group), 1
    )
    b_ref[...] = jnp.sum(jnp.where(eye, col, 0.0), axis=0, keepdims=True)


def rounds(plan):
    out = []
    for axis in ("space", "rep"):
        size, bit = lax.axis_size(axis), 1
        while bit < size:
            out.append((axis, bit))
            bit *= 2
    return out


def total_grads(part, plan, scale):
    rows = part.shape[0] - plan.group
    steps = rounds(plan)
    wire = call(functools.partial(wire_kernel, rows), shape(part.shape, BF), 0, 1, name="wire")(part)
    for n, (axis, bit) in enumerate(steps):
        got = lax.ppermute(wire, axis, [(i, i ^ bit) for i in range(lax.axis_size(axis))])
        if n < len(steps) - 1:
            part, wire = call(
                functools.partial(step_kernel, rows),
                (shape(part.shape, F32), shape(part.shape, BF)),
                0,
                2,
                name="step",
            )(part, got)
    weight, bias = call(
        functools.partial(last_kernel, rows, plan.group, scale),
        (shape((27, plan.group, plan.chan), F32), shape((1, plan.group), F32)),
        0,
        2,
        name="last",
    )(part, got)
    weight = jnp.transpose(weight.reshape(3, 3, 3, plan.group, plan.chan), (3, 4, 0, 1, 2))
    return weight, bias.reshape(plan.group)


def local(volume, weight1, bias1, weight2, bias2, upstream):
    _, group, layers, ny, nz = volume.shape
    chan = weight1.shape[1]
    spaces, groups = lax.axis_size("space"), lax.axis_size("filt")
    plan = Plan(layers, ny, nz, chan, groups, spaces)
    scale = 1.0 / math.sqrt(lax.axis_size("rep") * spaces * layers * ny * nz)

    v, w1 = pack(volume[0], weight1, bias1)
    u, w2 = pack(upstream[0], weight2, bias2)
    w1_all = gather_weight(w1, plan)
    v_all = gather_all(v, plan)
    w2_all = gather_weight(w2, plan)
    u_all = gather_halo(u, plan)
    v_places = [p[1:] for p in v_all]
    u_places = [p[1:] for p in u_all]
    v_all = [p[0] for p in v_all]
    u_all = [p[0] for p in u_all]

    cells = ny * nz
    conv = 2 * 27 * chan * chan * cells
    slots = VM((16, chan, 2 * chan), BF)
    dma = pltpu.SemaphoreType.DMA
    padded = plan.padded()
    grad_rows = 27 * group // 2 + group
    grad_scratch = [VM((layers, ny + 2, 3 * group, nz), BF), VM((9 * group, 3 * chan), F32)]

    turned1, turned2 = call(
        functools.partial(flipped_kernel, plan),
        (shape((3, chan, 9 * chan), BF),) * 2,
        2 * groups,
        0,
        [slots, slots, dma((2, groups))],
        moved=4 << 20,
        name="turn",
    )(*w1_all, *w2_all)

    hidden, slope = call(
        functools.partial(first_kernel, plan, v_places),
        (shape(padded, BF), shape((plan.count(3), ny, chan, nz), F32)),
        len(v_all) + groups,
        0,
        [VM(padded, BF), slots, dma((len(v_all),)), dma((groups,))],
        flops=conv * plan.count(3),
        name="first",
    )(*v_all, *w1_all)

    delta2, output, part2 = call(
        functools.partial(second_kernel, plan, u_places),
        (shape(padded, BF), shape((group, layers, ny, nz), BF), shape((grad_rows, 2 * chan), F32)),
        len(u_all) + groups,
        1,
        [
            VM((plan.count(2), ny, chan, nz), BF),
            slots,
            VM((plan.count(2), ny, chan, nz), F32),
            *grad_scratch,
            dma((len(u_all),)),
            dma((groups,)),
        ],
        flops=conv * plan.count(2),
        name="second",
    )(*u_all, *w2_all, hidden)

    delta1, part1 = call(
        functools.partial(third_kernel, plan, v_places),
        (shape(padded, BF), shape((grad_rows, 2 * chan), F32)),
        len(v_all),
        3,
        [VM(padded, BF), *grad_scratch, dma((len(v_all),))],
        flops=conv * plan.count(1),
        name="third",
    )(*v_all, slope, delta2, turned2)

    volume_grad = call(
        functools.partial(fourth_kernel, plan),
        shape((group, layers, ny, nz), BF),
        0,
        2,
        [VM((layers, ny, group, nz), F32)],
        flops=conv * layers // 4,
        name="fourth",
    )(delta1, turned1)

    grad2, bias_grad2 = total_grads(part2, plan, scale)
    grad1, bias_grad1 = total_grads(part1, plan, scale)
    return (output[None], volume_grad[None], grad1, bias_grad1, grad2, bias_grad2)


def solution(mesh):
    field = P("rep", "filt", "space", None, None)
    kernel = P("filt", None, None, None, None)
    return jax.shard_map(
        local,
        mesh=mesh,
        in_specs=(field, kernel, P("filt"), kernel, P("filt"), field),
        out_specs=(field, field, kernel, P("filt"), kernel, P("filt")),
        check_vma=False,
    )
```

```python
import functools
import math

import jax
import jax.numpy as jnp
from jax import lax
from jax.experimental import pallas as pl
from jax.experimental.pallas import tpu as pltpu
from jax.sharding import PartitionSpec as P

SLOPE = 0.3
NEAR = 3
BF = jnp.bfloat16
F32 = jnp.float32
VM = pltpu.VMEM
ANY = pl.BlockSpec(memory_space=pl.ANY)
WHOLE = pl.BlockSpec(memory_space=pltpu.VMEM)


def call(kernel, outs, n_any, n_vmem, scratch=(), flops=0, moved=0, name=None):
    return pl.pallas_call(
        kernel,
        out_shape=outs,
        in_specs=[ANY] * n_any + [WHOLE] * n_vmem,
        out_specs=jax.tree.map(lambda _: WHOLE, outs),
        scratch_shapes=list(scratch),
        compiler_params=pltpu.CompilerParams(vmem_limit_bytes=40 << 20),
        cost_estimate=pl.CostEstimate(flops=flops, bytes_accessed=moved, transcendentals=0),
        name=name,
    )


def shape(dims, kind):
    return jax.ShapeDtypeStruct(tuple(dims), kind)


def parts(values):
    e = jnp.exp(-jnp.abs(values))
    one = 1.0 + e
    soft = jnp.maximum(values, 0.0) + jnp.log(one)
    sig = jnp.where(values >= 0.0, 1.0, e) / one
    return SLOPE * values + (1.0 - SLOPE) * soft, SLOPE + (1.0 - SLOPE) * sig


def slope_of(values):
    e = jnp.exp(-jnp.abs(values))
    return SLOPE + (1.0 - SLOPE) * (jnp.where(values >= 0.0, 1.0, e) / (1.0 + e))


def smooth(values):
    e = jnp.exp(-jnp.abs(values))
    soft = jnp.maximum(values, 0.0) + jnp.log(1.0 + e)
    return SLOPE * values + (1.0 - SLOPE) * soft


def swap(block):
    return jnp.transpose(block.astype(F32), (1, 0, 2))


def pack_weight(w_ref, b_ref, o_ref, base):
    group, chan, ny = w_ref.shape[1], w_ref.shape[2], o_ref.shape[1]
    for pair in range(5):
        for kz in range(3):
            low = w_ref[6 * pair + kz]
            if pair < 4:
                high = w_ref[6 * pair + 3 + kz]
            else:
                high = jnp.zeros_like(low)
            slot = 3 * pair + kz
            o_ref[base + slot // ny, slot % ny] = jnp.concatenate([low, high], axis=1)
    eye = lax.broadcasted_iota(jnp.int32, (group, group), 0) == lax.broadcasted_iota(
        jnp.int32, (group, group), 1
    )
    col = jnp.sum(jnp.where(eye, jnp.broadcast_to(b_ref[...], (group, group)), 0.0), axis=1, keepdims=True)
    col = jnp.broadcast_to(col, (group, 2 * chan))
    first = col.astype(BF)
    rest = col - first.astype(F32)
    second = rest.astype(BF)
    third = (rest - second.astype(F32)).astype(BF)
    lane = lax.broadcasted_iota(jnp.int32, (group, 2 * chan), 1)
    picked = jnp.where(lane == 0, first.astype(F32), jnp.where(lane == 1, second.astype(F32), third.astype(F32)))
    o_ref[base + 15 // ny, 15 % ny] = picked.astype(BF)


def pack_kernel(edge, *refs):
    if edge:
        f_hbm, w_hbm, b_hbm, n_hbm, o_ref, e_ref, f_ref, w_ref, b_ref, n_ref, sem = refs
    else:
        f_hbm, w_hbm, b_hbm, o_ref, f_ref, w_ref, b_ref, sem = refs
    layers = f_ref.shape[1]
    pairs = [(f_hbm, f_ref), (w_hbm, w_ref), (b_hbm, b_ref)]
    if edge:
        facing = 1 - lax.axis_index("space")
        pairs.append((n_hbm.at[:, pl.ds(facing * (layers - 1), 1)], n_ref))
    copies = [pltpu.make_async_copy(src, dst, sem.at[n]) for n, (src, dst) in enumerate(pairs)]
    for copy in copies:
        copy.start()
    copies[0].wait()
    for x in range(layers):
        o_ref[x] = swap(f_ref[:, x]).astype(BF)
    if edge:
        copies[3].wait()
        for x in range(edge):
            e_ref[x] = o_ref[facing * (layers - edge) + x]
        e_ref[edge] = swap(n_ref[:, 0]).astype(BF)
    copies[1].wait()
    copies[2].wait()
    pack_weight(w_ref, b_ref, o_ref, layers)


def pack(field, weight, bias, name, beside=None, edge=0):
    group, layers, ny, nz = field.shape
    chan = weight.shape[1]
    taps = jnp.transpose(weight, (2, 3, 4, 0, 1)).reshape(27, group, chan)
    args = [field, taps, bias.reshape(1, group)]
    outs = [shape((layers + 16 // ny, ny, group, nz), BF)]
    scratch = [VM(field.shape, BF), VM((27, group, chan), BF), VM((1, group), F32)]
    if edge:
        args.append(beside)
        outs.append(shape((edge + 1, ny, group, nz), BF))
        scratch.append(VM((group, 1, ny, nz), BF))
    return pl.pallas_call(
        functools.partial(pack_kernel, edge),
        out_shape=tuple(outs),
        in_specs=[pl.BlockSpec(memory_space=pltpu.HBM)] * len(args),
        out_specs=(WHOLE,) * len(outs),
        scratch_shapes=scratch + [pltpu.SemaphoreType.DMA((len(args),))],
        compiler_params=pltpu.CompilerParams(vmem_limit_bytes=40 << 20),
        cost_estimate=pl.CostEstimate(flops=0, bytes_accessed=field.size * 4, transcendentals=0),
        name=name,
    )(*(pltpu.with_memory_space_constraint(v, pltpu.HBM) for v in args))


class Plan:
    def __init__(self, layers, ny, nz, chan, groups, spaces):
        self.layers, self.ny, self.nz, self.chan = layers, ny, nz, chan
        self.groups, self.spaces = groups, spaces
        self.group = chan // groups
        self.pair = spaces == 2
        self.quick = self.pair and groups == 4
        self.window = (2 if self.pair else 3) * layers
        self.sides = 1 if self.pair else 2

    def start(self, reach):
        if self.pair:
            return lax.axis_index("space") * (self.layers - reach)
        return self.layers - reach

    def count(self, reach):
        return self.layers + self.sides * reach

    def own(self):
        return self.start(0)

    def inside(self, layer):
        if self.pair:
            return None
        at = (lax.axis_index("space") - 1) * self.layers + layer
        return jnp.logical_and(at >= 0, at < self.spaces * self.layers)

    def chan_at(self, flip):
        return pl.multiple_of((lax.axis_index("filt") ^ flip) * self.group, self.group)

    def padded(self):
        return (self.window + 2, self.ny + 2, self.chan, self.nz)


def flip_perm(value, flip):
    n = lax.axis_size("filt")
    return lax.ppermute(value, "filt", [(i, i ^ flip) for i in range(n)])


def over(value):
    return lax.ppermute(value, "space", [(0, 1), (1, 0)])


def up(value):
    n = lax.axis_size("space")
    return lax.ppermute(value, "space", [(i, i + 1) for i in range(n - 1)])


def down(value):
    n = lax.axis_size("space")
    return lax.ppermute(value, "space", [(i + 1, i) for i in range(n - 1)])


def after(value, *others):
    return lax.optimization_barrier((value, *others))[0]


def gather_quick(volume, weight1, bias1, upstream, weight2, bias2, plan, early_layers):
    n = plan.layers
    packed, edge = pack(volume, weight1, bias1, "pack1", upstream, NEAR)
    x = flip_perm(packed, 2)
    y = over(edge)
    c = flip_perm(packed, 1)
    (second,) = pack(after(upstream, c), weight2, bias2, "pack2")
    y, x = lax.optimization_barrier((y, x, second))[:2]
    d = flip_perm(y, 2)
    xc = flip_perm(x, 1)
    yc = flip_perm(y, 1)
    x2 = flip_perm(second, 2)
    early = early_layers([(v, 0, n, "own", 0, k) for k, v in enumerate([packed, c, x, xc])])
    dc = flip_perm(after(d, early[0]), 1)
    c2 = flip_perm(after(second, early[0]), 1)
    own, other, own2 = [packed, c, x, xc], [y, yc, d, dc], [second, c2, x2, x2]
    return (
        [(v, 0, n, "own", 0, k) for k, v in enumerate(own)],
        [(v, 0, NEAR, "other", 0, k) for k, v in enumerate(other)],
        [(v, 0, n, "own", 0, k) for k, v in enumerate(own2)],
        [(v, NEAR, 1, "halo", 0, k) for k, v in enumerate(other)],
        early,
    )


def gather_plain(volume, weight1, bias1, upstream, weight2, bias2, plan, early_layers):
    n = plan.layers
    (packed,) = pack(volume, weight1, bias1, "pack1")
    (second,) = pack(upstream, weight2, bias2, "pack2")
    own, other, own2, halo = [], [], [], []
    for flip in range(plan.groups):
        mine = flip_perm(packed, flip) if flip else packed
        mine2 = flip_perm(second, flip) if flip else second
        own.append((mine, 0, n, "own", 0, flip))
        own2.append((mine2, 0, n, "own", 0, flip))
        if plan.pair:
            facing = 1 - lax.axis_index("space")
            near = lax.dynamic_slice_in_dim(mine, facing * (n - NEAR), NEAR, axis=0)
            other.append((over(near), 0, NEAR, "other", 0, flip))
            near = lax.dynamic_slice_in_dim(mine2, facing * (n - 1), 1, axis=0)
            halo.append((over(near), 0, 1, "halo", 0, flip))
        else:
            other.append((up(mine[n - NEAR : n]), 0, NEAR, "low", 0, flip))
            other.append((down(mine[:NEAR]), 0, NEAR, "high", 0, flip))
            halo.append((up(mine2[n - 1 : n]), 0, 1, "low", 0, flip))
            halo.append((down(mine2[:1]), 0, 1, "high", 0, flip))
    return own, other, own2, halo, ()


def field_place(plan, place, k):
    n = plan.layers
    if plan.pair:
        s = lax.axis_index("space")
        return 1 + k + (s * n if place == "own" else n - NEAR * s)
    return 1 + k + {"low": n - NEAR, "own": n, "high": 2 * n}[place]


def halo_place(plan, place):
    if plan.pair:
        s = lax.axis_index("space")
        return s if place == "own" else (1 - s) * plan.layers
    return {"low": 0, "own": 1, "high": plan.layers + 1}[place]


def load_weight(plan, refs, dst, sem, start):
    for flip, ref in enumerate(refs):
        copy = pltpu.make_async_copy(
            ref.at[pl.ds(ref.shape[0] - dst.shape[0], dst.shape[0])],
            dst.at[:, :, pl.ds(plan.chan_at(flip), plan.group), :],
            sem.at[flip],
        )
        copy.start() if start else copy.wait()


def load_pieces(plan, refs, places, dst, sem, start, halo=False, near=False):
    for n, (ref, (first, count, place, k, flip)) in enumerate(zip(refs, places)):
        if near and place == "own":
            first = k = (1 - lax.axis_index("space")) * (plan.layers - 2)
            count = 2
        rows = pl.ds(plan.chan_at(flip), plan.group)
        if halo:
            target = dst.at[pl.ds(halo_place(plan, place), count), :, rows, :]
        else:
            target = dst.at[pl.ds(field_place(plan, place, k), count), pl.ds(1, plan.ny), rows, :]
        copy = pltpu.make_async_copy(ref.at[pl.ds(first, count)], target, sem.at[n])
        copy.start() if start else copy.wait()


def zero_rows(ref):
    zero = jnp.zeros(ref.shape[2:], ref.dtype)
    for x in range(ref.shape[0]):
        ref[x, 0] = zero
        ref[x, ref.shape[1] - 1] = zero


def zero_layer(ref, x):
    zero = jnp.zeros(ref.shape[2:], ref.dtype)
    for y in range(1, ref.shape[1] - 1):
        ref[x, y] = zero


def zero_edges(plan, ref):
    zero_rows(ref)
    zero_layer(ref, 0)
    zero_layer(ref, ref.shape[0] - 1)


def slot(w_ref, n):
    return w_ref[n // w_ref.shape[1], n % w_ref.shape[1]]


def weight_matrix(w_ref, chan):
    cols = []
    for pair in range(5):
        block = jnp.concatenate([slot(w_ref, 3 * pair + kz) for kz in range(3)], axis=0)
        cols.append(block if pair < 4 else block[:, :chan])
    return jnp.concatenate(cols, axis=1)


def bias_column(w_ref):
    rows = slot(w_ref, 15).astype(F32)
    return rows[:, 0:1] + rows[:, 1:2] + rows[:, 2:3]


def taps(field_ref, x, y):
    c, nz = field_ref.shape[2], field_ref.shape[3]
    rows = []
    for kx in range(3):
        first = field_ref[x + kx, y : y + 3].reshape(3 * c, nz)
        second = field_ref[x + kx, y + 1 : y + 4].reshape(3 * c, nz)
        rows.append(jnp.concatenate([first, second], axis=1))
    return jnp.concatenate(rows, axis=0)


def z_shift(values, by):
    nz = values.shape[1]
    lane = lax.broadcasted_iota(jnp.int32, values.shape, 1)
    if by > 0:
        return jnp.where(lane == 0, 0.0, pltpu.roll(values, 1, 1))
    return jnp.where(lane == nz - 1, 0.0, pltpu.roll(values, nz - 1, 1))


def z_sum(product, rows, half, nz):
    part = product[:, half * nz : (half + 1) * nz]
    return part[rows : 2 * rows] + z_shift(part[:rows], 1) + z_shift(part[2 * rows :], -1)


def conv_rows(weight, field_ref, x, each):
    ny, nz = field_ref.shape[1] - 2, field_ref.shape[3]
    rows = weight.shape[0] // 3
    for y in range(0, ny, 2):
        product = jnp.dot(weight, taps(field_ref, x, y), preferred_element_type=F32)
        for half in range(2):
            each(y + half, z_sum(product, rows, half, nz))


def first_rows(plan, weight, bias, a_ref, start, count, put):
    def body(t, carry):
        x = start + t
        inside = plan.inside(x)

        def each(y, value):
            act, slope = parts(value + bias)
            if inside is not None:
                act = jnp.where(inside, act, 0.0)
            put(t, x, y, act.astype(BF), slope)

        conv_rows(weight, a_ref, x, each)
        return carry

    lax.fori_loop(0, count, body, 0, unroll=True)


def early_kernel(plan, places, *refs):
    n = len(places)
    pieces = refs[:n]
    h_ref, s_ref, a_ref, w_ref, sem, wsem = refs[n:]
    load_weight(plan, pieces[: plan.groups], w_ref, wsem, True)
    load_pieces(plan, pieces, places, a_ref, sem, True)
    zero_edges(plan, a_ref)
    load_weight(plan, pieces[: plan.groups], w_ref, wsem, False)
    load_pieces(plan, pieces, places, a_ref, sem, False)

    def put(t, x, y, act, slope):
        h_ref[t, y] = act
        s_ref[t, y] = slope

    start = lax.axis_index("space") * (plan.layers + 1)
    first_rows(plan, weight_matrix(w_ref, plan.chan), bias_column(w_ref), a_ref, start, plan.layers - 1, put)


def first_kernel(plan, places, *refs):
    n = len(places)
    pieces, refs = refs[:n], refs[n:]
    if plan.quick:
        eh_ref, es_ref, refs = refs[0], refs[1], refs[2:]
    h_ref, s_ref, a_ref, w_ref, sem, wsem, esem = refs
    load_weight(plan, pieces[: plan.groups], w_ref, wsem, True)
    load_pieces(plan, pieces, places, a_ref, sem, True, near=plan.quick)
    zero_edges(plan, a_ref)
    zero_edges(plan, h_ref)
    base = plan.start(2)
    start, count = base, plan.count(2)
    copies = []
    if plan.quick:
        s = lax.axis_index("space")
        done = s * (plan.layers + 1)
        start, count = plan.layers - 1 - s, count - plan.layers + 1
        copies = [
            pltpu.make_async_copy(
                eh_ref, h_ref.at[pl.ds(done + 1, plan.layers - 1), pl.ds(1, plan.ny)], esem.at[0]
            ),
            pltpu.make_async_copy(es_ref, s_ref.at[pl.ds(done - base, plan.layers - 1)], esem.at[1]),
        ]
    for copy in copies:
        copy.start()
    load_weight(plan, pieces[: plan.groups], w_ref, wsem, False)
    load_pieces(plan, pieces, places, a_ref, sem, False, near=plan.quick)

    def put(t, x, y, act, slope):
        h_ref[x + 1, y + 1] = act
        s_ref[x - base, y] = slope

    first_rows(plan, weight_matrix(w_ref, plan.chan), bias_column(w_ref), a_ref, start, count, put)
    for copy in copies:
        copy.wait()


def grads(plan, get, f_ref, sh_ref, acc_ref, g_ref):
    group, nz, ny, chan = plan.group, plan.nz, plan.ny, plan.chan
    rows = pl.ds(plan.chan_at(0), group)
    own = plan.own()
    zero = jnp.zeros((3 * group, nz), BF)

    def shift(t, total):
        sh_ref[t, 0] = zero
        sh_ref[t, ny + 1] = zero
        for y in range(ny):
            value = get(t, y, rows).astype(F32)
            total = total + value
            sh_ref[t, y + 1] = jnp.concatenate([z_shift(value, -1), value, z_shift(value, 1)], axis=0).astype(BF)
        return total

    total = lax.fori_loop(0, plan.layers, shift, jnp.zeros((group, nz), F32), unroll=True)
    total_w = jnp.zeros(acc_ref.shape, F32)
    for t in range(plan.layers):
        x = own + t
        left = jnp.concatenate(
            [jnp.concatenate([sh_ref[t, y + 2 - ky] for y in range(ny)], axis=1) for ky in range(3)], axis=0
        )
        right = jnp.concatenate(
            [jnp.concatenate([f_ref[x + kx, y + 1] for y in range(ny)], axis=1) for kx in range(3)], axis=0
        )
        total_w += lax.dot_general(left, right, (((1,), (1,)), ((), ())), preferred_element_type=F32)
    acc_ref[...] = total_w
    n = 9 * group
    g_ref[0:n] = acc_ref[:, 0 : 2 * chan]
    last = acc_ref[:, 2 * chan :]
    g_ref[n : n + n // 2] = jnp.concatenate([last[: n // 2], last[n // 2 :]], axis=1)
    g_ref[n + n // 2 :] = jnp.broadcast_to(jnp.sum(total, axis=1, keepdims=True), (group, 2 * chan))


def second_kernel(plan, places, *refs):
    n = len(places)
    pieces = refs[:n]
    weights = pieces[: plan.groups]
    h_ref, d_ref, o_ref, g_ref, t_ref, u_ref, w_ref, p_ref, sh_ref, acc_ref, sem, wsem = refs[n:]
    load_weight(plan, weights, w_ref, wsem, True)
    load_pieces(plan, pieces, places, u_ref, sem, True, halo=True)
    zero_edges(plan, d_ref)
    load_weight(plan, weights, w_ref, wsem, False)
    turn(w_ref, t_ref, plan.chan)
    load_pieces(plan, pieces, places, u_ref, sem, False, halo=True)
    start = plan.start(1)
    m_ref = weight_matrix(w_ref, plan.chan)
    bias = bias_column(w_ref)

    def body(t, carry):
        x = start + t

        def each(y, value):
            pre = value + bias
            p_ref[t, y] = pre
            d_ref[x + 1, y + 1] = (u_ref[t, y].astype(F32) * slope_of(pre)).astype(BF)

        conv_rows(m_ref, h_ref, x, each)
        return carry

    lax.fori_loop(0, plan.count(1), body, 0, unroll=True)
    rows = pl.ds(plan.chan_at(0), plan.group)
    own = plan.own()
    first = own - start
    for t in range(plan.layers):
        o_ref[:, t] = jnp.transpose(smooth(p_ref[first + t, :, rows, :]), (1, 0, 2)).astype(BF)
    grads(plan, lambda t, y, rows: d_ref[own + t + 1, y + 1, rows, :], h_ref, sh_ref, acc_ref, g_ref)


def turn(w_ref, out, chan):
    for kz in range(3):
        turned = [jnp.transpose(slot(w_ref, 3 * pair + 2 - kz).astype(F32), (1, 0)) for pair in range(5)]
        for pair in range(5):
            low = turned[4 - pair][:chan]
            if pair < 4:
                block = jnp.concatenate([low, turned[3 - pair][chan:]], axis=1)
                out[kz, :, 2 * chan * pair : 2 * chan * (pair + 1)] = block.astype(BF)
            else:
                out[kz, :, 2 * chan * pair :] = low.astype(BF)


def turn_kernel(plan, *refs):
    out, w_ref, sem = refs[plan.groups :]
    for go in (True, False):
        load_weight(plan, refs[: plan.groups], w_ref, sem, go)
    turn(w_ref, out, plan.chan)


def third_kernel(plan, places, *refs):
    n = len(places)
    pieces = refs[:n]
    s_ref, d2_ref, t_ref, d_ref, g_ref, a_ref, sh_ref, acc_ref, sem = refs[n:]
    load_pieces(plan, pieces, places, a_ref, sem, True)
    zero_edges(plan, a_ref)
    start = plan.own()
    skip = start - plan.start(2)
    m_ref = t_ref[...].reshape(3 * plan.chan, 9 * plan.chan)

    def body(t, carry):
        def each(y, value):
            d_ref[t, y] = (value * s_ref[skip + t, y]).astype(BF)

        conv_rows(m_ref, d2_ref, start + t, each)
        return carry

    lax.fori_loop(0, plan.layers, body, 0, unroll=True)
    load_pieces(plan, pieces, places, a_ref, sem, False)
    grads(plan, lambda t, y, rows: d_ref[t, y, rows, :], a_ref, sh_ref, acc_ref, g_ref)


def fourth_kernel(plan, d_ref, t_ref, r_ref, *refs):
    *outs, a_ref, sem = refs
    layers, ny = plan.layers, plan.ny
    copy = pltpu.make_async_copy(d_ref, a_ref.at[pl.ds(2, layers), pl.ds(1, ny)], sem)
    copy.start()
    zero_rows(a_ref)
    for x in (0, 1, layers + 2, layers + 3):
        zero_layer(a_ref, x)
    copy.wait()
    rows = pl.ds(plan.chan_at(0), plan.group)
    m_ref = t_ref[:, rows, :].reshape(3 * plan.group, 9 * plan.chan)
    for t in range(layers):

        def each(y, value, t=t):
            r_ref[t, y] = value

        conv_rows(m_ref, a_ref, t + 1, each)
    if plan.pair:
        places = [(1 - lax.axis_index("space")) * (layers + 1)]
    else:
        places = [0, layers + 1]
    for out, place in zip(outs, places):

        def beside(y, value, out=out):
            out[y * plan.group : (y + 1) * plan.group] = value.astype(BF)

        conv_rows(m_ref, a_ref, place, beside)


def finish_volume(plan, r_ref, shares, o_ref):
    layers, ny, group = plan.layers, plan.ny, plan.group
    for layer, ref, base in shares:
        for y in range(ny):
            r_ref[layer, y] += ref[base + y * group : base + (y + 1) * group].astype(F32)
    for t in range(layers):
        o_ref[:, t] = jnp.transpose(r_ref[t], (1, 0, 2)).astype(BF)


def finish_kernel(plan, r_hbm, low_ref, high_ref, o_ref, r_ref, sem):
    copy = pltpu.make_async_copy(r_hbm, r_ref, sem)
    copy.start()
    copy.wait()
    finish_volume(plan, r_ref, [(0, low_ref, 0), (plan.layers - 1, high_ref, 0)], o_ref)


def to_wire(values, rows):
    row = lax.broadcasted_iota(jnp.int32, values.shape, 0)
    lane = lax.broadcasted_iota(jnp.int32, values.shape, 1)
    high = values.astype(BF).astype(F32)
    second = jnp.logical_and(row >= rows, lane >= values.shape[1] // 2)
    return jnp.where(second, values - high, high).astype(BF)


def add_wire(values, wire, rows):
    got = wire.astype(F32)
    row = lax.broadcasted_iota(jnp.int32, values.shape, 0)
    return values + got + jnp.where(row >= rows, pltpu.roll(got, values.shape[1] // 2, 1), 0.0)


def wire_kernel(rows, a_ref, w_ref):
    w_ref[...] = to_wire(a_ref[...], rows)


def step_kernel(rows, a_ref, got_ref, o_ref, w_ref):
    total = add_wire(a_ref[...], got_ref[...], rows)
    o_ref[...] = total
    w_ref[...] = to_wire(total, rows)


def join_kernel(rows, a_ref, got_ref, share_ref, o_ref, w_ref):
    total = add_wire(a_ref[...], got_ref[...], rows)
    o_ref[...] = total
    w_ref[: total.shape[0]] = to_wire(total, rows)
    w_ref[total.shape[0] :] = share_ref[...]


def close_kernel(plan, rows, scale, r_hbm, a_ref, got_ref, w_ref, b_ref, o_ref, r_ref, sem):
    copy = pltpu.make_async_copy(r_hbm, r_ref, sem)
    copy.start()
    last_kernel(rows, plan.group, scale, a_ref, got_ref, w_ref, b_ref)
    copy.wait()
    layer = (1 - lax.axis_index("space")) * (plan.layers - 1)
    finish_volume(plan, r_ref, [(layer, got_ref, a_ref.shape[0])], o_ref)


def last_kernel(rows, group, scale, a_ref, got_ref, w_ref, b_ref):
    total = add_wire(a_ref[...], got_ref[: a_ref.shape[0]], rows) * scale
    n = 9 * group
    chan = total.shape[1] // 2
    w_ref[0:9] = total[:n, :chan].reshape(9, group, chan)
    w_ref[9:18] = total[:n, chan:].reshape(9, group, chan)
    tail = total[n : n + n // 2]
    w_ref[18:27] = jnp.concatenate([tail[:, :chan], tail[:, chan:]], axis=0).reshape(9, group, chan)
    col = total[rows:, :group]
    eye = lax.broadcasted_iota(jnp.int32, (group, group), 0) == lax.broadcasted_iota(
        jnp.int32, (group, group), 1
    )
    b_ref[...] = jnp.sum(jnp.where(eye, col, 0.0), axis=0, keepdims=True)


def rounds(plan):
    out = []
    for axis in ("space", "rep"):
        size, bit = lax.axis_size(axis), 1
        while bit < size:
            out.append((axis, bit))
            bit *= 2
    return out


def exchange(wire, step):
    axis, bit = step
    return lax.ppermute(wire, axis, [(i, i ^ bit) for i in range(lax.axis_size(axis))])


def first_wire(part, plan):
    rows = part.shape[0] - plan.group
    return call(functools.partial(wire_kernel, rows), shape(part.shape, BF), 0, 1, name="wire")(part)


def grad_shapes(plan):
    return shape((27, plan.group, plan.chan), F32), shape((1, plan.group), F32)


def as_grads(weight, bias, plan):
    weight = jnp.transpose(weight.reshape(3, 3, 3, plan.group, plan.chan), (3, 4, 0, 1, 2))
    return weight, bias.reshape(plan.group)


def total_step(part, got, step, plan, share=None):
    rows = part.shape[0] - plan.group
    kernel, args, more = step_kernel, (part, got), 0
    if share is not None:
        kernel, args, more = join_kernel, (part, got, share), share.shape[0]
    part, wire = call(
        functools.partial(kernel, rows),
        (shape(part.shape, F32), shape((part.shape[0] + more, part.shape[1]), BF)),
        0,
        len(args),
        name="step",
    )(*args)
    return part, exchange(wire, step)


def total_last(part, got, plan, scale):
    rows = part.shape[0] - plan.group
    weight, bias = call(
        functools.partial(last_kernel, rows, plan.group, scale), grad_shapes(plan), 0, 2, name="last"
    )(part, got)
    return as_grads(weight, bias, plan)


def local(volume, weight1, bias1, weight2, bias2, upstream):
    _, group, layers, ny, nz = volume.shape
    chan = weight1.shape[1]
    spaces, groups = lax.axis_size("space"), lax.axis_size("filt")
    plan = Plan(layers, ny, nz, chan, groups, spaces)
    scale = 1.0 / math.sqrt(lax.axis_size("rep") * spaces * layers * ny * nz)

    cells = ny * nz
    conv = 2 * 27 * chan * chan * cells
    slots = VM((16 // ny, ny, chan, 2 * chan), BF)
    dma = pltpu.SemaphoreType.DMA
    padded = plan.padded()
    grad_rows = 27 * group // 2 + group
    grad_scratch = [VM((layers, ny + 2, 3 * group, nz), BF), VM((9 * group, 3 * chan), F32)]

    def early_layers(pieces):
        return call(
            functools.partial(early_kernel, plan, [p[1:] for p in pieces]),
            (shape((layers - 1, ny, chan, nz), BF), shape((layers - 1, ny, chan, nz), F32)),
            len(pieces),
            0,
            [VM(padded, BF), slots, dma((len(pieces),)), dma((groups,))],
            flops=1,
            name="early",
        )(*(p[0] for p in pieces))

    gather = gather_quick if plan.quick else gather_plain
    v_own, v_other, u_own, u_other, early = gather(
        volume[0], weight1, bias1, upstream[0], weight2, bias2, plan, early_layers
    )
    v_places = [p[1:] for p in v_own + v_other]
    u_places = [p[1:] for p in u_own + u_other]
    v_all = [p[0] for p in v_own + v_other]
    u_all = [p[0] for p in u_own + u_other]

    turned1 = call(
        functools.partial(turn_kernel, plan),
        shape((3, chan, 9 * chan), BF),
        groups,
        0,
        [slots, dma((groups,))],
        moved=2 << 20,
        name="turn",
    )(*v_all[:groups])

    hidden, slope = call(
        functools.partial(first_kernel, plan, v_places),
        (shape(padded, BF), shape((plan.count(2), ny, chan, nz), F32)),
        len(v_all) + len(early),
        0,
        [VM(padded, BF), slots, dma((len(v_all),)), dma((groups,)), dma((2,))],
        flops=1,
        name="first",
    )(*v_all, *early)

    if plan.quick:
        u_all[3] = flip_perm(after(u_all[2], hidden), 1)
    delta2, output, part2, turned2 = call(
        functools.partial(second_kernel, plan, u_places),
        (
            shape(padded, BF),
            shape((group, layers, ny, nz), BF),
            shape((grad_rows, 2 * chan), F32),
            shape((3, chan, 9 * chan), BF),
        ),
        len(u_all),
        1,
        [
            VM((plan.count(1), ny, chan, nz), BF),
            slots,
            VM((plan.count(1), ny, chan, nz), F32),
            *grad_scratch,
            dma((len(u_all),)),
            dma((groups,)),
        ],
        flops=1,
        name="second",
    )(*u_all, hidden)

    delta1, part1 = call(
        functools.partial(third_kernel, plan, v_places),
        (shape((layers, ny, chan, nz), BF), shape((grad_rows, 2 * chan), F32)),
        len(v_all),
        3,
        [VM(padded, BF), *grad_scratch, dma((len(v_all),))],
        flops=conv * layers,
        name="third",
    )(*v_all, slope, delta2, turned2)

    beside = [shape((ny * group, nz), BF)] * plan.sides
    own_grad, *shares = call(
        functools.partial(fourth_kernel, plan),
        (shape((layers, ny, group, nz), F32), *beside),
        1,
        1,
        [VM((layers + 4, ny + 2, chan, nz), BF), dma],
        flops=1,
        name="fourth",
    )(delta1, turned1)

    steps1 = rounds(plan)
    steps2 = steps1[1:] + steps1[:1]
    got1 = exchange(first_wire(part1, plan), steps1[0])
    got2 = exchange(first_wire(after(part2, part1), plan), steps2[0])
    for step in steps1[1:]:
        part1, got1 = total_step(part1, got1, step, plan)
    for n, step in enumerate(steps2[1:], 2):
        share = shares[0] if plan.pair and n == len(steps2) else None
        part2, got2 = total_step(part2, got2, step, plan, share)
    grad1, bias_grad1 = total_last(part1, got1, plan, scale)
    volume_shape = shape((group, layers, ny, nz), BF)
    finish_scratch = [VM((layers, ny, group, nz), F32), dma]
    if plan.pair:
        *grads2, volume_grad = call(
            functools.partial(close_kernel, plan, part2.shape[0] - group, scale),
            (*grad_shapes(plan), volume_shape),
            1,
            2,
            finish_scratch,
            name="close",
        )(own_grad, part2, got2)
        grad2, bias_grad2 = as_grads(*grads2, plan)
    else:
        grad2, bias_grad2 = total_last(part2, got2, plan, scale)
        volume_grad = call(
            functools.partial(finish_kernel, plan), volume_shape, 1, 2, finish_scratch, name="finish"
        )(own_grad, up(shares[1]), down(shares[0]))
    return (output[None], volume_grad[None], grad1, bias_grad1, grad2, bias_grad2)


def solution(mesh):
    field = P("rep", "filt", "space", None, None)
    kernel = P("filt", None, None, None, None)
    return jax.shard_map(
        local,
        mesh=mesh,
        in_specs=(field, kernel, P("filt"), kernel, P("filt"), field),
        out_specs=(field, field, kernel, P("filt"), kernel, P("filt")),
        check_vma=False,
    )
```

```python
import functools
import math

import jax
import jax.numpy as jnp
from jax import lax
from jax.experimental import pallas as pl
from jax.experimental.pallas import tpu as pltpu
from jax.sharding import PartitionSpec as P

SLOPE = 0.3
NEAR = 3
BF = jnp.bfloat16
F32 = jnp.float32
VM = pltpu.VMEM
ANY = pl.BlockSpec(memory_space=pl.ANY)
WHOLE = pl.BlockSpec(memory_space=pltpu.VMEM)


def call(kernel, outs, n_any, n_vmem, scratch=(), flops=0, moved=0, name=None):
    return pl.pallas_call(
        kernel,
        out_shape=outs,
        in_specs=[ANY] * n_any + [WHOLE] * n_vmem,
        out_specs=jax.tree.map(lambda _: WHOLE, outs),
        scratch_shapes=list(scratch),
        compiler_params=pltpu.CompilerParams(vmem_limit_bytes=40 << 20),
        cost_estimate=pl.CostEstimate(flops=flops, bytes_accessed=moved, transcendentals=0),
        name=name,
    )


def shape(dims, kind):
    return jax.ShapeDtypeStruct(tuple(dims), kind)


def parts(values):
    e = jnp.exp(-jnp.abs(values))
    one = 1.0 + e
    soft = jnp.maximum(values, 0.0) + jnp.log(one)
    sig = jnp.where(values >= 0.0, 1.0, e) / one
    return SLOPE * values + (1.0 - SLOPE) * soft, SLOPE + (1.0 - SLOPE) * sig


def slope_of(values):
    e = jnp.exp(-jnp.abs(values))
    return SLOPE + (1.0 - SLOPE) * (jnp.where(values >= 0.0, 1.0, e) / (1.0 + e))


def smooth(values):
    e = jnp.exp(-jnp.abs(values))
    soft = jnp.maximum(values, 0.0) + jnp.log(1.0 + e)
    return SLOPE * values + (1.0 - SLOPE) * soft


def swap(block):
    return jnp.transpose(block.astype(F32), (1, 0, 2))


def pack_weight(w_ref, b_ref, o_ref, base):
    group, chan, ny = w_ref.shape[1], w_ref.shape[2], o_ref.shape[1]
    for pair in range(5):
        for kz in range(3):
            low = w_ref[6 * pair + kz]
            if pair < 4:
                high = w_ref[6 * pair + 3 + kz]
            else:
                high = jnp.zeros_like(low)
            slot = 3 * pair + kz
            o_ref[base + slot // ny, slot % ny] = jnp.concatenate([low, high], axis=1)
    eye = lax.broadcasted_iota(jnp.int32, (group, group), 0) == lax.broadcasted_iota(
        jnp.int32, (group, group), 1
    )
    col = jnp.sum(jnp.where(eye, jnp.broadcast_to(b_ref[...], (group, group)), 0.0), axis=1, keepdims=True)
    col = jnp.broadcast_to(col, (group, 2 * chan))
    first = col.astype(BF)
    rest = col - first.astype(F32)
    second = rest.astype(BF)
    third = (rest - second.astype(F32)).astype(BF)
    lane = lax.broadcasted_iota(jnp.int32, (group, 2 * chan), 1)
    picked = jnp.where(lane == 0, first.astype(F32), jnp.where(lane == 1, second.astype(F32), third.astype(F32)))
    o_ref[base + 15 // ny, 15 % ny] = picked.astype(BF)


def pack_kernel(edge, *refs):
    if edge:
        f_hbm, w_hbm, b_hbm, n_hbm, o_ref, e_ref, f_ref, w_ref, b_ref, n_ref, sem = refs
    else:
        f_hbm, w_hbm, b_hbm, o_ref, f_ref, w_ref, b_ref, sem = refs
    layers = f_ref.shape[1]
    pairs = [(f_hbm, f_ref), (w_hbm, w_ref), (b_hbm, b_ref)]
    if edge:
        facing = 1 - lax.axis_index("space")
        pairs.append((n_hbm.at[:, pl.ds(facing * (layers - 1), 1)], n_ref))
    copies = [pltpu.make_async_copy(src, dst, sem.at[n]) for n, (src, dst) in enumerate(pairs)]
    for copy in copies:
        copy.start()
    copies[0].wait()
    for x in range(layers):
        o_ref[x] = swap(f_ref[:, x]).astype(BF)
    if edge:
        copies[3].wait()
        for x in range(edge):
            e_ref[x] = o_ref[facing * (layers - edge) + x]
        e_ref[edge] = swap(n_ref[:, 0]).astype(BF)
    copies[1].wait()
    copies[2].wait()
    pack_weight(w_ref, b_ref, o_ref, layers)


def pack(field, weight, bias, name, beside=None, edge=0):
    group, layers, ny, nz = field.shape
    chan = weight.shape[1]
    taps = jnp.transpose(weight, (2, 3, 4, 0, 1)).reshape(27, group, chan)
    args = [field, taps, bias.reshape(1, group)]
    outs = [shape((layers + 16 // ny, ny, group, nz), BF)]
    scratch = [VM(field.shape, BF), VM((27, group, chan), BF), VM((1, group), F32)]
    if edge:
        args.append(beside)
        outs.append(shape((edge + 1, ny, group, nz), BF))
        scratch.append(VM((group, 1, ny, nz), BF))
    return pl.pallas_call(
        functools.partial(pack_kernel, edge),
        out_shape=tuple(outs),
        in_specs=[pl.BlockSpec(memory_space=pltpu.HBM)] * len(args),
        out_specs=(WHOLE,) * len(outs),
        scratch_shapes=scratch + [pltpu.SemaphoreType.DMA((len(args),))],
        compiler_params=pltpu.CompilerParams(vmem_limit_bytes=40 << 20),
        cost_estimate=pl.CostEstimate(flops=0, bytes_accessed=field.size * 4, transcendentals=0),
        name=name,
    )(*(pltpu.with_memory_space_constraint(v, pltpu.HBM) for v in args))


class Plan:
    def __init__(self, layers, ny, nz, chan, groups, spaces):
        self.layers, self.ny, self.nz, self.chan = layers, ny, nz, chan
        self.groups, self.spaces = groups, spaces
        self.group = chan // groups
        self.pair = spaces == 2
        self.quick = self.pair and groups == 4
        self.window = (2 if self.pair else 3) * layers
        self.sides = 1 if self.pair else 2

    def start(self, reach):
        if self.pair:
            return lax.axis_index("space") * (self.layers - reach)
        return self.layers - reach

    def count(self, reach):
        return self.layers + self.sides * reach

    def own(self):
        return self.start(0)

    def inside(self, layer):
        if self.pair:
            return None
        at = (lax.axis_index("space") - 1) * self.layers + layer
        return jnp.logical_and(at >= 0, at < self.spaces * self.layers)

    def chan_at(self, flip):
        return pl.multiple_of((lax.axis_index("filt") ^ flip) * self.group, self.group)

    def padded(self):
        return (self.window + 2, self.ny + 2, self.chan, self.nz)


def flip_perm(value, flip):
    n = lax.axis_size("filt")
    return lax.ppermute(value, "filt", [(i, i ^ flip) for i in range(n)])


def over(value):
    return lax.ppermute(value, "space", [(0, 1), (1, 0)])


def up(value):
    n = lax.axis_size("space")
    return lax.ppermute(value, "space", [(i, i + 1) for i in range(n - 1)])


def down(value):
    n = lax.axis_size("space")
    return lax.ppermute(value, "space", [(i + 1, i) for i in range(n - 1)])


def after(value, *others):
    return lax.optimization_barrier((value, *others))[0]


def gather_quick(volume, weight1, bias1, upstream, weight2, bias2, plan, early_layers):
    n = plan.layers
    packed, edge = pack(volume, weight1, bias1, "pack1", upstream, NEAR)
    x = flip_perm(packed, 2)
    y = over(edge)
    c = flip_perm(packed, 1)
    (second,) = pack(after(upstream, c), weight2, bias2, "pack2")
    y, x = lax.optimization_barrier((y, x, second))[:2]
    d = flip_perm(y, 2)
    xc = flip_perm(x, 1)
    yc = flip_perm(y, 1)
    x2 = flip_perm(second, 2)
    early = early_layers([(v, 0, n, "own", 0, k) for k, v in enumerate([packed, c, x, xc])])
    dc = flip_perm(after(d, early[0]), 1)
    c2 = flip_perm(after(second, early[0]), 1)
    own, other, own2 = [packed, c, x, xc], [y, yc, d, dc], [second, c2, x2, x2]
    return (
        [(v, 0, n, "own", 0, k) for k, v in enumerate(own)],
        [(v, 0, NEAR, "other", 0, k) for k, v in enumerate(other)],
        [(v, 0, n, "own", 0, k) for k, v in enumerate(own2)],
        [(v, NEAR, 1, "halo", 0, k) for k, v in enumerate(other)],
        early,
    )


def gather_plain(volume, weight1, bias1, upstream, weight2, bias2, plan, early_layers):
    n = plan.layers
    (packed,) = pack(volume, weight1, bias1, "pack1")
    (second,) = pack(upstream, weight2, bias2, "pack2")
    own, other, own2, halo = [], [], [], []
    for flip in range(plan.groups):
        mine = flip_perm(packed, flip) if flip else packed
        mine2 = flip_perm(second, flip) if flip else second
        own.append((mine, 0, n, "own", 0, flip))
        own2.append((mine2, 0, n, "own", 0, flip))
        if plan.pair:
            facing = 1 - lax.axis_index("space")
            near = lax.dynamic_slice_in_dim(mine, facing * (n - NEAR), NEAR, axis=0)
            other.append((over(near), 0, NEAR, "other", 0, flip))
            near = lax.dynamic_slice_in_dim(mine2, facing * (n - 1), 1, axis=0)
            halo.append((over(near), 0, 1, "halo", 0, flip))
        else:
            other.append((up(mine[n - NEAR : n]), 0, NEAR, "low", 0, flip))
            other.append((down(mine[:NEAR]), 0, NEAR, "high", 0, flip))
            halo.append((up(mine2[n - 1 : n]), 0, 1, "low", 0, flip))
            halo.append((down(mine2[:1]), 0, 1, "high", 0, flip))
    return own, other, own2, halo, ()


def field_place(plan, place, k):
    n = plan.layers
    if plan.pair:
        s = lax.axis_index("space")
        return 1 + k + (s * n if place == "own" else n - NEAR * s)
    return 1 + k + {"low": n - NEAR, "own": n, "high": 2 * n}[place]


def halo_place(plan, place):
    if plan.pair:
        s = lax.axis_index("space")
        return s if place == "own" else (1 - s) * plan.layers
    return {"low": 0, "own": 1, "high": plan.layers + 1}[place]


def load_weight(plan, refs, dst, sem, start):
    for flip, ref in enumerate(refs):
        copy = pltpu.make_async_copy(
            ref.at[pl.ds(ref.shape[0] - dst.shape[0], dst.shape[0])],
            dst.at[:, :, pl.ds(plan.chan_at(flip), plan.group), :],
            sem.at[flip],
        )
        copy.start() if start else copy.wait()


def load_pieces(plan, refs, places, dst, sem, start, halo=False, near=False):
    for n, (ref, (first, count, place, k, flip)) in enumerate(zip(refs, places)):
        if near and place == "own":
            first = k = (1 - lax.axis_index("space")) * (plan.layers - 2)
            count = 2
        rows = pl.ds(plan.chan_at(flip), plan.group)
        if halo:
            target = dst.at[pl.ds(halo_place(plan, place), count), :, rows, :]
        else:
            target = dst.at[pl.ds(field_place(plan, place, k), count), pl.ds(1, plan.ny), rows, :]
        copy = pltpu.make_async_copy(ref.at[pl.ds(first, count)], target, sem.at[n])
        copy.start() if start else copy.wait()


def zero_rows(ref):
    zero = jnp.zeros(ref.shape[2:], ref.dtype)
    for x in range(ref.shape[0]):
        ref[x, 0] = zero
        ref[x, ref.shape[1] - 1] = zero


def zero_layer(ref, x):
    zero = jnp.zeros(ref.shape[2:], ref.dtype)
    for y in range(1, ref.shape[1] - 1):
        ref[x, y] = zero


def zero_edges(plan, ref):
    zero_rows(ref)
    zero_layer(ref, 0)
    zero_layer(ref, ref.shape[0] - 1)


def slot(w_ref, n):
    return w_ref[n // w_ref.shape[1], n % w_ref.shape[1]]


def weight_matrix(w_ref, chan):
    cols = []
    for pair in range(5):
        block = jnp.concatenate([slot(w_ref, 3 * pair + kz) for kz in range(3)], axis=0)
        cols.append(block if pair < 4 else block[:, :chan])
    return jnp.concatenate(cols, axis=1)


def bias_column(w_ref):
    rows = slot(w_ref, 15).astype(F32)
    return rows[:, 0:1] + rows[:, 1:2] + rows[:, 2:3]


def taps(field_ref, x, y):
    c, nz = field_ref.shape[2], field_ref.shape[3]
    rows = []
    for kx in range(3):
        first = field_ref[x + kx, y : y + 3].reshape(3 * c, nz)
        second = field_ref[x + kx, y + 1 : y + 4].reshape(3 * c, nz)
        rows.append(jnp.concatenate([first, second], axis=1))
    return jnp.concatenate(rows, axis=0)


def z_shift(values, by):
    nz = values.shape[1]
    lane = lax.broadcasted_iota(jnp.int32, values.shape, 1)
    if by > 0:
        return jnp.where(lane == 0, 0.0, pltpu.roll(values, 1, 1))
    return jnp.where(lane == nz - 1, 0.0, pltpu.roll(values, nz - 1, 1))


def z_sum(product, rows, half, nz):
    part = product[:, half * nz : (half + 1) * nz]
    return part[rows : 2 * rows] + z_shift(part[:rows], 1) + z_shift(part[2 * rows :], -1)


def conv_rows(weight, field_ref, x, each):
    ny, nz = field_ref.shape[1] - 2, field_ref.shape[3]
    rows = weight.shape[0] // 3
    for y in range(0, ny, 2):
        product = jnp.dot(weight, taps(field_ref, x, y), preferred_element_type=F32)
        for half in range(2):
            each(y + half, z_sum(product, rows, half, nz))


def first_rows(plan, weight, bias, a_ref, start, count, put):
    def body(t, carry):
        x = start + t
        inside = plan.inside(x)

        def each(y, value):
            act, slope = parts(value + bias)
            if inside is not None:
                act = jnp.where(inside, act, 0.0)
            put(t, x, y, act.astype(BF), slope)

        conv_rows(weight, a_ref, x, each)
        return carry

    lax.fori_loop(0, count, body, 0, unroll=True)


def early_kernel(plan, places, *refs):
    n = len(places)
    pieces = refs[:n]
    h_ref, s_ref, a_ref, w_ref, sem, wsem = refs[n:]
    load_weight(plan, pieces[: plan.groups], w_ref, wsem, True)
    load_pieces(plan, pieces, places, a_ref, sem, True)
    zero_edges(plan, a_ref)
    load_weight(plan, pieces[: plan.groups], w_ref, wsem, False)
    load_pieces(plan, pieces, places, a_ref, sem, False)

    def put(t, x, y, act, slope):
        h_ref[t, y] = act
        s_ref[t, y] = slope

    start = lax.axis_index("space") * (plan.layers + 1)
    first_rows(plan, weight_matrix(w_ref, plan.chan), bias_column(w_ref), a_ref, start, plan.layers - 1, put)


def first_kernel(plan, places, *refs):
    n = len(places)
    pieces, refs = refs[:n], refs[n:]
    if plan.quick:
        eh_ref, es_ref, refs = refs[0], refs[1], refs[2:]
    h_ref, s_ref, a_ref, w_ref, sem, wsem, esem = refs
    load_weight(plan, pieces[: plan.groups], w_ref, wsem, True)
    load_pieces(plan, pieces, places, a_ref, sem, True, near=plan.quick)
    zero_edges(plan, a_ref)
    zero_edges(plan, h_ref)
    base = plan.start(2)
    start, count = base, plan.count(2)
    copies = []
    if plan.quick:
        s = lax.axis_index("space")
        done = s * (plan.layers + 1)
        start, count = plan.layers - 1 - s, count - plan.layers + 1
        copies = [
            pltpu.make_async_copy(
                eh_ref, h_ref.at[pl.ds(done + 1, plan.layers - 1), pl.ds(1, plan.ny)], esem.at[0]
            ),
            pltpu.make_async_copy(es_ref, s_ref.at[pl.ds(done - base, plan.layers - 1)], esem.at[1]),
        ]
    for copy in copies:
        copy.start()
    load_weight(plan, pieces[: plan.groups], w_ref, wsem, False)
    load_pieces(plan, pieces, places, a_ref, sem, False, near=plan.quick)

    def put(t, x, y, act, slope):
        h_ref[x + 1, y + 1] = act
        s_ref[x - base, y] = slope

    first_rows(plan, weight_matrix(w_ref, plan.chan), bias_column(w_ref), a_ref, start, count, put)
    for copy in copies:
        copy.wait()


def grads(plan, get, f_ref, sh_ref, acc_ref, g_ref):
    group, nz, ny, chan = plan.group, plan.nz, plan.ny, plan.chan
    rows = pl.ds(plan.chan_at(0), group)
    own = plan.own()
    zero = jnp.zeros((3 * group, nz), BF)

    def shift(t, total):
        sh_ref[t, 0] = zero
        sh_ref[t, ny + 1] = zero
        for y in range(ny):
            value = get(t, y, rows).astype(F32)
            total = total + value
            sh_ref[t, y + 1] = jnp.concatenate([z_shift(value, -1), value, z_shift(value, 1)], axis=0).astype(BF)
        return total

    total = lax.fori_loop(0, plan.layers, shift, jnp.zeros((group, nz), F32), unroll=True)
    total_w = jnp.zeros(acc_ref.shape, F32)
    for t in range(plan.layers):
        x = own + t
        left = jnp.concatenate(
            [jnp.concatenate([sh_ref[t, y + 2 - ky] for y in range(ny)], axis=1) for ky in range(3)], axis=0
        )
        right = jnp.concatenate(
            [jnp.concatenate([f_ref[x + kx, y + 1] for y in range(ny)], axis=1) for kx in range(3)], axis=0
        )
        total_w += lax.dot_general(left, right, (((1,), (1,)), ((), ())), preferred_element_type=F32)
    acc_ref[...] = total_w
    n = 9 * group
    g_ref[0:n] = acc_ref[:, 0 : 2 * chan]
    last = acc_ref[:, 2 * chan :]
    g_ref[n : n + n // 2] = jnp.concatenate([last[: n // 2], last[n // 2 :]], axis=1)
    g_ref[n + n // 2 :] = jnp.broadcast_to(jnp.sum(total, axis=1, keepdims=True), (group, 2 * chan))


def second_kernel(plan, places, *refs):
    n = len(places)
    pieces = refs[:n]
    weights = pieces[: plan.groups]
    h_ref, d_ref, o_ref, g_ref, t_ref, u_ref, w_ref, p_ref, sh_ref, acc_ref, sem, wsem = refs[n:]
    load_weight(plan, weights, w_ref, wsem, True)
    load_pieces(plan, pieces, places, u_ref, sem, True, halo=True)
    zero_edges(plan, d_ref)
    load_weight(plan, weights, w_ref, wsem, False)
    turn(w_ref, t_ref, plan.chan)
    load_pieces(plan, pieces, places, u_ref, sem, False, halo=True)
    start = plan.start(1)
    m_ref = weight_matrix(w_ref, plan.chan)
    bias = bias_column(w_ref)

    def body(t, carry):
        x = start + t

        def each(y, value):
            pre = value + bias
            p_ref[t, y] = pre
            d_ref[x + 1, y + 1] = (u_ref[t, y].astype(F32) * slope_of(pre)).astype(BF)

        conv_rows(m_ref, h_ref, x, each)
        return carry

    lax.fori_loop(0, plan.count(1), body, 0, unroll=True)
    rows = pl.ds(plan.chan_at(0), plan.group)
    own = plan.own()
    first = own - start
    for t in range(plan.layers):
        o_ref[:, t] = jnp.transpose(smooth(p_ref[first + t, :, rows, :]), (1, 0, 2)).astype(BF)
    grads(plan, lambda t, y, rows: d_ref[own + t + 1, y + 1, rows, :], h_ref, sh_ref, acc_ref, g_ref)


def turn(w_ref, out, chan):
    for kz in range(3):
        turned = [jnp.transpose(slot(w_ref, 3 * pair + 2 - kz).astype(F32), (1, 0)) for pair in range(5)]
        for pair in range(5):
            low = turned[4 - pair][:chan]
            if pair < 4:
                block = jnp.concatenate([low, turned[3 - pair][chan:]], axis=1)
                out[kz, :, 2 * chan * pair : 2 * chan * (pair + 1)] = block.astype(BF)
            else:
                out[kz, :, 2 * chan * pair :] = low.astype(BF)


def turn_kernel(plan, *refs):
    out, w_ref, sem = refs[plan.groups :]
    for go in (True, False):
        load_weight(plan, refs[: plan.groups], w_ref, sem, go)
    turn(w_ref, out, plan.chan)


def third_kernel(plan, places, *refs):
    n = len(places)
    pieces = refs[:n]
    s_ref, d2_ref, t_ref, d_ref, g_ref, a_ref, sh_ref, acc_ref, sem = refs[n:]
    load_pieces(plan, pieces, places, a_ref, sem, True)
    zero_edges(plan, a_ref)
    start = plan.own()
    skip = start - plan.start(2)
    m_ref = t_ref[...].reshape(3 * plan.chan, 9 * plan.chan)

    def body(t, carry):
        def each(y, value):
            d_ref[t, y] = (value * s_ref[skip + t, y]).astype(BF)

        conv_rows(m_ref, d2_ref, start + t, each)
        return carry

    lax.fori_loop(0, plan.layers, body, 0, unroll=True)
    load_pieces(plan, pieces, places, a_ref, sem, False)
    grads(plan, lambda t, y, rows: d_ref[t, y, rows, :], a_ref, sh_ref, acc_ref, g_ref)


def fourth_kernel(plan, d_ref, t_ref, r_ref, *refs):
    *outs, a_ref, sem = refs
    layers, ny = plan.layers, plan.ny
    copy = pltpu.make_async_copy(d_ref, a_ref.at[pl.ds(2, layers), pl.ds(1, ny)], sem)
    copy.start()
    zero_rows(a_ref)
    for x in (0, 1, layers + 2, layers + 3):
        zero_layer(a_ref, x)
    copy.wait()
    rows = pl.ds(plan.chan_at(0), plan.group)
    m_ref = t_ref[:, rows, :].reshape(3 * plan.group, 9 * plan.chan)
    for t in range(layers):

        def each(y, value, t=t):
            r_ref[t, y] = value

        conv_rows(m_ref, a_ref, t + 1, each)
    if plan.pair:
        places = [(1 - lax.axis_index("space")) * (layers + 1)]
    else:
        places = [0, layers + 1]
    for out, place in zip(outs, places):

        def beside(y, value, out=out):
            out[y * plan.group : (y + 1) * plan.group] = value.astype(BF)

        conv_rows(m_ref, a_ref, place, beside)


def finish_volume(plan, r_ref, shares, o_ref):
    layers, ny, group = plan.layers, plan.ny, plan.group
    for layer, ref, base in shares:
        for y in range(ny):
            r_ref[layer, y] += ref[base + y * group : base + (y + 1) * group].astype(F32)
    for t in range(layers):
        o_ref[:, t] = jnp.transpose(r_ref[t], (1, 0, 2)).astype(BF)


def finish_kernel(plan, r_hbm, low_ref, high_ref, o_ref, r_ref, sem):
    copy = pltpu.make_async_copy(r_hbm, r_ref, sem)
    copy.start()
    copy.wait()
    finish_volume(plan, r_ref, [(0, low_ref, 0), (plan.layers - 1, high_ref, 0)], o_ref)


def to_wire(values, rows):
    row = lax.broadcasted_iota(jnp.int32, values.shape, 0)
    lane = lax.broadcasted_iota(jnp.int32, values.shape, 1)
    high = values.astype(BF).astype(F32)
    second = jnp.logical_and(row >= rows, lane >= values.shape[1] // 2)
    return jnp.where(second, values - high, high).astype(BF)


def add_wire(values, wire, rows):
    got = wire.astype(F32)
    row = lax.broadcasted_iota(jnp.int32, values.shape, 0)
    return values + got + jnp.where(row >= rows, pltpu.roll(got, values.shape[1] // 2, 1), 0.0)


def wire_kernel(rows, a_ref, w_ref):
    w_ref[...] = to_wire(a_ref[...], rows)


def step_kernel(rows, a_ref, got_ref, o_ref, w_ref):
    total = add_wire(a_ref[...], got_ref[...], rows)
    o_ref[...] = total
    w_ref[...] = to_wire(total, rows)


def join_kernel(rows, a_ref, got_ref, share_ref, o_ref, w_ref):
    total = add_wire(a_ref[...], got_ref[...], rows)
    o_ref[...] = total
    w_ref[: total.shape[0]] = to_wire(total, rows)
    w_ref[total.shape[0] :] = share_ref[...]


def close_kernel(plan, rows, scale, r_hbm, a1_ref, got1_ref, a2_ref, got2_ref, *refs):
    w1_ref, b1_ref, w2_ref, b2_ref, o_ref, r_ref, sem = refs
    copy = pltpu.make_async_copy(r_hbm, r_ref, sem)
    copy.start()
    last_kernel(rows, plan.group, scale, a1_ref, got1_ref, w1_ref, b1_ref)
    last_kernel(rows, plan.group, scale, a2_ref, got2_ref, w2_ref, b2_ref)
    copy.wait()
    layer = (1 - lax.axis_index("space")) * (plan.layers - 1)
    finish_volume(plan, r_ref, [(layer, got2_ref, a2_ref.shape[0])], o_ref)


def last_kernel(rows, group, scale, a_ref, got_ref, w_ref, b_ref):
    total = add_wire(a_ref[...], got_ref[: a_ref.shape[0]], rows) * scale
    n = 9 * group
    chan = total.shape[1] // 2
    w_ref[0:9] = total[:n, :chan].reshape(9, group, chan)
    w_ref[9:18] = total[:n, chan:].reshape(9, group, chan)
    tail = total[n : n + n // 2]
    w_ref[18:27] = jnp.concatenate([tail[:, :chan], tail[:, chan:]], axis=0).reshape(9, group, chan)
    col = total[rows:, :group]
    eye = lax.broadcasted_iota(jnp.int32, (group, group), 0) == lax.broadcasted_iota(
        jnp.int32, (group, group), 1
    )
    b_ref[...] = jnp.sum(jnp.where(eye, col, 0.0), axis=0, keepdims=True)


def rounds(plan):
    out = []
    for axis in ("space", "rep"):
        size, bit = lax.axis_size(axis), 1
        while bit < size:
            out.append((axis, bit))
            bit *= 2
    return out


def exchange(wire, step):
    axis, bit = step
    return lax.ppermute(wire, axis, [(i, i ^ bit) for i in range(lax.axis_size(axis))])


def first_wire(part, plan):
    rows = part.shape[0] - plan.group
    return call(functools.partial(wire_kernel, rows), shape(part.shape, BF), 0, 1, name="wire")(part)


def grad_shapes(plan):
    return shape((27, plan.group, plan.chan), F32), shape((1, plan.group), F32)


def as_grads(weight, bias, plan):
    weight = jnp.transpose(weight.reshape(3, 3, 3, plan.group, plan.chan), (3, 4, 0, 1, 2))
    return weight, bias.reshape(plan.group)


def total_step(part, got, step, plan, share=None):
    rows = part.shape[0] - plan.group
    kernel, args, more = step_kernel, (part, got), 0
    if share is not None:
        kernel, args, more = join_kernel, (part, got, share), share.shape[0]
    part, wire = call(
        functools.partial(kernel, rows),
        (shape(part.shape, F32), shape((part.shape[0] + more, part.shape[1]), BF)),
        0,
        len(args),
        name="step",
    )(*args)
    return part, exchange(wire, step)


def total_last(part, got, plan, scale):
    rows = part.shape[0] - plan.group
    weight, bias = call(
        functools.partial(last_kernel, rows, plan.group, scale), grad_shapes(plan), 0, 2, name="last"
    )(part, got)
    return as_grads(weight, bias, plan)


def local(volume, weight1, bias1, weight2, bias2, upstream):
    _, group, layers, ny, nz = volume.shape
    chan = weight1.shape[1]
    spaces, groups = lax.axis_size("space"), lax.axis_size("filt")
    plan = Plan(layers, ny, nz, chan, groups, spaces)
    scale = 1.0 / math.sqrt(lax.axis_size("rep") * spaces * layers * ny * nz)

    cells = ny * nz
    conv = 2 * 27 * chan * chan * cells
    slots = VM((16 // ny, ny, chan, 2 * chan), BF)
    dma = pltpu.SemaphoreType.DMA
    padded = plan.padded()
    grad_rows = 27 * group // 2 + group
    grad_scratch = [VM((layers, ny + 2, 3 * group, nz), BF), VM((9 * group, 3 * chan), F32)]

    def early_layers(pieces):
        return call(
            functools.partial(early_kernel, plan, [p[1:] for p in pieces]),
            (shape((layers - 1, ny, chan, nz), BF), shape((layers - 1, ny, chan, nz), F32)),
            len(pieces),
            0,
            [VM(padded, BF), slots, dma((len(pieces),)), dma((groups,))],
            flops=1,
            name="early",
        )(*(p[0] for p in pieces))

    gather = gather_quick if plan.quick else gather_plain
    v_own, v_other, u_own, u_other, early = gather(
        volume[0], weight1, bias1, upstream[0], weight2, bias2, plan, early_layers
    )
    v_places = [p[1:] for p in v_own + v_other]
    u_places = [p[1:] for p in u_own + u_other]
    v_all = [p[0] for p in v_own + v_other]
    u_all = [p[0] for p in u_own + u_other]

    turned1 = call(
        functools.partial(turn_kernel, plan),
        shape((3, chan, 9 * chan), BF),
        groups,
        0,
        [slots, dma((groups,))],
        moved=2 << 20,
        name="turn",
    )(*v_all[:groups])

    hidden, slope = call(
        functools.partial(first_kernel, plan, v_places),
        (shape(padded, BF), shape((plan.count(2), ny, chan, nz), F32)),
        len(v_all) + len(early),
        0,
        [VM(padded, BF), slots, dma((len(v_all),)), dma((groups,)), dma((2,))],
        flops=1,
        name="first",
    )(*v_all, *early)

    if plan.quick:
        u_all[3] = flip_perm(after(u_all[2], hidden), 1)
    delta2, output, part2, turned2 = call(
        functools.partial(second_kernel, plan, u_places),
        (
            shape(padded, BF),
            shape((group, layers, ny, nz), BF),
            shape((grad_rows, 2 * chan), F32),
            shape((3, chan, 9 * chan), BF),
        ),
        len(u_all),
        1,
        [
            VM((plan.count(1), ny, chan, nz), BF),
            slots,
            VM((plan.count(1), ny, chan, nz), F32),
            *grad_scratch,
            dma((len(u_all),)),
            dma((groups,)),
        ],
        flops=1,
        name="second",
    )(*u_all, hidden)

    delta1, part1 = call(
        functools.partial(third_kernel, plan, v_places),
        (shape((layers, ny, chan, nz), BF), shape((grad_rows, 2 * chan), F32)),
        len(v_all),
        3,
        [VM(padded, BF), *grad_scratch, dma((len(v_all),))],
        flops=1,
        name="third",
    )(*v_all, slope, delta2, turned2)

    beside = [shape((ny * group, nz), BF)] * plan.sides
    own_grad, *shares = call(
        functools.partial(fourth_kernel, plan),
        (shape((layers, ny, group, nz), F32), *beside),
        1,
        1,
        [VM((layers + 4, ny + 2, chan, nz), BF), dma],
        flops=1,
        name="fourth",
    )(delta1, turned1)

    steps1 = rounds(plan)
    steps2 = steps1[1:] + steps1[:1]
    got1 = exchange(first_wire(part1, plan), steps1[0])
    got2 = exchange(first_wire(part2, plan), steps2[0])
    for step in steps1[1:]:
        part1, got1 = total_step(part1, got1, step, plan)
    for n, step in enumerate(steps2[1:], 2):
        share = shares[0] if plan.pair and n == len(steps2) else None
        part2, got2 = total_step(part2, got2, step, plan, share)
    volume_shape = shape((group, layers, ny, nz), BF)
    finish_scratch = [VM((layers, ny, group, nz), F32), dma]
    if plan.pair:
        w1, b1, w2, b2, volume_grad = call(
            functools.partial(close_kernel, plan, part2.shape[0] - group, scale),
            (*grad_shapes(plan), *grad_shapes(plan), volume_shape),
            1,
            4,
            finish_scratch,
            name="close",
        )(own_grad, part1, got1, part2, got2)
        grad1, bias_grad1 = as_grads(w1, b1, plan)
        grad2, bias_grad2 = as_grads(w2, b2, plan)
    else:
        grad1, bias_grad1 = total_last(part1, got1, plan, scale)
        grad2, bias_grad2 = total_last(part2, got2, plan, scale)
        volume_grad = call(
            functools.partial(finish_kernel, plan), volume_shape, 1, 2, finish_scratch, name="finish"
        )(own_grad, up(shares[1]), down(shares[0]))
    return (output[None], volume_grad[None], grad1, bias_grad1, grad2, bias_grad2)


def solution(mesh):
    field = P("rep", "filt", "space", None, None)
    kernel = P("filt", None, None, None, None)
    return jax.shard_map(
        local,
        mesh=mesh,
        in_specs=(field, kernel, P("filt"), kernel, P("filt"), field),
        out_specs=(field, field, kernel, P("filt"), kernel, P("filt")),
        check_vma=False,
    )
```

```python
import functools
import math

import jax
import jax.numpy as jnp
from jax import lax
from jax.experimental import pallas as pl
from jax.experimental.pallas import tpu as pltpu
from jax.sharding import PartitionSpec as P

SLOPE = 0.3
NEAR = 3
BF = jnp.bfloat16
F32 = jnp.float32
VM = pltpu.VMEM
ANY = pl.BlockSpec(memory_space=pl.ANY)
WHOLE = pl.BlockSpec(memory_space=pltpu.VMEM)


def call(kernel, outs, n_any, n_vmem, scratch=(), flops=0, moved=0, name=None):
    return pl.pallas_call(
        kernel,
        out_shape=outs,
        in_specs=[ANY] * n_any + [WHOLE] * n_vmem,
        out_specs=jax.tree.map(lambda _: WHOLE, outs),
        scratch_shapes=list(scratch),
        compiler_params=pltpu.CompilerParams(vmem_limit_bytes=40 << 20),
        cost_estimate=pl.CostEstimate(flops=flops, bytes_accessed=moved, transcendentals=0),
        name=name,
    )


def shape(dims, kind):
    return jax.ShapeDtypeStruct(tuple(dims), kind)


def parts(values):
    e = jnp.exp(-jnp.abs(values))
    one = 1.0 + e
    soft = jnp.maximum(values, 0.0) + jnp.log(one)
    sig = jnp.where(values >= 0.0, 1.0, e) / one
    return SLOPE * values + (1.0 - SLOPE) * soft, SLOPE + (1.0 - SLOPE) * sig


def slope_of(values):
    e = jnp.exp(-jnp.abs(values))
    return SLOPE + (1.0 - SLOPE) * (jnp.where(values >= 0.0, 1.0, e) / (1.0 + e))


def smooth(values):
    e = jnp.exp(-jnp.abs(values))
    soft = jnp.maximum(values, 0.0) + jnp.log(1.0 + e)
    return SLOPE * values + (1.0 - SLOPE) * soft


def swap(block):
    return jnp.transpose(block.astype(F32), (1, 0, 2))


def pack_weight(w_ref, b_ref, o_ref, base):
    group, chan, ny = w_ref.shape[1], w_ref.shape[2], o_ref.shape[1]
    for pair in range(5):
        for kz in range(3):
            low = w_ref[6 * pair + kz]
            if pair < 4:
                high = w_ref[6 * pair + 3 + kz]
            else:
                high = jnp.zeros_like(low)
            slot = 3 * pair + kz
            o_ref[base + slot // ny, slot % ny] = jnp.concatenate([low, high], axis=1)
    eye = lax.broadcasted_iota(jnp.int32, (group, group), 0) == lax.broadcasted_iota(
        jnp.int32, (group, group), 1
    )
    col = jnp.sum(jnp.where(eye, jnp.broadcast_to(b_ref[...], (group, group)), 0.0), axis=1, keepdims=True)
    col = jnp.broadcast_to(col, (group, 2 * chan))
    first = col.astype(BF)
    rest = col - first.astype(F32)
    second = rest.astype(BF)
    third = (rest - second.astype(F32)).astype(BF)
    lane = lax.broadcasted_iota(jnp.int32, (group, 2 * chan), 1)
    picked = jnp.where(lane == 0, first.astype(F32), jnp.where(lane == 1, second.astype(F32), third.astype(F32)))
    o_ref[base + 15 // ny, 15 % ny] = picked.astype(BF)


def pack_kernel(edge, *refs):
    if edge:
        f_hbm, w_hbm, b_hbm, n_hbm, o_ref, e_ref, f_ref, w_ref, b_ref, n_ref, sem = refs
    else:
        f_hbm, w_hbm, b_hbm, o_ref, f_ref, w_ref, b_ref, sem = refs
    layers = f_ref.shape[1]
    pairs = [(f_hbm, f_ref), (w_hbm, w_ref), (b_hbm, b_ref)]
    if edge:
        facing = 1 - lax.axis_index("space")
        pairs.append((n_hbm.at[:, pl.ds(facing * (layers - 1), 1)], n_ref))
    copies = [pltpu.make_async_copy(src, dst, sem.at[n]) for n, (src, dst) in enumerate(pairs)]
    for copy in copies:
        copy.start()
    copies[0].wait()
    for x in range(layers):
        o_ref[x] = swap(f_ref[:, x]).astype(BF)
    if edge:
        copies[3].wait()
        for x in range(edge):
            e_ref[x] = o_ref[facing * (layers - edge) + x]
        e_ref[edge] = swap(n_ref[:, 0]).astype(BF)
    copies[1].wait()
    copies[2].wait()
    pack_weight(w_ref, b_ref, o_ref, layers)


def pack(field, weight, bias, name, beside=None, edge=0):
    group, layers, ny, nz = field.shape
    chan = weight.shape[1]
    taps = jnp.transpose(weight, (2, 3, 4, 0, 1)).reshape(27, group, chan)
    args = [field, taps, bias.reshape(1, group)]
    outs = [shape((layers + 16 // ny, ny, group, nz), BF)]
    scratch = [VM(field.shape, BF), VM((27, group, chan), BF), VM((1, group), F32)]
    if edge:
        args.append(beside)
        outs.append(shape((edge + 1, ny, group, nz), BF))
        scratch.append(VM((group, 1, ny, nz), BF))
    return pl.pallas_call(
        functools.partial(pack_kernel, edge),
        out_shape=tuple(outs),
        in_specs=[pl.BlockSpec(memory_space=pltpu.HBM)] * len(args),
        out_specs=(WHOLE,) * len(outs),
        scratch_shapes=scratch + [pltpu.SemaphoreType.DMA((len(args),))],
        compiler_params=pltpu.CompilerParams(vmem_limit_bytes=40 << 20),
        cost_estimate=pl.CostEstimate(flops=0, bytes_accessed=field.size * 4, transcendentals=0),
        name=name,
    )(*(pltpu.with_memory_space_constraint(v, pltpu.HBM) for v in args))


class Plan:
    def __init__(self, layers, ny, nz, chan, groups, spaces):
        self.layers, self.ny, self.nz, self.chan = layers, ny, nz, chan
        self.groups, self.spaces = groups, spaces
        self.group = chan // groups
        self.pair = spaces == 2
        self.quick = self.pair and groups == 4
        self.window = (2 if self.pair else 3) * layers
        self.sides = 1 if self.pair else 2

    def start(self, reach):
        if self.pair:
            return lax.axis_index("space") * (self.layers - reach)
        return self.layers - reach

    def count(self, reach):
        return self.layers + self.sides * reach

    def own(self):
        return self.start(0)

    def inside(self, layer):
        if self.pair:
            return None
        at = (lax.axis_index("space") - 1) * self.layers + layer
        return jnp.logical_and(at >= 0, at < self.spaces * self.layers)

    def chan_at(self, flip):
        return pl.multiple_of((lax.axis_index("filt") ^ flip) * self.group, self.group)

    def padded(self):
        return (self.window + 2, self.ny + 2, self.chan, self.nz)


def flip_perm(value, flip):
    n = lax.axis_size("filt")
    return lax.ppermute(value, "filt", [(i, i ^ flip) for i in range(n)])


def over(value):
    return lax.ppermute(value, "space", [(0, 1), (1, 0)])


def up(value):
    n = lax.axis_size("space")
    return lax.ppermute(value, "space", [(i, i + 1) for i in range(n - 1)])


def down(value):
    n = lax.axis_size("space")
    return lax.ppermute(value, "space", [(i + 1, i) for i in range(n - 1)])


def after(value, *others):
    return lax.optimization_barrier((value, *others))[0]


def gather_quick(volume, weight1, bias1, upstream, weight2, bias2, plan, early_layers):
    n = plan.layers
    packed, edge = pack(volume, weight1, bias1, "pack1", upstream, NEAR)
    x = flip_perm(packed, 2)
    y = over(edge)
    c = flip_perm(packed, 1)
    (second,) = pack(after(upstream, c), weight2, bias2, "pack2")
    y, x = lax.optimization_barrier((y, x, second))[:2]
    d = flip_perm(y, 2)
    xc = flip_perm(x, 1)
    yc = flip_perm(y, 1)
    x2 = flip_perm(second, 2)
    c2 = flip_perm(second, 1)
    early, ahead = early_layers([(v, 0, n, "own", 0, k) for k, v in enumerate([packed, c, x, xc])], (second, c2))
    dc = flip_perm(after(d, ahead[0]), 1)
    own, other, own2 = [packed, c, x, xc], [y, yc, d, dc], [second, c2, x2, x2]
    return (
        [(v, 0, n, "own", 0, k) for k, v in enumerate(own)],
        [(v, 0, NEAR, "other", 0, k) for k, v in enumerate(other)],
        [(v, 0, n, "own", 0, k) for k, v in enumerate(own2)],
        [(v, NEAR, 1, "halo", 0, k) for k, v in enumerate(other)],
        early,
        ahead,
    )


def gather_plain(volume, weight1, bias1, upstream, weight2, bias2, plan, early_layers):
    n = plan.layers
    (packed,) = pack(volume, weight1, bias1, "pack1")
    (second,) = pack(upstream, weight2, bias2, "pack2")
    own, other, own2, halo = [], [], [], []
    for flip in range(plan.groups):
        mine = flip_perm(packed, flip) if flip else packed
        mine2 = flip_perm(second, flip) if flip else second
        own.append((mine, 0, n, "own", 0, flip))
        own2.append((mine2, 0, n, "own", 0, flip))
        if plan.pair:
            facing = 1 - lax.axis_index("space")
            near = lax.dynamic_slice_in_dim(mine, facing * (n - NEAR), NEAR, axis=0)
            other.append((over(near), 0, NEAR, "other", 0, flip))
            near = lax.dynamic_slice_in_dim(mine2, facing * (n - 1), 1, axis=0)
            halo.append((over(near), 0, 1, "halo", 0, flip))
        else:
            other.append((up(mine[n - NEAR : n]), 0, NEAR, "low", 0, flip))
            other.append((down(mine[:NEAR]), 0, NEAR, "high", 0, flip))
            halo.append((up(mine2[n - 1 : n]), 0, 1, "low", 0, flip))
            halo.append((down(mine2[:1]), 0, 1, "high", 0, flip))
    return own, other, own2, halo, (), ()


def field_place(plan, place, k):
    n = plan.layers
    if plan.pair:
        s = lax.axis_index("space")
        return 1 + k + (s * n if place == "own" else n - NEAR * s)
    return 1 + k + {"low": n - NEAR, "own": n, "high": 2 * n}[place]


def halo_place(plan, place):
    if plan.pair:
        s = lax.axis_index("space")
        return s if place == "own" else (1 - s) * plan.layers
    return {"low": 0, "own": 1, "high": plan.layers + 1}[place]


def load_weight(plan, refs, dst, sem, start, flips=None):
    for n, ref in enumerate(refs):
        flip = flips[n] if flips else n
        copy = pltpu.make_async_copy(
            ref.at[pl.ds(ref.shape[0] - dst.shape[0], dst.shape[0])],
            dst.at[:, :, pl.ds(plan.chan_at(flip), plan.group), :],
            sem.at[n],
        )
        copy.start() if start else copy.wait()


def load_pieces(plan, refs, places, dst, sem, start, halo=False, near=False):
    for n, (ref, (first, count, place, k, flip)) in enumerate(zip(refs, places)):
        if near and place == "own":
            first = k = (1 - lax.axis_index("space")) * (plan.layers - 2)
            count = 2
        rows = pl.ds(plan.chan_at(flip), plan.group)
        if halo:
            target = dst.at[pl.ds(halo_place(plan, place), count), :, rows, :]
        else:
            target = dst.at[pl.ds(field_place(plan, place, k), count), pl.ds(1, plan.ny), rows, :]
        copy = pltpu.make_async_copy(ref.at[pl.ds(first, count)], target, sem.at[n])
        copy.start() if start else copy.wait()


def zero_rows(ref):
    zero = jnp.zeros(ref.shape[2:], ref.dtype)
    for x in range(ref.shape[0]):
        ref[x, 0] = zero
        ref[x, ref.shape[1] - 1] = zero


def zero_layer(ref, x):
    zero = jnp.zeros(ref.shape[2:], ref.dtype)
    for y in range(1, ref.shape[1] - 1):
        ref[x, y] = zero


def zero_edges(plan, ref):
    zero_rows(ref)
    zero_layer(ref, 0)
    zero_layer(ref, ref.shape[0] - 1)


def slot(w_ref, n, rows=slice(None)):
    return w_ref[n // w_ref.shape[1], n % w_ref.shape[1], rows, :]


def weight_matrix(w_ref, chan, rows=slice(None)):
    cols = []
    for pair in range(5):
        block = jnp.concatenate([slot(w_ref, 3 * pair + kz, rows) for kz in range(3)], axis=0)
        cols.append(block if pair < 4 else block[:, :chan])
    return jnp.concatenate(cols, axis=1)


def bias_column(w_ref, rows=slice(None)):
    terms = slot(w_ref, 15, rows).astype(F32)
    return terms[:, 0:1] + terms[:, 1:2] + terms[:, 2:3]


def taps(field_ref, x, y):
    c, nz = field_ref.shape[2], field_ref.shape[3]
    rows = []
    for kx in range(3):
        first = field_ref[x + kx, y : y + 3].reshape(3 * c, nz)
        second = field_ref[x + kx, y + 1 : y + 4].reshape(3 * c, nz)
        rows.append(jnp.concatenate([first, second], axis=1))
    return jnp.concatenate(rows, axis=0)


def z_shift(values, by):
    nz = values.shape[1]
    lane = lax.broadcasted_iota(jnp.int32, values.shape, 1)
    if by > 0:
        return jnp.where(lane == 0, 0.0, pltpu.roll(values, 1, 1))
    return jnp.where(lane == nz - 1, 0.0, pltpu.roll(values, nz - 1, 1))


def z_sum(product, rows, half, nz):
    part = product[:, half * nz : (half + 1) * nz]
    return part[rows : 2 * rows] + z_shift(part[:rows], 1) + z_shift(part[2 * rows :], -1)


def conv_rows(weight, field_ref, x, each):
    ny, nz = field_ref.shape[1] - 2, field_ref.shape[3]
    rows = weight.shape[0] // 3
    for y in range(0, ny, 2):
        product = jnp.dot(weight, taps(field_ref, x, y), preferred_element_type=F32)
        for half in range(2):
            each(y + half, z_sum(product, rows, half, nz))


def first_rows(plan, weight, bias, a_ref, start, count, put):
    def body(t, carry):
        x = start + t
        inside = plan.inside(x)

        def each(y, value):
            act, slope = parts(value + bias)
            if inside is not None:
                act = jnp.where(inside, act, 0.0)
            put(t, x, y, act.astype(BF), slope)

        conv_rows(weight, a_ref, x, each)
        return carry

    lax.fori_loop(0, count, body, 0, unroll=True)


def early_kernel(plan, places, *refs):
    n = len(places)
    pieces = refs[:n]
    h_ref, s_ref, a_ref, w_ref, sem, wsem = refs[n:]
    load_weight(plan, pieces[: plan.groups], w_ref, wsem, True)
    load_pieces(plan, pieces, places, a_ref, sem, True)
    zero_edges(plan, a_ref)
    load_weight(plan, pieces[: plan.groups], w_ref, wsem, False)
    load_pieces(plan, pieces, places, a_ref, sem, False)

    def put(t, x, y, act, slope):
        h_ref[t, y] = act
        s_ref[t, y] = slope

    start = lax.axis_index("space") * (plan.layers + 1)
    first_rows(plan, weight_matrix(w_ref, plan.chan), bias_column(w_ref), a_ref, start, plan.layers - 1, put)


def first_kernel(plan, places, *refs):
    n = len(places)
    pieces, refs = refs[:n], refs[n:]
    if plan.quick:
        eh_ref, es_ref, refs = refs[0], refs[1], refs[2:]
    h_ref, s_ref, a_ref, w_ref, sem, wsem, esem = refs
    load_weight(plan, pieces[: plan.groups], w_ref, wsem, True)
    load_pieces(plan, pieces, places, a_ref, sem, True, near=plan.quick)
    zero_edges(plan, a_ref)
    zero_edges(plan, h_ref)
    base = plan.start(2)
    start, count = base, plan.count(2)
    copies = []
    if plan.quick:
        s = lax.axis_index("space")
        done = s * (plan.layers + 1)
        start, count = plan.layers - 1 - s, count - plan.layers + 1
        copies = [
            pltpu.make_async_copy(
                eh_ref, h_ref.at[pl.ds(done + 1, plan.layers - 1), pl.ds(1, plan.ny)], esem.at[0]
            ),
            pltpu.make_async_copy(es_ref, s_ref.at[pl.ds(done - base, plan.layers - 1)], esem.at[1]),
        ]
    for copy in copies:
        copy.start()
    load_weight(plan, pieces[: plan.groups], w_ref, wsem, False)
    load_pieces(plan, pieces, places, a_ref, sem, False, near=plan.quick)

    def put(t, x, y, act, slope):
        h_ref[x + 1, y + 1] = act
        s_ref[x - base, y] = slope

    first_rows(plan, weight_matrix(w_ref, plan.chan), bias_column(w_ref), a_ref, start, count, put)
    for copy in copies:
        copy.wait()


def grad_sums(plan, count, get, f_ref, base, sh_ref):
    group, nz, ny, chan = plan.group, plan.nz, plan.ny, plan.chan
    zero = jnp.zeros((3 * group, nz), BF)
    total = jnp.zeros((group, nz), F32)
    sums = jnp.zeros((9 * group, 3 * chan), F32)
    for t in range(count):
        sh_ref[t, 0] = zero
        sh_ref[t, ny + 1] = zero
        for y in range(ny):
            value = get(t, y).astype(F32)
            total = total + value
            sh_ref[t, y + 1] = jnp.concatenate([z_shift(value, -1), value, z_shift(value, 1)], axis=0).astype(BF)
    for t in range(count):
        left = jnp.concatenate(
            [jnp.concatenate([sh_ref[t, y + 2 - ky] for y in range(ny)], axis=1) for ky in range(3)], axis=0
        )
        right = jnp.concatenate(
            [jnp.concatenate([f_ref[base + t + kx, y + 1] for y in range(ny)], axis=1) for kx in range(3)], axis=0
        )
        sums += lax.dot_general(left, right, (((1,), (1,)), ((), ())), preferred_element_type=F32)
    return sums, total


def pack_grads(plan, sums, total, acc_ref, g_ref):
    group, chan = plan.group, plan.chan
    acc_ref[...] = sums
    n = 9 * group
    g_ref[0:n] = acc_ref[:, 0 : 2 * chan]
    last = acc_ref[:, 2 * chan :]
    g_ref[n : n + n // 2] = jnp.concatenate([last[: n // 2], last[n // 2 :]], axis=1)
    g_ref[n + n // 2 :] = jnp.broadcast_to(jnp.sum(total, axis=1, keepdims=True), (group, 2 * chan))


def grads(plan, get, f_ref, sh_ref, acc_ref, g_ref):
    rows = pl.ds(plan.chan_at(0), plan.group)
    sums, total = grad_sums(plan, plan.layers, lambda t, y: get(t, y, rows), f_ref, plan.own(), sh_ref)
    pack_grads(plan, sums, total, acc_ref, g_ref)


def second_rows(plan, rows, h_ref, u_ref, w_ref, put, first, count, layer):
    matrix = weight_matrix(w_ref, plan.chan, rows)
    bias = bias_column(w_ref, rows)
    for n in range(count):

        def each(y, value, t=first + n, x=layer + n):
            pre = value + bias
            delta = (u_ref[t, y, rows, :].astype(F32) * slope_of(pre)).astype(BF)
            put(t, x, y, pre, delta)

        conv_rows(matrix, h_ref, layer + n, each)


def put_output(plan, p_ref, rows, o_ref):
    first = plan.own() - plan.start(1)
    for t in range(plan.layers):
        o_ref[:, t] = jnp.transpose(smooth(p_ref[first + t, :, rows, :]), (1, 0, 2)).astype(BF)


def second_kernel(plan, places, *refs):
    n = len(places)
    pieces = refs[:n]
    weights = pieces[: plan.groups]
    h_ref, d_ref, o_ref, g_ref, t_ref, u_ref, w_ref, p_ref, sh_ref, acc_ref, sem, wsem = refs[n:]
    load_weight(plan, weights, w_ref, wsem, True)
    load_pieces(plan, pieces, places, u_ref, sem, True, halo=True)
    zero_edges(plan, d_ref)
    load_weight(plan, weights, w_ref, wsem, False)
    turn(w_ref, t_ref, plan.chan)
    load_pieces(plan, pieces, places, u_ref, sem, False, halo=True)

    def put(t, x, y, pre, delta):
        p_ref[t, y] = pre
        d_ref[x + 1, y + 1] = delta

    second_rows(plan, pl.ds(0, plan.chan), h_ref, u_ref, w_ref, put, 0, plan.count(1), plan.start(1))
    put_output(plan, p_ref, pl.ds(plan.chan_at(0), plan.group), o_ref)
    own = plan.own()
    grads(plan, lambda t, y, rows: d_ref[own + t + 1, y + 1, rows, :], h_ref, sh_ref, acc_ref, g_ref)


def chip_rows(plan, other):
    half = plan.chan // 2
    return pl.ds(pl.multiple_of(((lax.axis_index("filt") >> 1) ^ other) * half, half), half)


def own_rows(plan):
    return pl.ds(pl.multiple_of((lax.axis_index("filt") & 1) * plan.group, plan.group), plan.group)


def ahead_kernel(plan, eh_hbm, own_hbm, chip_hbm, d_ref, o_ref, a_ref, b_ref, h_ref, u_ref, w_ref, p_ref, sh_ref, sem, wsem):
    s = lax.axis_index("space")
    count = plan.layers - 2
    load_weight(plan, (own_hbm, chip_hbm), w_ref, wsem, True, (0, 1))
    copies = [
        pltpu.make_async_copy(eh_hbm, h_ref.at[pl.ds(1 - s, count + 1), pl.ds(1, plan.ny)], sem.at[2])
    ]
    for flip, ref in enumerate((own_hbm, chip_hbm)):
        target = u_ref.at[:, :, pl.ds(plan.chan_at(flip), plan.group), :]
        copies.append(pltpu.make_async_copy(ref.at[pl.ds(2 * s, count)], target, sem.at[flip]))
    for copy in copies:
        copy.start()
    zero_rows(h_ref)
    zero_layer(h_ref, s * (count + 1))
    load_weight(plan, (own_hbm, chip_hbm), w_ref, wsem, False, (0, 1))
    for copy in copies:
        copy.wait()

    def put(t, x, y, pre, delta):
        p_ref[t, y] = pre
        d_ref[t, y] = delta

    second_rows(plan, chip_rows(plan, 0), h_ref, u_ref, w_ref, put, 0, count, 0)
    mine = own_rows(plan)
    for t in range(count):
        o_ref[:, t] = jnp.transpose(smooth(p_ref[t, :, mine, :]), (1, 0, 2)).astype(BF)
    a_ref[...], b_ref[...] = grad_sums(plan, count, lambda t, y: d_ref[t, y, mine, :], h_ref, 0, sh_ref)


def near_kernel(plan, places, *refs):
    n = len(places)
    pieces, ahead, refs = refs[:n], refs[n], refs[n + 1 :]
    h_ref, ao_ref, aa_ref, ab_ref, d_ref, o_ref, g_ref, u_ref, w_ref, p_ref, sh_ref, acc_ref, sem, wsem, asem = refs
    s = lax.axis_index("space")
    done = plan.layers - 2
    left = plan.count(1) - done
    load_weight(plan, pieces[:2], w_ref, wsem, True, (0, 1))
    load_pieces(plan, pieces, places, u_ref, sem, True, halo=True)
    copy = pltpu.make_async_copy(ahead, d_ref.at[pl.ds(s * left, done)], asem)
    copy.start()
    load_weight(plan, pieces[:2], w_ref, wsem, False, (0, 1))
    load_pieces(plan, pieces, places, u_ref, sem, False, halo=True)

    def put(t, x, y, pre, delta):
        p_ref[t, y] = pre
        d_ref[t, y] = delta

    start, first, slab = plan.start(1), (1 - s) * done, (1 - s) * done
    second_rows(plan, chip_rows(plan, 0), h_ref, u_ref, w_ref, put, first, left, start + first)
    mine = own_rows(plan)
    o_ref[:, pl.ds(2 * s, done)] = ao_ref[...]
    at = plan.own() - start + slab
    for t in range(2):
        value = jnp.transpose(smooth(p_ref[at + t, :, mine, :]), (1, 0, 2)).astype(BF)
        o_ref[:, pl.ds(slab + t, 1)] = value[:, None]
    sums, total = grad_sums(plan, 2, lambda t, y: d_ref[at + t, y, mine, :], h_ref, plan.own() + slab, sh_ref)
    pack_grads(plan, sums + aa_ref[...], total + ab_ref[...], acc_ref, g_ref)
    copy.wait()


def far_kernel(plan, places, *refs):
    n = len(places)
    pieces, weights, refs = refs[:n], refs[n : n + 4], refs[n + 4 :]
    near_ref, h_ref, d_ref, t_ref, u_ref, w_ref, sem, wsem, nsem = refs
    load_weight(plan, weights, w_ref, wsem, True)
    load_pieces(plan, pieces, places, u_ref, sem, True, halo=True)
    joined = d_ref.at[pl.ds(plan.start(1) + 1, plan.count(1)), pl.ds(1, plan.ny), chip_rows(plan, 0), :]
    copy = pltpu.make_async_copy(near_ref, joined, nsem)
    copy.start()
    zero_edges(plan, d_ref)
    load_weight(plan, weights, w_ref, wsem, False)
    turn(w_ref, t_ref, plan.chan)
    load_pieces(plan, pieces, places, u_ref, sem, False, halo=True)
    rows = chip_rows(plan, 1)

    def put(t, x, y, pre, delta):
        d_ref[x + 1, y + 1, rows, :] = delta

    second_rows(plan, rows, h_ref, u_ref, w_ref, put, 0, plan.count(1), plan.start(1))
    copy.wait()


def turn(w_ref, out, chan):
    for kz in range(3):
        turned = [jnp.transpose(slot(w_ref, 3 * pair + 2 - kz).astype(F32), (1, 0)) for pair in range(5)]
        for pair in range(5):
            low = turned[4 - pair][:chan]
            if pair < 4:
                block = jnp.concatenate([low, turned[3 - pair][chan:]], axis=1)
                out[kz, :, 2 * chan * pair : 2 * chan * (pair + 1)] = block.astype(BF)
            else:
                out[kz, :, 2 * chan * pair :] = low.astype(BF)


def turn_kernel(plan, *refs):
    out, w_ref, sem = refs[plan.groups :]
    for go in (True, False):
        load_weight(plan, refs[: plan.groups], w_ref, sem, go)
    turn(w_ref, out, plan.chan)


def third_kernel(plan, places, *refs):
    n = len(places)
    pieces = refs[:n]
    s_ref, d2_ref, t_ref, d_ref, g_ref, a_ref, sh_ref, acc_ref, sem = refs[n:]
    load_pieces(plan, pieces, places, a_ref, sem, True)
    zero_edges(plan, a_ref)
    start = plan.own()
    skip = start - plan.start(2)
    m_ref = t_ref[...].reshape(3 * plan.chan, 9 * plan.chan)

    def body(t, carry):
        def each(y, value):
            d_ref[t, y] = (value * s_ref[skip + t, y]).astype(BF)

        conv_rows(m_ref, d2_ref, start + t, each)
        return carry

    lax.fori_loop(0, plan.layers, body, 0, unroll=True)
    load_pieces(plan, pieces, places, a_ref, sem, False)
    grads(plan, lambda t, y, rows: d_ref[t, y, rows, :], a_ref, sh_ref, acc_ref, g_ref)


def fourth_kernel(plan, d_ref, t_ref, r_ref, *refs):
    *outs, a_ref, sem = refs
    layers, ny = plan.layers, plan.ny
    copy = pltpu.make_async_copy(d_ref, a_ref.at[pl.ds(2, layers), pl.ds(1, ny)], sem)
    copy.start()
    zero_rows(a_ref)
    for x in (0, 1, layers + 2, layers + 3):
        zero_layer(a_ref, x)
    copy.wait()
    rows = pl.ds(plan.chan_at(0), plan.group)
    m_ref = t_ref[:, rows, :].reshape(3 * plan.group, 9 * plan.chan)
    for t in range(layers):

        def each(y, value, t=t):
            r_ref[t, y] = value

        conv_rows(m_ref, a_ref, t + 1, each)
    if plan.pair:
        places = [(1 - lax.axis_index("space")) * (layers + 1)]
    else:
        places = [0, layers + 1]
    for out, place in zip(outs, places):

        def beside(y, value, out=out):
            out[y * plan.group : (y + 1) * plan.group] = value.astype(BF)

        conv_rows(m_ref, a_ref, place, beside)


def finish_volume(plan, r_ref, shares, o_ref):
    layers, ny, group = plan.layers, plan.ny, plan.group
    for layer, ref, base in shares:
        for y in range(ny):
            r_ref[layer, y] += ref[base + y * group : base + (y + 1) * group].astype(F32)
    for t in range(layers):
        o_ref[:, t] = jnp.transpose(r_ref[t], (1, 0, 2)).astype(BF)


def finish_kernel(plan, r_hbm, low_ref, high_ref, o_ref, r_ref, sem):
    copy = pltpu.make_async_copy(r_hbm, r_ref, sem)
    copy.start()
    copy.wait()
    finish_volume(plan, r_ref, [(0, low_ref, 0), (plan.layers - 1, high_ref, 0)], o_ref)


def to_wire(values, rows):
    row = lax.broadcasted_iota(jnp.int32, values.shape, 0)
    lane = lax.broadcasted_iota(jnp.int32, values.shape, 1)
    high = values.astype(BF).astype(F32)
    second = jnp.logical_and(row >= rows, lane >= values.shape[1] // 2)
    return jnp.where(second, values - high, high).astype(BF)


def add_wire(values, wire, rows):
    got = wire.astype(F32)
    row = lax.broadcasted_iota(jnp.int32, values.shape, 0)
    return values + got + jnp.where(row >= rows, pltpu.roll(got, values.shape[1] // 2, 1), 0.0)


def wire_kernel(rows, a_ref, w_ref):
    w_ref[...] = to_wire(a_ref[...], rows)


def step_kernel(rows, a_ref, got_ref, o_ref, w_ref):
    total = add_wire(a_ref[...], got_ref[...], rows)
    o_ref[...] = total
    w_ref[...] = to_wire(total, rows)


def join_kernel(rows, a_ref, got_ref, share_ref, o_ref, w_ref):
    total = add_wire(a_ref[...], got_ref[...], rows)
    o_ref[...] = total
    w_ref[: total.shape[0]] = to_wire(total, rows)
    w_ref[total.shape[0] :] = share_ref[...]


def close_kernel(plan, rows, scale, r_hbm, a1_ref, got1_ref, a2_ref, got2_ref, out_ref, *refs):
    w1_ref, b1_ref, w2_ref, b2_ref, o_ref, out2_ref, r_ref, sem = refs
    copy = pltpu.make_async_copy(r_hbm, r_ref, sem)
    copy.start()
    out2_ref[...] = out_ref[...]
    last_kernel(rows, plan.group, scale, a1_ref, got1_ref, w1_ref, b1_ref)
    last_kernel(rows, plan.group, scale, a2_ref, got2_ref, w2_ref, b2_ref)
    copy.wait()
    layer = (1 - lax.axis_index("space")) * (plan.layers - 1)
    finish_volume(plan, r_ref, [(layer, got2_ref, a2_ref.shape[0])], o_ref)


def last_kernel(rows, group, scale, a_ref, got_ref, w_ref, b_ref):
    total = add_wire(a_ref[...], got_ref[: a_ref.shape[0]], rows) * scale
    n = 9 * group
    chan = total.shape[1] // 2
    w_ref[0:9] = total[:n, :chan].reshape(9, group, chan)
    w_ref[9:18] = total[:n, chan:].reshape(9, group, chan)
    tail = total[n : n + n // 2]
    w_ref[18:27] = jnp.concatenate([tail[:, :chan], tail[:, chan:]], axis=0).reshape(9, group, chan)
    col = total[rows:, :group]
    eye = lax.broadcasted_iota(jnp.int32, (group, group), 0) == lax.broadcasted_iota(
        jnp.int32, (group, group), 1
    )
    b_ref[...] = jnp.sum(jnp.where(eye, col, 0.0), axis=0, keepdims=True)


def rounds(plan):
    out = []
    for axis in ("space", "rep"):
        size, bit = lax.axis_size(axis), 1
        while bit < size:
            out.append((axis, bit))
            bit *= 2
    return out


def exchange(wire, step):
    axis, bit = step
    return lax.ppermute(wire, axis, [(i, i ^ bit) for i in range(lax.axis_size(axis))])


def first_wire(part, plan):
    rows = part.shape[0] - plan.group
    return call(functools.partial(wire_kernel, rows), shape(part.shape, BF), 0, 1, name="wire")(part)


def grad_shapes(plan):
    return shape((27, plan.group, plan.chan), F32), shape((1, plan.group), F32)


def as_grads(weight, bias, plan):
    weight = jnp.transpose(weight.reshape(3, 3, 3, plan.group, plan.chan), (3, 4, 0, 1, 2))
    return weight, bias.reshape(plan.group)


def total_step(part, got, step, plan, share=None):
    rows = part.shape[0] - plan.group
    kernel, args, more = step_kernel, (part, got), 0
    if share is not None:
        kernel, args, more = join_kernel, (part, got, share), share.shape[0]
    part, wire = call(
        functools.partial(kernel, rows),
        (shape(part.shape, F32), shape((part.shape[0] + more, part.shape[1]), BF)),
        0,
        len(args),
        name="step",
    )(*args)
    return part, exchange(wire, step)


def total_last(part, got, plan, scale):
    rows = part.shape[0] - plan.group
    weight, bias = call(
        functools.partial(last_kernel, rows, plan.group, scale), grad_shapes(plan), 0, 2, name="last"
    )(part, got)
    return as_grads(weight, bias, plan)


def local(volume, weight1, bias1, weight2, bias2, upstream):
    _, group, layers, ny, nz = volume.shape
    chan = weight1.shape[1]
    spaces, groups = lax.axis_size("space"), lax.axis_size("filt")
    plan = Plan(layers, ny, nz, chan, groups, spaces)
    scale = 1.0 / math.sqrt(lax.axis_size("rep") * spaces * layers * ny * nz)

    cells = ny * nz
    conv = 2 * 27 * chan * chan * cells
    slots = VM((16 // ny, ny, chan, 2 * chan), BF)
    dma = pltpu.SemaphoreType.DMA
    padded = plan.padded()
    grad_rows = 27 * group // 2 + group
    grad_scratch = [VM((layers, ny + 2, 3 * group, nz), BF), VM((9 * group, 3 * chan), F32)]

    half = lambda n: (n, ny, chan // 2, nz)

    def early_layers(pieces, pieces2):
        early = call(
            functools.partial(early_kernel, plan, [p[1:] for p in pieces]),
            (shape((layers - 1, ny, chan, nz), BF), shape((layers - 1, ny, chan, nz), F32)),
            len(pieces),
            0,
            [VM(padded, BF), slots, dma((len(pieces),)), dma((groups,))],
            flops=1,
            name="early",
        )(*(p[0] for p in pieces))
        some = layers - 2
        ahead, ahead_output, ahead_sums, ahead_total = call(
            functools.partial(ahead_kernel, plan),
            (
                shape(half(some), BF),
                shape((group, some, ny, nz), BF),
                shape((9 * group, 3 * chan), F32),
                shape((group, nz), F32),
            ),
            3,
            0,
            [
                VM((layers, ny + 2, chan, nz), BF),
                VM((some, ny, chan, nz), BF),
                slots,
                VM(half(some), F32),
                VM((some, ny + 2, 3 * group, nz), BF),
                dma((3,)),
                dma((2,)),
            ],
            flops=1,
            name="ahead",
        )(early[0], *pieces2)
        return early, (ahead, ahead_output, ahead_sums, ahead_total)

    gather = gather_quick if plan.quick else gather_plain
    v_own, v_other, u_own, u_other, early, ahead = gather(
        volume[0], weight1, bias1, upstream[0], weight2, bias2, plan, early_layers
    )
    v_places = [p[1:] for p in v_own + v_other]
    u_places = [p[1:] for p in u_own + u_other]
    v_all = [p[0] for p in v_own + v_other]
    u_all = [p[0] for p in u_own + u_other]

    turned1 = call(
        functools.partial(turn_kernel, plan),
        shape((3, chan, 9 * chan), BF),
        groups,
        0,
        [slots, dma((groups,))],
        moved=2 << 20,
        name="turn",
    )(*v_all[:groups])

    hidden, slope = call(
        functools.partial(first_kernel, plan, v_places),
        (shape(padded, BF), shape((plan.count(2), ny, chan, nz), F32)),
        len(v_all) + len(early),
        0,
        [VM(padded, BF), slots, dma((len(v_all),)), dma((groups,)), dma((2,))],
        flops=1,
        name="first",
    )(*v_all, *early)

    if plan.quick:
        u_all[3] = flip_perm(after(u_all[2], hidden), 1)
        here, there = (0, 1, 4, 5), (2, 3, 6, 7)
        near2, output, part2 = call(
            functools.partial(near_kernel, plan, [u_places[k] for k in here]),
            (
                shape(half(plan.count(1)), BF),
                shape((group, layers, ny, nz), BF),
                shape((grad_rows, 2 * chan), F32),
            ),
            5,
            4,
            [
                VM((plan.count(1), ny, chan, nz), BF),
                slots,
                VM(half(plan.count(1)), F32),
                *grad_scratch,
                dma((4,)),
                dma((2,)),
                dma,
            ],
            flops=1,
            name="near",
        )(*(u_all[k] for k in here), ahead[0], hidden, *ahead[1:])
        delta2, turned2 = call(
            functools.partial(far_kernel, plan, [u_places[k] for k in there]),
            (shape(padded, BF), shape((3, chan, 9 * chan), BF)),
            9,
            1,
            [VM((plan.count(1), ny, chan, nz), BF), slots, dma((4,)), dma((4,)), dma],
            flops=1,
            name="far",
        )(*(u_all[k] for k in there), *u_all[:4], near2, hidden)
    else:
        delta2, output, part2, turned2 = call(
            functools.partial(second_kernel, plan, u_places),
            (
                shape(padded, BF),
                shape((group, layers, ny, nz), BF),
                shape((grad_rows, 2 * chan), F32),
                shape((3, chan, 9 * chan), BF),
            ),
            len(u_all),
            1,
            [
                VM((plan.count(1), ny, chan, nz), BF),
                slots,
                VM((plan.count(1), ny, chan, nz), F32),
                *grad_scratch,
                dma((len(u_all),)),
                dma((groups,)),
            ],
            flops=1,
            name="second",
        )(*u_all, hidden)

    delta1, part1 = call(
        functools.partial(third_kernel, plan, v_places),
        (shape((layers, ny, chan, nz), BF), shape((grad_rows, 2 * chan), F32)),
        len(v_all),
        3,
        [VM(padded, BF), *grad_scratch, dma((len(v_all),))],
        flops=1,
        name="third",
    )(*v_all, slope, delta2, turned2)

    beside = [shape((ny * group, nz), BF)] * plan.sides
    own_grad, *shares = call(
        functools.partial(fourth_kernel, plan),
        (shape((layers, ny, group, nz), F32), *beside),
        1,
        1,
        [VM((layers + 4, ny + 2, chan, nz), BF), dma],
        flops=1,
        name="fourth",
    )(delta1, turned1)

    steps1 = rounds(plan)
    steps2 = steps1[1:] + steps1[:1]
    got1 = exchange(first_wire(part1, plan), steps1[0])
    got2 = exchange(first_wire(part2, plan), steps2[0])
    for step in steps1[1:]:
        part1, got1 = total_step(part1, got1, step, plan)
    for n, step in enumerate(steps2[1:], 2):
        share = shares[0] if plan.pair and n == len(steps2) else None
        part2, got2 = total_step(part2, got2, step, plan, share)
    volume_shape = shape((group, layers, ny, nz), BF)
    finish_scratch = [VM((layers, ny, group, nz), F32), dma]
    if plan.pair:
        w1, b1, w2, b2, volume_grad, output = call(
            functools.partial(close_kernel, plan, part2.shape[0] - group, scale),
            (*grad_shapes(plan), *grad_shapes(plan), volume_shape, volume_shape),
            1,
            5,
            finish_scratch,
            name="close",
        )(own_grad, part1, got1, part2, got2, output)
        grad1, bias_grad1 = as_grads(w1, b1, plan)
        grad2, bias_grad2 = as_grads(w2, b2, plan)
    else:
        grad1, bias_grad1 = total_last(part1, got1, plan, scale)
        grad2, bias_grad2 = total_last(part2, got2, plan, scale)
        volume_grad = call(
            functools.partial(finish_kernel, plan), volume_shape, 1, 2, finish_scratch, name="finish"
        )(own_grad, up(shares[1]), down(shares[0]))
    return (output[None], volume_grad[None], grad1, bias_grad1, grad2, bias_grad2)


def solution(mesh):
    field = P("rep", "filt", "space", None, None)
    kernel = P("filt", None, None, None, None)
    return jax.shard_map(
        local,
        mesh=mesh,
        in_specs=(field, kernel, P("filt"), kernel, P("filt"), field),
        out_specs=(field, field, kernel, P("filt"), kernel, P("filt")),
        check_vma=False,
    )
```

```python
import functools
import math

import jax
import jax.numpy as jnp
from jax import lax
from jax.experimental import pallas as pl
from jax.experimental.pallas import tpu as pltpu
from jax.sharding import PartitionSpec as P

SLOPE = 0.3
NEAR = 3
BF = jnp.bfloat16
F32 = jnp.float32
VM = pltpu.VMEM
ANY = pl.BlockSpec(memory_space=pl.ANY)
WHOLE = pl.BlockSpec(memory_space=pltpu.VMEM)


def call(kernel, outs, n_any, n_vmem, scratch=(), flops=0, moved=0, name=None):
    return pl.pallas_call(
        kernel,
        out_shape=outs,
        in_specs=[ANY] * n_any + [WHOLE] * n_vmem,
        out_specs=jax.tree.map(lambda _: WHOLE, outs),
        scratch_shapes=list(scratch),
        compiler_params=pltpu.CompilerParams(vmem_limit_bytes=40 << 20),
        cost_estimate=pl.CostEstimate(flops=flops, bytes_accessed=moved, transcendentals=0),
        name=name,
    )


def shape(dims, kind):
    return jax.ShapeDtypeStruct(tuple(dims), kind)


def parts(values):
    e = jnp.exp(-jnp.abs(values))
    one = 1.0 + e
    soft = jnp.maximum(values, 0.0) + jnp.log(one)
    sig = jnp.where(values >= 0.0, 1.0, e) / one
    return SLOPE * values + (1.0 - SLOPE) * soft, SLOPE + (1.0 - SLOPE) * sig


def slope_of(values):
    e = jnp.exp(-jnp.abs(values))
    return SLOPE + (1.0 - SLOPE) * (jnp.where(values >= 0.0, 1.0, e) / (1.0 + e))


def smooth(values):
    e = jnp.exp(-jnp.abs(values))
    soft = jnp.maximum(values, 0.0) + jnp.log(1.0 + e)
    return SLOPE * values + (1.0 - SLOPE) * soft


def swap(block):
    return jnp.transpose(block.astype(F32), (1, 0, 2))


def pack_weight(w_ref, b_ref, o_ref, base):
    group, chan, ny = w_ref.shape[1], w_ref.shape[2], o_ref.shape[1]
    for pair in range(5):
        for kz in range(3):
            low = w_ref[6 * pair + kz]
            if pair < 4:
                high = w_ref[6 * pair + 3 + kz]
            else:
                high = jnp.zeros_like(low)
            slot = 3 * pair + kz
            o_ref[base + slot // ny, slot % ny] = jnp.concatenate([low, high], axis=1)
    eye = lax.broadcasted_iota(jnp.int32, (group, group), 0) == lax.broadcasted_iota(
        jnp.int32, (group, group), 1
    )
    col = jnp.sum(jnp.where(eye, jnp.broadcast_to(b_ref[...], (group, group)), 0.0), axis=1, keepdims=True)
    col = jnp.broadcast_to(col, (group, 2 * chan))
    first = col.astype(BF)
    rest = col - first.astype(F32)
    second = rest.astype(BF)
    third = (rest - second.astype(F32)).astype(BF)
    lane = lax.broadcasted_iota(jnp.int32, (group, 2 * chan), 1)
    picked = jnp.where(lane == 0, first.astype(F32), jnp.where(lane == 1, second.astype(F32), third.astype(F32)))
    o_ref[base + 15 // ny, 15 % ny] = picked.astype(BF)


def pack_kernel(edge, *refs):
    if edge:
        f_hbm, w_hbm, b_hbm, n_hbm, o_ref, e_ref, f_ref, w_ref, b_ref, n_ref, sem = refs
    else:
        f_hbm, w_hbm, b_hbm, o_ref, f_ref, w_ref, b_ref, sem = refs
    layers = f_ref.shape[1]
    pairs = [(f_hbm, f_ref), (w_hbm, w_ref), (b_hbm, b_ref)]
    if edge:
        facing = 1 - lax.axis_index("space")
        pairs.append((n_hbm.at[:, pl.ds(facing * (layers - 1), 1)], n_ref))
    copies = [pltpu.make_async_copy(src, dst, sem.at[n]) for n, (src, dst) in enumerate(pairs)]
    for copy in copies:
        copy.start()
    copies[0].wait()
    for x in range(layers):
        o_ref[x] = swap(f_ref[:, x]).astype(BF)
    if edge:
        copies[3].wait()
        for x in range(edge):
            e_ref[x] = o_ref[facing * (layers - edge) + x]
        e_ref[edge] = swap(n_ref[:, 0]).astype(BF)
    copies[1].wait()
    copies[2].wait()
    pack_weight(w_ref, b_ref, o_ref, layers)


def pack(field, weight, bias, name, beside=None, edge=0):
    group, layers, ny, nz = field.shape
    chan = weight.shape[1]
    taps = jnp.transpose(weight, (2, 3, 4, 0, 1)).reshape(27, group, chan)
    args = [field, taps, bias.reshape(1, group)]
    outs = [shape((layers + 16 // ny, ny, group, nz), BF)]
    scratch = [VM(field.shape, BF), VM((27, group, chan), BF), VM((1, group), F32)]
    if edge:
        args.append(beside)
        outs.append(shape((edge + 1, ny, group, nz), BF))
        scratch.append(VM((group, 1, ny, nz), BF))
    return pl.pallas_call(
        functools.partial(pack_kernel, edge),
        out_shape=tuple(outs),
        in_specs=[pl.BlockSpec(memory_space=pltpu.HBM)] * len(args),
        out_specs=(WHOLE,) * len(outs),
        scratch_shapes=scratch + [pltpu.SemaphoreType.DMA((len(args),))],
        compiler_params=pltpu.CompilerParams(vmem_limit_bytes=40 << 20),
        cost_estimate=pl.CostEstimate(flops=0, bytes_accessed=field.size * 4, transcendentals=0),
        name=name,
    )(*(pltpu.with_memory_space_constraint(v, pltpu.HBM) for v in args))


class Plan:
    def __init__(self, layers, ny, nz, chan, groups, spaces):
        self.layers, self.ny, self.nz, self.chan = layers, ny, nz, chan
        self.groups, self.spaces = groups, spaces
        self.group = chan // groups
        self.pair = spaces == 2
        self.quick = self.pair and groups == 4
        self.window = (2 if self.pair else 3) * layers
        self.sides = 1 if self.pair else 2

    def start(self, reach):
        if self.pair:
            return lax.axis_index("space") * (self.layers - reach)
        return self.layers - reach

    def count(self, reach):
        return self.layers + self.sides * reach

    def own(self):
        return self.start(0)

    def inside(self, layer):
        if self.pair:
            return None
        at = (lax.axis_index("space") - 1) * self.layers + layer
        return jnp.logical_and(at >= 0, at < self.spaces * self.layers)

    def chan_at(self, flip):
        return pl.multiple_of((lax.axis_index("filt") ^ flip) * self.group, self.group)

    def padded(self):
        return (self.window + 2, self.ny + 2, self.chan, self.nz)


def flip_perm(value, flip):
    n = lax.axis_size("filt")
    return lax.ppermute(value, "filt", [(i, i ^ flip) for i in range(n)])


def over(value):
    return lax.ppermute(value, "space", [(0, 1), (1, 0)])


def up(value):
    n = lax.axis_size("space")
    return lax.ppermute(value, "space", [(i, i + 1) for i in range(n - 1)])


def down(value):
    n = lax.axis_size("space")
    return lax.ppermute(value, "space", [(i + 1, i) for i in range(n - 1)])


def after(value, *others):
    return lax.optimization_barrier((value, *others))[0]


def gather_quick(volume, weight1, bias1, upstream, weight2, bias2, plan, early_layers):
    n = plan.layers
    packed, edge = pack(volume, weight1, bias1, "pack1", upstream, NEAR)
    x = flip_perm(packed, 2)
    y = over(edge)
    c = flip_perm(packed, 1)
    (second,) = pack(upstream, weight2, bias2, "pack2")
    y, x = lax.optimization_barrier((y, x, second))[:2]
    d = flip_perm(y, 2)
    xc = flip_perm(x, 1)
    yc = flip_perm(y, 1)
    x2 = flip_perm(second, 2)
    c2 = flip_perm(second, 1)
    early, ahead = early_layers([(v, 0, n, "own", 0, k) for k, v in enumerate([packed, c, x, xc])], (second, c2))
    dc = flip_perm(after(d, ahead[0]), 1)
    own, other, own2 = [packed, c, x, xc], [y, yc, d, dc], [second, c2, x2, x2]
    return (
        [(v, 0, n, "own", 0, k) for k, v in enumerate(own)],
        [(v, 0, NEAR, "other", 0, k) for k, v in enumerate(other)],
        [(v, 0, n, "own", 0, k) for k, v in enumerate(own2)],
        [(v, NEAR, 1, "halo", 0, k) for k, v in enumerate(other)],
        early,
        ahead,
    )


def gather_plain(volume, weight1, bias1, upstream, weight2, bias2, plan, early_layers):
    n = plan.layers
    (packed,) = pack(volume, weight1, bias1, "pack1")
    (second,) = pack(upstream, weight2, bias2, "pack2")
    own, other, own2, halo = [], [], [], []
    for flip in range(plan.groups):
        mine = flip_perm(packed, flip) if flip else packed
        mine2 = flip_perm(second, flip) if flip else second
        own.append((mine, 0, n, "own", 0, flip))
        own2.append((mine2, 0, n, "own", 0, flip))
        if plan.pair:
            facing = 1 - lax.axis_index("space")
            near = lax.dynamic_slice_in_dim(mine, facing * (n - NEAR), NEAR, axis=0)
            other.append((over(near), 0, NEAR, "other", 0, flip))
            near = lax.dynamic_slice_in_dim(mine2, facing * (n - 1), 1, axis=0)
            halo.append((over(near), 0, 1, "halo", 0, flip))
        else:
            other.append((up(mine[n - NEAR : n]), 0, NEAR, "low", 0, flip))
            other.append((down(mine[:NEAR]), 0, NEAR, "high", 0, flip))
            halo.append((up(mine2[n - 1 : n]), 0, 1, "low", 0, flip))
            halo.append((down(mine2[:1]), 0, 1, "high", 0, flip))
    return own, other, own2, halo, (), ()


def field_place(plan, place, k):
    n = plan.layers
    if plan.pair:
        s = lax.axis_index("space")
        return 1 + k + (s * n if place == "own" else n - NEAR * s)
    return 1 + k + {"low": n - NEAR, "own": n, "high": 2 * n}[place]


def halo_place(plan, place):
    if plan.pair:
        s = lax.axis_index("space")
        return s if place == "own" else (1 - s) * plan.layers
    return {"low": 0, "own": 1, "high": plan.layers + 1}[place]


def load_weight(plan, refs, dst, sem, start, flips=None):
    for n, ref in enumerate(refs):
        flip = flips[n] if flips else n
        copy = pltpu.make_async_copy(
            ref.at[pl.ds(ref.shape[0] - dst.shape[0], dst.shape[0])],
            dst.at[:, :, pl.ds(plan.chan_at(flip), plan.group), :],
            sem.at[n],
        )
        copy.start() if start else copy.wait()


def load_pieces(plan, refs, places, dst, sem, start, halo=False, near=False):
    for n, (ref, (first, count, place, k, flip)) in enumerate(zip(refs, places)):
        if near and place == "own":
            first = k = (1 - lax.axis_index("space")) * (plan.layers - 2)
            count = 2
        rows = pl.ds(plan.chan_at(flip), plan.group)
        if halo:
            target = dst.at[pl.ds(halo_place(plan, place), count), :, rows, :]
        else:
            target = dst.at[pl.ds(field_place(plan, place, k), count), pl.ds(1, plan.ny), rows, :]
        copy = pltpu.make_async_copy(ref.at[pl.ds(first, count)], target, sem.at[n])
        copy.start() if start else copy.wait()


def zero_rows(ref):
    zero = jnp.zeros(ref.shape[2:], ref.dtype)
    for x in range(ref.shape[0]):
        ref[x, 0] = zero
        ref[x, ref.shape[1] - 1] = zero


def zero_layer(ref, x):
    zero = jnp.zeros(ref.shape[2:], ref.dtype)
    for y in range(1, ref.shape[1] - 1):
        ref[x, y] = zero


def zero_edges(plan, ref):
    zero_rows(ref)
    zero_layer(ref, 0)
    zero_layer(ref, ref.shape[0] - 1)


def slot(w_ref, n, rows=slice(None)):
    return w_ref[n // w_ref.shape[1], n % w_ref.shape[1], rows, :]


def weight_matrix(w_ref, chan, rows=slice(None)):
    cols = []
    for pair in range(5):
        block = jnp.concatenate([slot(w_ref, 3 * pair + kz, rows) for kz in range(3)], axis=0)
        cols.append(block if pair < 4 else block[:, :chan])
    return jnp.concatenate(cols, axis=1)


def bias_column(w_ref, rows=slice(None)):
    terms = slot(w_ref, 15, rows).astype(F32)
    return terms[:, 0:1] + terms[:, 1:2] + terms[:, 2:3]


def taps(field_ref, x, y):
    c, nz = field_ref.shape[2], field_ref.shape[3]
    rows = []
    for kx in range(3):
        first = field_ref[x + kx, y : y + 3].reshape(3 * c, nz)
        second = field_ref[x + kx, y + 1 : y + 4].reshape(3 * c, nz)
        rows.append(jnp.concatenate([first, second], axis=1))
    return jnp.concatenate(rows, axis=0)


def z_shift(values, by):
    nz = values.shape[1]
    lane = lax.broadcasted_iota(jnp.int32, values.shape, 1)
    if by > 0:
        return jnp.where(lane == 0, 0.0, pltpu.roll(values, 1, 1))
    return jnp.where(lane == nz - 1, 0.0, pltpu.roll(values, nz - 1, 1))


def z_sum(product, rows, half, nz):
    part = product[:, half * nz : (half + 1) * nz]
    return part[rows : 2 * rows] + z_shift(part[:rows], 1) + z_shift(part[2 * rows :], -1)


def conv_rows(weight, field_ref, x, each):
    ny, nz = field_ref.shape[1] - 2, field_ref.shape[3]
    rows = weight.shape[0] // 3
    for y in range(0, ny, 2):
        product = jnp.dot(weight, taps(field_ref, x, y), preferred_element_type=F32)
        for half in range(2):
            each(y + half, z_sum(product, rows, half, nz))


def first_rows(plan, weight, bias, a_ref, start, count, put):
    def body(t, carry):
        x = start + t
        inside = plan.inside(x)

        def each(y, value):
            act, slope = parts(value + bias)
            if inside is not None:
                act = jnp.where(inside, act, 0.0)
            put(t, x, y, act.astype(BF), slope)

        conv_rows(weight, a_ref, x, each)
        return carry

    lax.fori_loop(0, count, body, 0, unroll=True)


def early_kernel(plan, places, *refs):
    n = len(places)
    pieces = refs[:n]
    h_ref, s_ref, a_ref, w_ref, sem, wsem = refs[n:]
    load_weight(plan, pieces[: plan.groups], w_ref, wsem, True)
    load_pieces(plan, pieces, places, a_ref, sem, True)
    zero_edges(plan, a_ref)
    load_weight(plan, pieces[: plan.groups], w_ref, wsem, False)
    load_pieces(plan, pieces, places, a_ref, sem, False)

    def put(t, x, y, act, slope):
        h_ref[t, y] = act
        s_ref[t, y] = slope

    start = lax.axis_index("space") * (plan.layers + 1)
    first_rows(plan, weight_matrix(w_ref, plan.chan), bias_column(w_ref), a_ref, start, plan.layers - 1, put)


def first_kernel(plan, places, *refs):
    n = len(places)
    pieces, refs = refs[:n], refs[n:]
    if plan.quick:
        eh_ref, es_ref, refs = refs[0], refs[1], refs[2:]
    h_ref, s_ref, a_ref, w_ref, sem, wsem, esem = refs
    load_weight(plan, pieces[: plan.groups], w_ref, wsem, True)
    load_pieces(plan, pieces, places, a_ref, sem, True, near=plan.quick)
    zero_edges(plan, a_ref)
    zero_edges(plan, h_ref)
    base = plan.start(2)
    start, count = base, plan.count(2)
    copies = []
    if plan.quick:
        s = lax.axis_index("space")
        done = s * (plan.layers + 1)
        start, count = plan.layers - 1 - s, count - plan.layers + 1
        copies = [
            pltpu.make_async_copy(
                eh_ref, h_ref.at[pl.ds(done + 1, plan.layers - 1), pl.ds(1, plan.ny)], esem.at[0]
            ),
            pltpu.make_async_copy(es_ref, s_ref.at[pl.ds(done - base, plan.layers - 1)], esem.at[1]),
        ]
    for copy in copies:
        copy.start()
    load_weight(plan, pieces[: plan.groups], w_ref, wsem, False)
    load_pieces(plan, pieces, places, a_ref, sem, False, near=plan.quick)

    def put(t, x, y, act, slope):
        h_ref[x + 1, y + 1] = act
        s_ref[x - base, y] = slope

    first_rows(plan, weight_matrix(w_ref, plan.chan), bias_column(w_ref), a_ref, start, count, put)
    for copy in copies:
        copy.wait()


def grad_sums(plan, count, get, f_ref, base, sh_ref):
    group, nz, ny, chan = plan.group, plan.nz, plan.ny, plan.chan
    zero = jnp.zeros((3 * group, nz), BF)
    total = jnp.zeros((group, nz), F32)
    sums = jnp.zeros((9 * group, 3 * chan), F32)
    for t in range(count):
        sh_ref[t, 0] = zero
        sh_ref[t, ny + 1] = zero
        for y in range(ny):
            value = get(t, y).astype(F32)
            total = total + value
            sh_ref[t, y + 1] = jnp.concatenate([z_shift(value, -1), value, z_shift(value, 1)], axis=0).astype(BF)
    for t in range(count):
        left = jnp.concatenate(
            [jnp.concatenate([sh_ref[t, y + 2 - ky] for y in range(ny)], axis=1) for ky in range(3)], axis=0
        )
        right = jnp.concatenate(
            [jnp.concatenate([f_ref[base + t + kx, y + 1] for y in range(ny)], axis=1) for kx in range(3)], axis=0
        )
        sums += lax.dot_general(left, right, (((1,), (1,)), ((), ())), preferred_element_type=F32)
    return sums, total


def pack_grads(plan, sums, total, acc_ref, g_ref):
    group, chan = plan.group, plan.chan
    acc_ref[...] = sums
    n = 9 * group
    g_ref[0:n] = acc_ref[:, 0 : 2 * chan]
    last = acc_ref[:, 2 * chan :]
    g_ref[n : n + n // 2] = jnp.concatenate([last[: n // 2], last[n // 2 :]], axis=1)
    g_ref[n + n // 2 :] = jnp.broadcast_to(jnp.sum(total, axis=1, keepdims=True), (group, 2 * chan))


def grads(plan, get, f_ref, sh_ref, acc_ref, g_ref):
    rows = pl.ds(plan.chan_at(0), plan.group)
    sums, total = grad_sums(plan, plan.layers, lambda t, y: get(t, y, rows), f_ref, plan.own(), sh_ref)
    pack_grads(plan, sums, total, acc_ref, g_ref)


def second_rows(plan, rows, h_ref, u_ref, w_ref, put, first, count, layer):
    matrix = weight_matrix(w_ref, plan.chan, rows)
    bias = bias_column(w_ref, rows)
    for n in range(count):

        def each(y, value, t=first + n, x=layer + n):
            pre = value + bias
            delta = (u_ref[t, y, rows, :].astype(F32) * slope_of(pre)).astype(BF)
            put(t, x, y, pre, delta)

        conv_rows(matrix, h_ref, layer + n, each)


def put_output(plan, p_ref, rows, o_ref):
    first = plan.own() - plan.start(1)
    for t in range(plan.layers):
        o_ref[:, t] = jnp.transpose(smooth(p_ref[first + t, :, rows, :]), (1, 0, 2)).astype(BF)


def second_kernel(plan, places, *refs):
    n = len(places)
    pieces = refs[:n]
    weights = pieces[: plan.groups]
    h_ref, d_ref, o_ref, g_ref, t_ref, u_ref, w_ref, p_ref, sh_ref, acc_ref, sem, wsem = refs[n:]
    load_weight(plan, weights, w_ref, wsem, True)
    load_pieces(plan, pieces, places, u_ref, sem, True, halo=True)
    zero_edges(plan, d_ref)
    load_weight(plan, weights, w_ref, wsem, False)
    turn(w_ref, t_ref, plan.chan)
    load_pieces(plan, pieces, places, u_ref, sem, False, halo=True)

    def put(t, x, y, pre, delta):
        p_ref[t, y] = pre
        d_ref[x + 1, y + 1] = delta

    second_rows(plan, pl.ds(0, plan.chan), h_ref, u_ref, w_ref, put, 0, plan.count(1), plan.start(1))
    put_output(plan, p_ref, pl.ds(plan.chan_at(0), plan.group), o_ref)
    own = plan.own()
    grads(plan, lambda t, y, rows: d_ref[own + t + 1, y + 1, rows, :], h_ref, sh_ref, acc_ref, g_ref)


def chip_rows(plan, other):
    half = plan.chan // 2
    return pl.ds(pl.multiple_of(((lax.axis_index("filt") >> 1) ^ other) * half, half), half)


def own_rows(plan):
    return pl.ds(pl.multiple_of((lax.axis_index("filt") & 1) * plan.group, plan.group), plan.group)


def ahead_kernel(plan, eh_hbm, own_hbm, chip_hbm, d_ref, o_ref, a_ref, b_ref, h_ref, u_ref, w_ref, p_ref, sh_ref, sem, wsem):
    s = lax.axis_index("space")
    count = plan.layers - 2
    load_weight(plan, (own_hbm, chip_hbm), w_ref, wsem, True, (0, 1))
    copies = [
        pltpu.make_async_copy(eh_hbm, h_ref.at[pl.ds(1 - s, count + 1), pl.ds(1, plan.ny)], sem.at[2])
    ]
    for flip, ref in enumerate((own_hbm, chip_hbm)):
        target = u_ref.at[:, :, pl.ds(plan.chan_at(flip), plan.group), :]
        copies.append(pltpu.make_async_copy(ref.at[pl.ds(2 * s, count)], target, sem.at[flip]))
    for copy in copies:
        copy.start()
    zero_rows(h_ref)
    zero_layer(h_ref, s * (count + 1))
    load_weight(plan, (own_hbm, chip_hbm), w_ref, wsem, False, (0, 1))
    for copy in copies:
        copy.wait()

    def put(t, x, y, pre, delta):
        p_ref[t, y] = pre
        d_ref[t, y] = delta

    second_rows(plan, chip_rows(plan, 0), h_ref, u_ref, w_ref, put, 0, count, 0)
    mine = own_rows(plan)
    for t in range(count):
        o_ref[:, t] = jnp.transpose(smooth(p_ref[t, :, mine, :]), (1, 0, 2)).astype(BF)
    a_ref[...], b_ref[...] = grad_sums(plan, count, lambda t, y: d_ref[t, y, mine, :], h_ref, 0, sh_ref)


def near_kernel(plan, places, *refs):
    n = len(places)
    pieces, ahead, refs = refs[:n], refs[n], refs[n + 1 :]
    h_ref, ao_ref, aa_ref, ab_ref, d_ref, o_ref, g_ref, u_ref, w_ref, p_ref, sh_ref, acc_ref, sem, wsem, asem = refs
    s = lax.axis_index("space")
    done = plan.layers - 2
    left = plan.count(1) - done
    load_weight(plan, pieces[:2], w_ref, wsem, True, (0, 1))
    load_pieces(plan, pieces, places, u_ref, sem, True, halo=True)
    copy = pltpu.make_async_copy(ahead, d_ref.at[pl.ds(s * left, done)], asem)
    copy.start()
    load_weight(plan, pieces[:2], w_ref, wsem, False, (0, 1))
    load_pieces(plan, pieces, places, u_ref, sem, False, halo=True)

    def put(t, x, y, pre, delta):
        p_ref[t, y] = pre
        d_ref[t, y] = delta

    start, first, slab = plan.start(1), (1 - s) * done, (1 - s) * done
    second_rows(plan, chip_rows(plan, 0), h_ref, u_ref, w_ref, put, first, left, start + first)
    mine = own_rows(plan)
    o_ref[:, pl.ds(2 * s, done)] = ao_ref[...]
    at = plan.own() - start + slab
    for t in range(2):
        value = jnp.transpose(smooth(p_ref[at + t, :, mine, :]), (1, 0, 2)).astype(BF)
        o_ref[:, pl.ds(slab + t, 1)] = value[:, None]
    sums, total = grad_sums(plan, 2, lambda t, y: d_ref[at + t, y, mine, :], h_ref, plan.own() + slab, sh_ref)
    pack_grads(plan, sums + aa_ref[...], total + ab_ref[...], acc_ref, g_ref)
    copy.wait()


def far_kernel(plan, places, *refs):
    n = len(places)
    pieces, weights, refs = refs[:n], refs[n : n + 4], refs[n + 4 :]
    near_ref, h_ref, d_ref, t_ref, u_ref, w_ref, sem, wsem, nsem = refs
    load_weight(plan, weights, w_ref, wsem, True)
    load_pieces(plan, pieces, places, u_ref, sem, True, halo=True)
    joined = d_ref.at[pl.ds(plan.start(1) + 1, plan.count(1)), pl.ds(1, plan.ny), chip_rows(plan, 0), :]
    copy = pltpu.make_async_copy(near_ref, joined, nsem)
    copy.start()
    zero_edges(plan, d_ref)
    load_weight(plan, weights, w_ref, wsem, False)
    turn(w_ref, t_ref, plan.chan)
    load_pieces(plan, pieces, places, u_ref, sem, False, halo=True)
    rows = chip_rows(plan, 1)

    def put(t, x, y, pre, delta):
        d_ref[x + 1, y + 1, rows, :] = delta

    second_rows(plan, rows, h_ref, u_ref, w_ref, put, 0, plan.count(1), plan.start(1))
    copy.wait()


def turn(w_ref, out, chan):
    for kz in range(3):
        turned = [jnp.transpose(slot(w_ref, 3 * pair + 2 - kz).astype(F32), (1, 0)) for pair in range(5)]
        for pair in range(5):
            low = turned[4 - pair][:chan]
            if pair < 4:
                block = jnp.concatenate([low, turned[3 - pair][chan:]], axis=1)
                out[kz, :, 2 * chan * pair : 2 * chan * (pair + 1)] = block.astype(BF)
            else:
                out[kz, :, 2 * chan * pair :] = low.astype(BF)


def turn_kernel(plan, *refs):
    out, w_ref, sem = refs[plan.groups :]
    for go in (True, False):
        load_weight(plan, refs[: plan.groups], w_ref, sem, go)
    turn(w_ref, out, plan.chan)


def third_kernel(plan, places, *refs):
    n = len(places)
    pieces = refs[:n]
    s_ref, d2_ref, t_ref, d_ref, g_ref, a_ref, sh_ref, acc_ref, sem = refs[n:]
    load_pieces(plan, pieces, places, a_ref, sem, True)
    zero_edges(plan, a_ref)
    start = plan.own()
    skip = start - plan.start(2)
    m_ref = t_ref[...].reshape(3 * plan.chan, 9 * plan.chan)

    def body(t, carry):
        def each(y, value):
            d_ref[t, y] = (value * s_ref[skip + t, y]).astype(BF)

        conv_rows(m_ref, d2_ref, start + t, each)
        return carry

    lax.fori_loop(0, plan.layers, body, 0, unroll=True)
    load_pieces(plan, pieces, places, a_ref, sem, False)
    grads(plan, lambda t, y, rows: d_ref[t, y, rows, :], a_ref, sh_ref, acc_ref, g_ref)


def fourth_kernel(plan, d_ref, t_ref, r_ref, *refs):
    *outs, a_ref, sem = refs
    layers, ny = plan.layers, plan.ny
    copy = pltpu.make_async_copy(d_ref, a_ref.at[pl.ds(2, layers), pl.ds(1, ny)], sem)
    copy.start()
    zero_rows(a_ref)
    for x in (0, 1, layers + 2, layers + 3):
        zero_layer(a_ref, x)
    copy.wait()
    rows = pl.ds(plan.chan_at(0), plan.group)
    m_ref = t_ref[:, rows, :].reshape(3 * plan.group, 9 * plan.chan)
    for t in range(layers):

        def each(y, value, t=t):
            r_ref[t, y] = value

        conv_rows(m_ref, a_ref, t + 1, each)
    if plan.pair:
        places = [(1 - lax.axis_index("space")) * (layers + 1)]
    else:
        places = [0, layers + 1]
    for out, place in zip(outs, places):

        def beside(y, value, out=out):
            out[y * plan.group : (y + 1) * plan.group] = value.astype(BF)

        conv_rows(m_ref, a_ref, place, beside)


def finish_volume(plan, r_ref, shares, o_ref):
    layers, ny, group = plan.layers, plan.ny, plan.group
    for layer, ref, base in shares:
        for y in range(ny):
            r_ref[layer, y] += ref[base + y * group : base + (y + 1) * group].astype(F32)
    for t in range(layers):
        o_ref[:, t] = jnp.transpose(r_ref[t], (1, 0, 2)).astype(BF)


def finish_kernel(plan, r_hbm, low_ref, high_ref, o_ref, r_ref, sem):
    copy = pltpu.make_async_copy(r_hbm, r_ref, sem)
    copy.start()
    copy.wait()
    finish_volume(plan, r_ref, [(0, low_ref, 0), (plan.layers - 1, high_ref, 0)], o_ref)


def to_wire(values, rows):
    row = lax.broadcasted_iota(jnp.int32, values.shape, 0)
    lane = lax.broadcasted_iota(jnp.int32, values.shape, 1)
    high = values.astype(BF).astype(F32)
    second = jnp.logical_and(row >= rows, lane >= values.shape[1] // 2)
    return jnp.where(second, values - high, high).astype(BF)


def add_wire(values, wire, rows):
    got = wire.astype(F32)
    row = lax.broadcasted_iota(jnp.int32, values.shape, 0)
    return values + got + jnp.where(row >= rows, pltpu.roll(got, values.shape[1] // 2, 1), 0.0)


def wire_kernel(rows, a_ref, w_ref):
    w_ref[...] = to_wire(a_ref[...], rows)


def step_kernel(rows, a_ref, got_ref, o_ref, w_ref):
    total = add_wire(a_ref[...], got_ref[...], rows)
    o_ref[...] = total
    w_ref[...] = to_wire(total, rows)


def join_kernel(rows, a_ref, got_ref, share_ref, o_ref, w_ref):
    total = add_wire(a_ref[...], got_ref[...], rows)
    o_ref[...] = total
    w_ref[: total.shape[0]] = to_wire(total, rows)
    w_ref[total.shape[0] :] = share_ref[...]


def close_kernel(plan, rows, scale, r_hbm, a1_ref, got1_ref, a2_ref, got2_ref, out_ref, *refs):
    w1_ref, b1_ref, w2_ref, b2_ref, o_ref, out2_ref, r_ref, sem = refs
    copy = pltpu.make_async_copy(r_hbm, r_ref, sem)
    copy.start()
    out2_ref[...] = out_ref[...]
    last_kernel(rows, plan.group, scale, a1_ref, got1_ref, w1_ref, b1_ref)
    last_kernel(rows, plan.group, scale, a2_ref, got2_ref, w2_ref, b2_ref)
    copy.wait()
    layer = (1 - lax.axis_index("space")) * (plan.layers - 1)
    finish_volume(plan, r_ref, [(layer, got2_ref, a2_ref.shape[0])], o_ref)


def last_kernel(rows, group, scale, a_ref, got_ref, w_ref, b_ref):
    total = add_wire(a_ref[...], got_ref[: a_ref.shape[0]], rows) * scale
    n = 9 * group
    chan = total.shape[1] // 2
    w_ref[0:9] = total[:n, :chan].reshape(9, group, chan)
    w_ref[9:18] = total[:n, chan:].reshape(9, group, chan)
    tail = total[n : n + n // 2]
    w_ref[18:27] = jnp.concatenate([tail[:, :chan], tail[:, chan:]], axis=0).reshape(9, group, chan)
    col = total[rows:, :group]
    eye = lax.broadcasted_iota(jnp.int32, (group, group), 0) == lax.broadcasted_iota(
        jnp.int32, (group, group), 1
    )
    b_ref[...] = jnp.sum(jnp.where(eye, col, 0.0), axis=0, keepdims=True)


def rounds(plan):
    out = []
    for axis in ("space", "rep"):
        size, bit = lax.axis_size(axis), 1
        while bit < size:
            out.append((axis, bit))
            bit *= 2
    return out


def exchange(wire, step):
    axis, bit = step
    return lax.ppermute(wire, axis, [(i, i ^ bit) for i in range(lax.axis_size(axis))])


def first_wire(part, plan):
    rows = part.shape[0] - plan.group
    return call(functools.partial(wire_kernel, rows), shape(part.shape, BF), 0, 1, name="wire")(part)


def grad_shapes(plan):
    return shape((27, plan.group, plan.chan), F32), shape((1, plan.group), F32)


def as_grads(weight, bias, plan):
    weight = jnp.transpose(weight.reshape(3, 3, 3, plan.group, plan.chan), (3, 4, 0, 1, 2))
    return weight, bias.reshape(plan.group)


def total_step(part, got, step, plan, share=None):
    rows = part.shape[0] - plan.group
    kernel, args, more = step_kernel, (part, got), 0
    if share is not None:
        kernel, args, more = join_kernel, (part, got, share), share.shape[0]
    part, wire = call(
        functools.partial(kernel, rows),
        (shape(part.shape, F32), shape((part.shape[0] + more, part.shape[1]), BF)),
        0,
        len(args),
        name="step",
    )(*args)
    return part, exchange(wire, step)


def total_last(part, got, plan, scale):
    rows = part.shape[0] - plan.group
    weight, bias = call(
        functools.partial(last_kernel, rows, plan.group, scale), grad_shapes(plan), 0, 2, name="last"
    )(part, got)
    return as_grads(weight, bias, plan)


def local(volume, weight1, bias1, weight2, bias2, upstream):
    _, group, layers, ny, nz = volume.shape
    chan = weight1.shape[1]
    spaces, groups = lax.axis_size("space"), lax.axis_size("filt")
    plan = Plan(layers, ny, nz, chan, groups, spaces)
    scale = 1.0 / math.sqrt(lax.axis_size("rep") * spaces * layers * ny * nz)

    cells = ny * nz
    conv = 2 * 27 * chan * chan * cells
    slots = VM((16 // ny, ny, chan, 2 * chan), BF)
    dma = pltpu.SemaphoreType.DMA
    padded = plan.padded()
    grad_rows = 27 * group // 2 + group
    grad_scratch = [VM((layers, ny + 2, 3 * group, nz), BF), VM((9 * group, 3 * chan), F32)]

    half = lambda n: (n, ny, chan // 2, nz)

    def early_layers(pieces, pieces2):
        early = call(
            functools.partial(early_kernel, plan, [p[1:] for p in pieces]),
            (shape((layers - 1, ny, chan, nz), BF), shape((layers - 1, ny, chan, nz), F32)),
            len(pieces),
            0,
            [VM(padded, BF), slots, dma((len(pieces),)), dma((groups,))],
            flops=1,
            name="early",
        )(*(p[0] for p in pieces))
        some = layers - 2
        ahead, ahead_output, ahead_sums, ahead_total = call(
            functools.partial(ahead_kernel, plan),
            (
                shape(half(some), BF),
                shape((group, some, ny, nz), BF),
                shape((9 * group, 3 * chan), F32),
                shape((group, nz), F32),
            ),
            3,
            0,
            [
                VM((layers, ny + 2, chan, nz), BF),
                VM((some, ny, chan, nz), BF),
                slots,
                VM(half(some), F32),
                VM((some, ny + 2, 3 * group, nz), BF),
                dma((3,)),
                dma((2,)),
            ],
            flops=1,
            name="ahead",
        )(early[0], *pieces2)
        return early, (ahead, ahead_output, ahead_sums, ahead_total)

    gather = gather_quick if plan.quick else gather_plain
    v_own, v_other, u_own, u_other, early, ahead = gather(
        volume[0], weight1, bias1, upstream[0], weight2, bias2, plan, early_layers
    )
    v_places = [p[1:] for p in v_own + v_other]
    u_places = [p[1:] for p in u_own + u_other]
    v_all = [p[0] for p in v_own + v_other]
    u_all = [p[0] for p in u_own + u_other]

    turned1 = call(
        functools.partial(turn_kernel, plan),
        shape((3, chan, 9 * chan), BF),
        groups,
        0,
        [slots, dma((groups,))],
        moved=2 << 20,
        name="turn",
    )(*v_all[:groups])

    hidden, slope = call(
        functools.partial(first_kernel, plan, v_places),
        (shape(padded, BF), shape((plan.count(2), ny, chan, nz), F32)),
        len(v_all) + len(early),
        0,
        [VM(padded, BF), slots, dma((len(v_all),)), dma((groups,)), dma((2,))],
        flops=1,
        name="first",
    )(*v_all, *early)

    if plan.quick:
        u_all[3] = flip_perm(after(u_all[2], hidden), 1)
        here, there = (0, 1, 4, 5), (2, 3, 6, 7)
        near2, output, part2 = call(
            functools.partial(near_kernel, plan, [u_places[k] for k in here]),
            (
                shape(half(plan.count(1)), BF),
                shape((group, layers, ny, nz), BF),
                shape((grad_rows, 2 * chan), F32),
            ),
            5,
            4,
            [
                VM((plan.count(1), ny, chan, nz), BF),
                slots,
                VM(half(plan.count(1)), F32),
                *grad_scratch,
                dma((4,)),
                dma((2,)),
                dma,
            ],
            flops=1,
            name="near",
        )(*(u_all[k] for k in here), ahead[0], hidden, *ahead[1:])
        delta2, turned2 = call(
            functools.partial(far_kernel, plan, [u_places[k] for k in there]),
            (shape(padded, BF), shape((3, chan, 9 * chan), BF)),
            9,
            1,
            [VM((plan.count(1), ny, chan, nz), BF), slots, dma((4,)), dma((4,)), dma],
            flops=1,
            name="far",
        )(*(u_all[k] for k in there), *u_all[:4], near2, hidden)
    else:
        delta2, output, part2, turned2 = call(
            functools.partial(second_kernel, plan, u_places),
            (
                shape(padded, BF),
                shape((group, layers, ny, nz), BF),
                shape((grad_rows, 2 * chan), F32),
                shape((3, chan, 9 * chan), BF),
            ),
            len(u_all),
            1,
            [
                VM((plan.count(1), ny, chan, nz), BF),
                slots,
                VM((plan.count(1), ny, chan, nz), F32),
                *grad_scratch,
                dma((len(u_all),)),
                dma((groups,)),
            ],
            flops=1,
            name="second",
        )(*u_all, hidden)

    delta1, part1 = call(
        functools.partial(third_kernel, plan, v_places),
        (shape((layers, ny, chan, nz), BF), shape((grad_rows, 2 * chan), F32)),
        len(v_all),
        3,
        [VM(padded, BF), *grad_scratch, dma((len(v_all),))],
        flops=1,
        name="third",
    )(*v_all, slope, delta2, turned2)

    beside = [shape((ny * group, nz), BF)] * plan.sides
    own_grad, *shares = call(
        functools.partial(fourth_kernel, plan),
        (shape((layers, ny, group, nz), F32), *beside),
        1,
        1,
        [VM((layers + 4, ny + 2, chan, nz), BF), dma],
        flops=1,
        name="fourth",
    )(delta1, turned1)

    steps1 = rounds(plan)
    steps2 = steps1[1:] + steps1[:1]
    got1 = exchange(first_wire(part1, plan), steps1[0])
    got2 = exchange(first_wire(after(part2, delta2), plan), steps2[0])
    for step in steps1[1:]:
        part1, got1 = total_step(part1, got1, step, plan)
    for n, step in enumerate(steps2[1:], 2):
        share = shares[0] if plan.pair and n == len(steps2) else None
        part2, got2 = total_step(part2, got2, step, plan, share)
    volume_shape = shape((group, layers, ny, nz), BF)
    finish_scratch = [VM((layers, ny, group, nz), F32), dma]
    if plan.pair:
        w1, b1, w2, b2, volume_grad, output = call(
            functools.partial(close_kernel, plan, part2.shape[0] - group, scale),
            (*grad_shapes(plan), *grad_shapes(plan), volume_shape, volume_shape),
            1,
            5,
            finish_scratch,
            name="close",
        )(own_grad, part1, got1, part2, got2, output)
        grad1, bias_grad1 = as_grads(w1, b1, plan)
        grad2, bias_grad2 = as_grads(w2, b2, plan)
    else:
        grad1, bias_grad1 = total_last(part1, got1, plan, scale)
        grad2, bias_grad2 = total_last(part2, got2, plan, scale)
        volume_grad = call(
            functools.partial(finish_kernel, plan), volume_shape, 1, 2, finish_scratch, name="finish"
        )(own_grad, up(shares[1]), down(shares[0]))
    return (output[None], volume_grad[None], grad1, bias_grad1, grad2, bias_grad2)


def solution(mesh):
    field = P("rep", "filt", "space", None, None)
    kernel = P("filt", None, None, None, None)
    return jax.shard_map(
        local,
        mesh=mesh,
        in_specs=(field, kernel, P("filt"), kernel, P("filt"), field),
        out_specs=(field, field, kernel, P("filt"), kernel, P("filt")),
        check_vma=False,
    )
```

```python
import functools
import math

import jax
import jax.numpy as jnp
from jax import lax
from jax.experimental import pallas as pl
from jax.experimental.pallas import tpu as pltpu
from jax.sharding import PartitionSpec as P

SLOPE = 0.3
NEAR = 3
BF = jnp.bfloat16
F32 = jnp.float32
VM = pltpu.VMEM
ANY = pl.BlockSpec(memory_space=pl.ANY)
WHOLE = pl.BlockSpec(memory_space=pltpu.VMEM)


def call(kernel, outs, n_any, n_vmem, scratch=(), flops=0, moved=0, name=None):
    return pl.pallas_call(
        kernel,
        out_shape=outs,
        in_specs=[ANY] * n_any + [WHOLE] * n_vmem,
        out_specs=jax.tree.map(lambda _: WHOLE, outs),
        scratch_shapes=list(scratch),
        compiler_params=pltpu.CompilerParams(vmem_limit_bytes=40 << 20),
        cost_estimate=pl.CostEstimate(flops=flops, bytes_accessed=moved, transcendentals=0),
        name=name,
    )


def shape(dims, kind):
    return jax.ShapeDtypeStruct(tuple(dims), kind)


def parts(values):
    e = jnp.exp(-jnp.abs(values))
    one = 1.0 + e
    soft = jnp.maximum(values, 0.0) + jnp.log(one)
    sig = jnp.where(values >= 0.0, 1.0, e) / one
    return SLOPE * values + (1.0 - SLOPE) * soft, SLOPE + (1.0 - SLOPE) * sig


def slope_of(values):
    e = jnp.exp(-jnp.abs(values))
    return SLOPE + (1.0 - SLOPE) * (jnp.where(values >= 0.0, 1.0, e) / (1.0 + e))


def smooth(values):
    e = jnp.exp(-jnp.abs(values))
    soft = jnp.maximum(values, 0.0) + jnp.log(1.0 + e)
    return SLOPE * values + (1.0 - SLOPE) * soft


def swap(block):
    return jnp.transpose(block.astype(F32), (1, 0, 2))


def pack_weight(w_ref, b_ref, o_ref, base):
    group, chan, ny = w_ref.shape[1], w_ref.shape[2], o_ref.shape[1]
    for pair in range(5):
        for kz in range(3):
            low = w_ref[6 * pair + kz]
            if pair < 4:
                high = w_ref[6 * pair + 3 + kz]
            else:
                high = jnp.zeros_like(low)
            slot = 3 * pair + kz
            o_ref[base + slot // ny, slot % ny] = jnp.concatenate([low, high], axis=1)
    eye = lax.broadcasted_iota(jnp.int32, (group, group), 0) == lax.broadcasted_iota(
        jnp.int32, (group, group), 1
    )
    col = jnp.sum(jnp.where(eye, jnp.broadcast_to(b_ref[...], (group, group)), 0.0), axis=1, keepdims=True)
    col = jnp.broadcast_to(col, (group, 2 * chan))
    first = col.astype(BF)
    rest = col - first.astype(F32)
    second = rest.astype(BF)
    third = (rest - second.astype(F32)).astype(BF)
    lane = lax.broadcasted_iota(jnp.int32, (group, 2 * chan), 1)
    picked = jnp.where(lane == 0, first.astype(F32), jnp.where(lane == 1, second.astype(F32), third.astype(F32)))
    o_ref[base + 15 // ny, 15 % ny] = picked.astype(BF)


def pack_kernel(edge, *refs):
    if edge:
        f_hbm, w_hbm, b_hbm, n_hbm, o_ref, e_ref, f_ref, w_ref, b_ref, n_ref, sem = refs
    else:
        f_hbm, w_hbm, b_hbm, o_ref, f_ref, w_ref, b_ref, sem = refs
    layers = f_ref.shape[1]
    pairs = [(f_hbm, f_ref), (w_hbm, w_ref), (b_hbm, b_ref)]
    if edge:
        facing = 1 - lax.axis_index("space")
        pairs.append((n_hbm.at[:, pl.ds(facing * (layers - 1), 1)], n_ref))
    copies = [pltpu.make_async_copy(src, dst, sem.at[n]) for n, (src, dst) in enumerate(pairs)]
    for copy in copies:
        copy.start()
    copies[0].wait()
    for x in range(layers):
        o_ref[x] = swap(f_ref[:, x]).astype(BF)
    if edge:
        copies[3].wait()
        for x in range(edge):
            e_ref[x] = o_ref[facing * (layers - edge) + x]
        e_ref[edge] = swap(n_ref[:, 0]).astype(BF)
    copies[1].wait()
    copies[2].wait()
    pack_weight(w_ref, b_ref, o_ref, layers)


def pack(field, weight, bias, name, beside=None, edge=0):
    group, layers, ny, nz = field.shape
    chan = weight.shape[1]
    taps = jnp.transpose(weight, (2, 3, 4, 0, 1)).reshape(27, group, chan)
    args = [field, taps, bias.reshape(1, group)]
    outs = [shape((layers + 16 // ny, ny, group, nz), BF)]
    scratch = [VM(field.shape, BF), VM((27, group, chan), BF), VM((1, group), F32)]
    if edge:
        args.append(beside)
        outs.append(shape((edge + 1, ny, group, nz), BF))
        scratch.append(VM((group, 1, ny, nz), BF))
    return pl.pallas_call(
        functools.partial(pack_kernel, edge),
        out_shape=tuple(outs),
        in_specs=[pl.BlockSpec(memory_space=pltpu.HBM)] * len(args),
        out_specs=(WHOLE,) * len(outs),
        scratch_shapes=scratch + [pltpu.SemaphoreType.DMA((len(args),))],
        compiler_params=pltpu.CompilerParams(vmem_limit_bytes=40 << 20),
        cost_estimate=pl.CostEstimate(flops=0, bytes_accessed=field.size * 4, transcendentals=0),
        name=name,
    )(*(pltpu.with_memory_space_constraint(v, pltpu.HBM) for v in args))


class Plan:
    def __init__(self, layers, ny, nz, chan, groups, spaces):
        self.layers, self.ny, self.nz, self.chan = layers, ny, nz, chan
        self.groups, self.spaces = groups, spaces
        self.group = chan // groups
        self.pair = spaces == 2
        self.quick = self.pair and groups == 4
        self.window = (2 if self.pair else 3) * layers
        self.sides = 1 if self.pair else 2

    def start(self, reach):
        if self.pair:
            return lax.axis_index("space") * (self.layers - reach)
        return self.layers - reach

    def count(self, reach):
        return self.layers + self.sides * reach

    def own(self):
        return self.start(0)

    def inside(self, layer):
        if self.pair:
            return None
        at = (lax.axis_index("space") - 1) * self.layers + layer
        return jnp.logical_and(at >= 0, at < self.spaces * self.layers)

    def chan_at(self, flip):
        return pl.multiple_of((lax.axis_index("filt") ^ flip) * self.group, self.group)

    def padded(self):
        return (self.window + 2, self.ny + 2, self.chan, self.nz)


def flip_perm(value, flip):
    n = lax.axis_size("filt")
    return lax.ppermute(value, "filt", [(i, i ^ flip) for i in range(n)])


def over(value):
    return lax.ppermute(value, "space", [(0, 1), (1, 0)])


def up(value):
    n = lax.axis_size("space")
    return lax.ppermute(value, "space", [(i, i + 1) for i in range(n - 1)])


def down(value):
    n = lax.axis_size("space")
    return lax.ppermute(value, "space", [(i + 1, i) for i in range(n - 1)])


def after(value, *others):
    return lax.optimization_barrier((value, *others))[0]


def gather_quick(volume, weight1, bias1, upstream, weight2, bias2, plan, early_layers):
    n = plan.layers
    packed, edge = pack(volume, weight1, bias1, "pack1", upstream, NEAR)
    x = flip_perm(packed, 2)
    y = over(edge)
    c = flip_perm(packed, 1)
    (second,) = pack(upstream, weight2, bias2, "pack2")
    y, x = lax.optimization_barrier((y, x, second))[:2]
    d = flip_perm(y, 2)
    xc = flip_perm(x, 1)
    yc = flip_perm(y, 1)
    x2 = flip_perm(second, 2)
    c2 = flip_perm(second, 1)
    early, ahead = early_layers([(v, 0, n, "own", 0, k) for k, v in enumerate([packed, c, x, xc])], (second, c2))
    dc = flip_perm(after(d, ahead[0]), 1)
    own, other, own2 = [packed, c, x, xc], [y, yc, d, dc], [second, c2, x2, x2]
    return (
        [(v, 0, n, "own", 0, k) for k, v in enumerate(own)],
        [(v, 0, NEAR, "other", 0, k) for k, v in enumerate(other)],
        [(v, 0, n, "own", 0, k) for k, v in enumerate(own2)],
        [(v, NEAR, 1, "halo", 0, k) for k, v in enumerate(other)],
        early,
        ahead,
    )


def gather_plain(volume, weight1, bias1, upstream, weight2, bias2, plan, early_layers):
    n = plan.layers
    (packed,) = pack(volume, weight1, bias1, "pack1")
    (second,) = pack(upstream, weight2, bias2, "pack2")
    own, other, own2, halo = [], [], [], []
    for flip in range(plan.groups):
        mine = flip_perm(packed, flip) if flip else packed
        mine2 = flip_perm(second, flip) if flip else second
        own.append((mine, 0, n, "own", 0, flip))
        own2.append((mine2, 0, n, "own", 0, flip))
        if plan.pair:
            facing = 1 - lax.axis_index("space")
            near = lax.dynamic_slice_in_dim(mine, facing * (n - NEAR), NEAR, axis=0)
            other.append((over(near), 0, NEAR, "other", 0, flip))
            near = lax.dynamic_slice_in_dim(mine2, facing * (n - 1), 1, axis=0)
            halo.append((over(near), 0, 1, "halo", 0, flip))
        else:
            other.append((up(mine[n - NEAR : n]), 0, NEAR, "low", 0, flip))
            other.append((down(mine[:NEAR]), 0, NEAR, "high", 0, flip))
            halo.append((up(mine2[n - 1 : n]), 0, 1, "low", 0, flip))
            halo.append((down(mine2[:1]), 0, 1, "high", 0, flip))
    return own, other, own2, halo, (), ()


def field_place(plan, place, k):
    n = plan.layers
    if plan.pair:
        s = lax.axis_index("space")
        return 1 + k + (s * n if place == "own" else n - NEAR * s)
    return 1 + k + {"low": n - NEAR, "own": n, "high": 2 * n}[place]


def halo_place(plan, place):
    if plan.pair:
        s = lax.axis_index("space")
        return s if place == "own" else (1 - s) * plan.layers
    return {"low": 0, "own": 1, "high": plan.layers + 1}[place]


def load_weight(plan, refs, dst, sem, start, flips=None):
    for n, ref in enumerate(refs):
        flip = flips[n] if flips else n
        copy = pltpu.make_async_copy(
            ref.at[pl.ds(ref.shape[0] - dst.shape[0], dst.shape[0])],
            dst.at[:, :, pl.ds(plan.chan_at(flip), plan.group), :],
            sem.at[n],
        )
        copy.start() if start else copy.wait()


def load_pieces(plan, refs, places, dst, sem, start, halo=False, near=False):
    for n, (ref, (first, count, place, k, flip)) in enumerate(zip(refs, places)):
        if near and place == "own":
            first = k = (1 - lax.axis_index("space")) * (plan.layers - 2)
            count = 2
        rows = pl.ds(plan.chan_at(flip), plan.group)
        if halo:
            target = dst.at[pl.ds(halo_place(plan, place), count), :, rows, :]
        else:
            target = dst.at[pl.ds(field_place(plan, place, k), count), pl.ds(1, plan.ny), rows, :]
        copy = pltpu.make_async_copy(ref.at[pl.ds(first, count)], target, sem.at[n])
        copy.start() if start else copy.wait()


def zero_rows(ref):
    zero = jnp.zeros(ref.shape[2:], ref.dtype)
    for x in range(ref.shape[0]):
        ref[x, 0] = zero
        ref[x, ref.shape[1] - 1] = zero


def zero_layer(ref, x):
    zero = jnp.zeros(ref.shape[2:], ref.dtype)
    for y in range(1, ref.shape[1] - 1):
        ref[x, y] = zero


def zero_edges(plan, ref):
    zero_rows(ref)
    zero_layer(ref, 0)
    zero_layer(ref, ref.shape[0] - 1)


def slot(w_ref, n, rows=slice(None)):
    return w_ref[n // w_ref.shape[1], n % w_ref.shape[1], rows, :]


def weight_matrix(w_ref, chan, rows=slice(None)):
    cols = []
    for pair in range(5):
        block = jnp.concatenate([slot(w_ref, 3 * pair + kz, rows) for kz in range(3)], axis=0)
        cols.append(block if pair < 4 else block[:, :chan])
    return jnp.concatenate(cols, axis=1)


def bias_column(w_ref, rows=slice(None)):
    terms = slot(w_ref, 15, rows).astype(F32)
    return terms[:, 0:1] + terms[:, 1:2] + terms[:, 2:3]


def taps(field_ref, x, y):
    c, nz = field_ref.shape[2], field_ref.shape[3]
    rows = []
    for kx in range(3):
        first = field_ref[x + kx, y : y + 3].reshape(3 * c, nz)
        second = field_ref[x + kx, y + 1 : y + 4].reshape(3 * c, nz)
        rows.append(jnp.concatenate([first, second], axis=1))
    return jnp.concatenate(rows, axis=0)


def z_shift(values, by):
    nz = values.shape[1]
    lane = lax.broadcasted_iota(jnp.int32, values.shape, 1)
    if by > 0:
        return jnp.where(lane == 0, 0.0, pltpu.roll(values, 1, 1))
    return jnp.where(lane == nz - 1, 0.0, pltpu.roll(values, nz - 1, 1))


def z_sum(product, rows, half, nz):
    part = product[:, half * nz : (half + 1) * nz]
    return part[rows : 2 * rows] + z_shift(part[:rows], 1) + z_shift(part[2 * rows :], -1)


def conv_rows(weight, field_ref, x, each):
    ny, nz = field_ref.shape[1] - 2, field_ref.shape[3]
    rows = weight.shape[0] // 3
    for y in range(0, ny, 2):
        product = jnp.dot(weight, taps(field_ref, x, y), preferred_element_type=F32)
        for half in range(2):
            each(y + half, z_sum(product, rows, half, nz))


def first_rows(plan, weight, bias, a_ref, start, count, put):
    def body(t, carry):
        x = start + t
        inside = plan.inside(x)

        def each(y, value):
            act, slope = parts(value + bias)
            if inside is not None:
                act = jnp.where(inside, act, 0.0)
            put(t, x, y, act.astype(BF), slope)

        conv_rows(weight, a_ref, x, each)
        return carry

    lax.fori_loop(0, count, body, 0, unroll=True)


def early_kernel(plan, places, *refs):
    n = len(places)
    pieces = refs[:n]
    h_ref, s_ref, a_ref, w_ref, sem, wsem = refs[n:]
    load_weight(plan, pieces[: plan.groups], w_ref, wsem, True)
    load_pieces(plan, pieces, places, a_ref, sem, True)
    zero_edges(plan, a_ref)
    load_weight(plan, pieces[: plan.groups], w_ref, wsem, False)
    load_pieces(plan, pieces, places, a_ref, sem, False)

    def put(t, x, y, act, slope):
        h_ref[t, y] = act
        s_ref[t, y] = slope

    start = lax.axis_index("space") * (plan.layers + 1)
    first_rows(plan, weight_matrix(w_ref, plan.chan), bias_column(w_ref), a_ref, start, plan.layers - 1, put)


def first_kernel(plan, places, *refs):
    n = len(places)
    pieces, refs = refs[:n], refs[n:]
    if plan.quick:
        eh_ref, es_ref, refs = refs[0], refs[1], refs[2:]
    h_ref, s_ref, a_ref, w_ref, sem, wsem, esem = refs
    load_weight(plan, pieces[: plan.groups], w_ref, wsem, True)
    load_pieces(plan, pieces, places, a_ref, sem, True, near=plan.quick)
    zero_edges(plan, a_ref)
    zero_edges(plan, h_ref)
    base = plan.start(2)
    start, count = base, plan.count(2)
    copies = []
    if plan.quick:
        s = lax.axis_index("space")
        done = s * (plan.layers + 1)
        start, count = plan.layers - 1 - s, count - plan.layers + 1
        copies = [
            pltpu.make_async_copy(
                eh_ref, h_ref.at[pl.ds(done + 1, plan.layers - 1), pl.ds(1, plan.ny)], esem.at[0]
            ),
            pltpu.make_async_copy(es_ref, s_ref.at[pl.ds(done - base, plan.layers - 1)], esem.at[1]),
        ]
    for copy in copies:
        copy.start()
    load_weight(plan, pieces[: plan.groups], w_ref, wsem, False)
    load_pieces(plan, pieces, places, a_ref, sem, False, near=plan.quick)

    def put(t, x, y, act, slope):
        h_ref[x + 1, y + 1] = act
        s_ref[x - base, y] = slope

    first_rows(plan, weight_matrix(w_ref, plan.chan), bias_column(w_ref), a_ref, start, count, put)
    for copy in copies:
        copy.wait()


def grad_sums(plan, count, get, f_ref, base, sh_ref):
    group, nz, ny, chan = plan.group, plan.nz, plan.ny, plan.chan
    zero = jnp.zeros((3 * group, nz), BF)
    total = jnp.zeros((group, nz), F32)
    sums = jnp.zeros((9 * group, 3 * chan), F32)
    for t in range(count):
        sh_ref[t, 0] = zero
        sh_ref[t, ny + 1] = zero
        for y in range(ny):
            value = get(t, y).astype(F32)
            total = total + value
            sh_ref[t, y + 1] = jnp.concatenate([z_shift(value, -1), value, z_shift(value, 1)], axis=0).astype(BF)
    for t in range(count):
        left = jnp.concatenate(
            [jnp.concatenate([sh_ref[t, y + 2 - ky] for y in range(ny)], axis=1) for ky in range(3)], axis=0
        )
        right = jnp.concatenate(
            [jnp.concatenate([f_ref[base + t + kx, y + 1] for y in range(ny)], axis=1) for kx in range(3)], axis=0
        )
        sums += lax.dot_general(left, right, (((1,), (1,)), ((), ())), preferred_element_type=F32)
    return sums, total


def pack_grads(plan, sums, total, acc_ref, g_ref):
    group, chan = plan.group, plan.chan
    acc_ref[...] = sums
    n = 9 * group
    g_ref[0:n] = acc_ref[:, 0 : 2 * chan]
    last = acc_ref[:, 2 * chan :]
    g_ref[n : n + n // 2] = jnp.concatenate([last[: n // 2], last[n // 2 :]], axis=1)
    g_ref[n + n // 2 :] = jnp.broadcast_to(jnp.sum(total, axis=1, keepdims=True), (group, 2 * chan))


def grads(plan, get, f_ref, sh_ref, acc_ref, g_ref):
    rows = pl.ds(plan.chan_at(0), plan.group)
    sums, total = grad_sums(plan, plan.layers, lambda t, y: get(t, y, rows), f_ref, plan.own(), sh_ref)
    pack_grads(plan, sums, total, acc_ref, g_ref)


def second_rows(plan, rows, h_ref, u_ref, w_ref, put, first, count, layer):
    matrix = weight_matrix(w_ref, plan.chan, rows)
    bias = bias_column(w_ref, rows)
    for n in range(count):

        def each(y, value, t=first + n, x=layer + n):
            pre = value + bias
            delta = (u_ref[t, y, rows, :].astype(F32) * slope_of(pre)).astype(BF)
            put(t, x, y, pre, delta)

        conv_rows(matrix, h_ref, layer + n, each)


def put_output(plan, p_ref, rows, o_ref):
    first = plan.own() - plan.start(1)
    for t in range(plan.layers):
        o_ref[:, t] = jnp.transpose(smooth(p_ref[first + t, :, rows, :]), (1, 0, 2)).astype(BF)


def second_kernel(plan, places, *refs):
    n = len(places)
    pieces = refs[:n]
    weights = pieces[: plan.groups]
    h_ref, d_ref, o_ref, g_ref, t_ref, u_ref, w_ref, p_ref, sh_ref, acc_ref, sem, wsem = refs[n:]
    load_weight(plan, weights, w_ref, wsem, True)
    load_pieces(plan, pieces, places, u_ref, sem, True, halo=True)
    zero_edges(plan, d_ref)
    load_weight(plan, weights, w_ref, wsem, False)
    turn(w_ref, t_ref, plan.chan)
    load_pieces(plan, pieces, places, u_ref, sem, False, halo=True)

    def put(t, x, y, pre, delta):
        p_ref[t, y] = pre
        d_ref[x + 1, y + 1] = delta

    second_rows(plan, pl.ds(0, plan.chan), h_ref, u_ref, w_ref, put, 0, plan.count(1), plan.start(1))
    put_output(plan, p_ref, pl.ds(plan.chan_at(0), plan.group), o_ref)
    own = plan.own()
    grads(plan, lambda t, y, rows: d_ref[own + t + 1, y + 1, rows, :], h_ref, sh_ref, acc_ref, g_ref)


def chip_rows(plan, other):
    half = plan.chan // 2
    return pl.ds(pl.multiple_of(((lax.axis_index("filt") >> 1) ^ other) * half, half), half)


def own_rows(plan):
    return pl.ds(pl.multiple_of((lax.axis_index("filt") & 1) * plan.group, plan.group), plan.group)


def ahead_kernel(plan, eh_hbm, own_hbm, chip_hbm, d_ref, o_ref, a_ref, b_ref, h_ref, u_ref, w_ref, p_ref, sh_ref, sem, wsem):
    s = lax.axis_index("space")
    count = plan.layers - 2
    load_weight(plan, (own_hbm, chip_hbm), w_ref, wsem, True, (0, 1))
    copies = [
        pltpu.make_async_copy(eh_hbm, h_ref.at[pl.ds(1 - s, count + 1), pl.ds(1, plan.ny)], sem.at[2])
    ]
    for flip, ref in enumerate((own_hbm, chip_hbm)):
        target = u_ref.at[:, :, pl.ds(plan.chan_at(flip), plan.group), :]
        copies.append(pltpu.make_async_copy(ref.at[pl.ds(2 * s, count)], target, sem.at[flip]))
    for copy in copies:
        copy.start()
    zero_rows(h_ref)
    zero_layer(h_ref, s * (count + 1))
    load_weight(plan, (own_hbm, chip_hbm), w_ref, wsem, False, (0, 1))
    for copy in copies:
        copy.wait()

    def put(t, x, y, pre, delta):
        p_ref[t, y] = pre
        d_ref[t, y] = delta

    second_rows(plan, chip_rows(plan, 0), h_ref, u_ref, w_ref, put, 0, count, 0)
    mine = own_rows(plan)
    for t in range(count):
        o_ref[:, t] = jnp.transpose(smooth(p_ref[t, :, mine, :]), (1, 0, 2)).astype(BF)
    a_ref[...], b_ref[...] = grad_sums(plan, count, lambda t, y: d_ref[t, y, mine, :], h_ref, 0, sh_ref)


def near_kernel(plan, places, *refs):
    n = len(places)
    pieces, ahead, refs = refs[:n], refs[n], refs[n + 1 :]
    h_ref, ao_ref, aa_ref, ab_ref, d_ref, o_ref, g_ref, u_ref, w_ref, p_ref, sh_ref, acc_ref, sem, wsem, asem = refs
    s = lax.axis_index("space")
    done = plan.layers - 2
    left = plan.count(1) - done
    load_weight(plan, pieces[:2], w_ref, wsem, True, (0, 1))
    load_pieces(plan, pieces, places, u_ref, sem, True, halo=True)
    copy = pltpu.make_async_copy(ahead, d_ref.at[pl.ds(s * left, done)], asem)
    copy.start()
    load_weight(plan, pieces[:2], w_ref, wsem, False, (0, 1))
    load_pieces(plan, pieces, places, u_ref, sem, False, halo=True)

    def put(t, x, y, pre, delta):
        p_ref[t, y] = pre
        d_ref[t, y] = delta

    start, first, slab = plan.start(1), (1 - s) * done, (1 - s) * done
    second_rows(plan, chip_rows(plan, 0), h_ref, u_ref, w_ref, put, first, left, start + first)
    mine = own_rows(plan)
    o_ref[:, pl.ds(2 * s, done)] = ao_ref[...]
    at = plan.own() - start + slab
    for t in range(2):
        value = jnp.transpose(smooth(p_ref[at + t, :, mine, :]), (1, 0, 2)).astype(BF)
        o_ref[:, pl.ds(slab + t, 1)] = value[:, None]
    sums, total = grad_sums(plan, 2, lambda t, y: d_ref[at + t, y, mine, :], h_ref, plan.own() + slab, sh_ref)
    pack_grads(plan, sums + aa_ref[...], total + ab_ref[...], acc_ref, g_ref)
    copy.wait()


def far_kernel(plan, places, *refs):
    n = len(places)
    pieces, weights, refs = refs[:n], refs[n : n + 4], refs[n + 4 :]
    near_ref, h_ref, d_ref, t_ref, u_ref, w_ref, sem, wsem, nsem = refs
    load_weight(plan, weights, w_ref, wsem, True)
    load_pieces(plan, pieces, places, u_ref, sem, True, halo=True)
    joined = d_ref.at[pl.ds(plan.start(1) + 1, plan.count(1)), pl.ds(1, plan.ny), chip_rows(plan, 0), :]
    copy = pltpu.make_async_copy(near_ref, joined, nsem)
    copy.start()
    zero_edges(plan, d_ref)
    load_weight(plan, weights, w_ref, wsem, False)
    turn(w_ref, t_ref, plan.chan)
    load_pieces(plan, pieces, places, u_ref, sem, False, halo=True)
    rows = chip_rows(plan, 1)

    def put(t, x, y, pre, delta):
        d_ref[x + 1, y + 1, rows, :] = delta

    second_rows(plan, rows, h_ref, u_ref, w_ref, put, 0, plan.count(1), plan.start(1))
    copy.wait()


def turn(w_ref, out, chan):
    for kz in range(3):
        turned = [jnp.transpose(slot(w_ref, 3 * pair + 2 - kz).astype(F32), (1, 0)) for pair in range(5)]
        for pair in range(5):
            low = turned[4 - pair][:chan]
            if pair < 4:
                block = jnp.concatenate([low, turned[3 - pair][chan:]], axis=1)
                out[kz, :, 2 * chan * pair : 2 * chan * (pair + 1)] = block.astype(BF)
            else:
                out[kz, :, 2 * chan * pair :] = low.astype(BF)


def turn_kernel(plan, *refs):
    out, w_ref, sem = refs[plan.groups :]
    for go in (True, False):
        load_weight(plan, refs[: plan.groups], w_ref, sem, go)
    turn(w_ref, out, plan.chan)


def third_kernel(plan, places, *refs):
    n = len(places)
    pieces = refs[:n]
    s_ref, d2_ref, t_ref, d_ref, g_ref, a_ref, sh_ref, acc_ref, sem = refs[n:]
    load_pieces(plan, pieces, places, a_ref, sem, True)
    zero_edges(plan, a_ref)
    start = plan.own()
    skip = start - plan.start(2)
    m_ref = t_ref[...].reshape(3 * plan.chan, 9 * plan.chan)

    def body(t, carry):
        def each(y, value):
            d_ref[t, y] = (value * s_ref[skip + t, y]).astype(BF)

        conv_rows(m_ref, d2_ref, start + t, each)
        return carry

    lax.fori_loop(0, plan.layers, body, 0, unroll=True)
    load_pieces(plan, pieces, places, a_ref, sem, False)
    grads(plan, lambda t, y, rows: d_ref[t, y, rows, :], a_ref, sh_ref, acc_ref, g_ref)


def fourth_kernel(plan, d_ref, t_ref, r_ref, *refs):
    *outs, a_ref, sem = refs
    layers, ny = plan.layers, plan.ny
    copy = pltpu.make_async_copy(d_ref, a_ref.at[pl.ds(2, layers), pl.ds(1, ny)], sem)
    copy.start()
    zero_rows(a_ref)
    for x in (0, 1, layers + 2, layers + 3):
        zero_layer(a_ref, x)
    copy.wait()
    rows = pl.ds(plan.chan_at(0), plan.group)
    m_ref = t_ref[:, rows, :].reshape(3 * plan.group, 9 * plan.chan)
    for t in range(layers):

        def each(y, value, t=t):
            r_ref[t, y] = value

        conv_rows(m_ref, a_ref, t + 1, each)
    if plan.pair:
        places = [(1 - lax.axis_index("space")) * (layers + 1)]
    else:
        places = [0, layers + 1]
    for out, place in zip(outs, places):

        def beside(y, value, out=out):
            out[y * plan.group : (y + 1) * plan.group] = value.astype(BF)

        conv_rows(m_ref, a_ref, place, beside)


def finish_volume(plan, r_ref, shares, o_ref):
    layers, ny, group = plan.layers, plan.ny, plan.group
    for layer, ref, base in shares:
        for y in range(ny):
            r_ref[layer, y] += ref[base + y * group : base + (y + 1) * group].astype(F32)
    for t in range(layers):
        o_ref[:, t] = jnp.transpose(r_ref[t], (1, 0, 2)).astype(BF)


def finish_kernel(plan, r_hbm, low_ref, high_ref, o_ref, r_ref, sem):
    copy = pltpu.make_async_copy(r_hbm, r_ref, sem)
    copy.start()
    copy.wait()
    finish_volume(plan, r_ref, [(0, low_ref, 0), (plan.layers - 1, high_ref, 0)], o_ref)


def to_wire(values, rows):
    row = lax.broadcasted_iota(jnp.int32, values.shape, 0)
    lane = lax.broadcasted_iota(jnp.int32, values.shape, 1)
    high = values.astype(BF).astype(F32)
    second = jnp.logical_and(row >= rows, lane >= values.shape[1] // 2)
    return jnp.where(second, values - high, high).astype(BF)


def add_wire(values, wire, rows):
    got = wire.astype(F32)
    row = lax.broadcasted_iota(jnp.int32, values.shape, 0)
    return values + got + jnp.where(row >= rows, pltpu.roll(got, values.shape[1] // 2, 1), 0.0)


def wire_kernel(rows, a_ref, w_ref):
    w_ref[...] = to_wire(a_ref[...], rows)


def step_kernel(rows, a_ref, got_ref, o_ref, w_ref):
    total = add_wire(a_ref[...], got_ref[...], rows)
    o_ref[...] = total
    w_ref[...] = to_wire(total, rows)


def join_kernel(rows, a_ref, got_ref, share_ref, o_ref, w_ref):
    total = add_wire(a_ref[...], got_ref[...], rows)
    o_ref[...] = total
    w_ref[: total.shape[0]] = to_wire(total, rows)
    w_ref[total.shape[0] :] = share_ref[...]


def close_kernel(plan, rows, scale, r_hbm, a2_ref, got2_ref, out_ref, *refs):
    w2_ref, b2_ref, o_ref, out2_ref, r_ref, sem = refs
    copy = pltpu.make_async_copy(r_hbm, r_ref, sem)
    copy.start()
    out2_ref[...] = out_ref[...]
    last_kernel(rows, plan.group, scale, a2_ref, got2_ref, w2_ref, b2_ref)
    copy.wait()
    layer = (1 - lax.axis_index("space")) * (plan.layers - 1)
    finish_volume(plan, r_ref, [(layer, got2_ref, a2_ref.shape[0])], o_ref)


def last_kernel(rows, group, scale, a_ref, got_ref, w_ref, b_ref):
    total = add_wire(a_ref[...], got_ref[: a_ref.shape[0]], rows) * scale
    n = 9 * group
    chan = total.shape[1] // 2
    w_ref[0:9] = total[:n, :chan].reshape(9, group, chan)
    w_ref[9:18] = total[:n, chan:].reshape(9, group, chan)
    tail = total[n : n + n // 2]
    w_ref[18:27] = jnp.concatenate([tail[:, :chan], tail[:, chan:]], axis=0).reshape(9, group, chan)
    col = total[rows:, :group]
    eye = lax.broadcasted_iota(jnp.int32, (group, group), 0) == lax.broadcasted_iota(
        jnp.int32, (group, group), 1
    )
    b_ref[...] = jnp.sum(jnp.where(eye, col, 0.0), axis=0, keepdims=True)


def rounds(plan):
    out = []
    for axis in ("space", "rep"):
        size, bit = lax.axis_size(axis), 1
        while bit < size:
            out.append((axis, bit))
            bit *= 2
    return out


def exchange(wire, step):
    axis, bit = step
    return lax.ppermute(wire, axis, [(i, i ^ bit) for i in range(lax.axis_size(axis))])


def first_wire(part, plan):
    rows = part.shape[0] - plan.group
    return call(functools.partial(wire_kernel, rows), shape(part.shape, BF), 0, 1, name="wire")(part)


def grad_shapes(plan):
    return shape((27, plan.group, plan.chan), F32), shape((1, plan.group), F32)


def as_grads(weight, bias, plan):
    weight = jnp.transpose(weight.reshape(3, 3, 3, plan.group, plan.chan), (3, 4, 0, 1, 2))
    return weight, bias.reshape(plan.group)


def total_step(part, got, step, plan, share=None):
    rows = part.shape[0] - plan.group
    kernel, args, more = step_kernel, (part, got), 0
    if share is not None:
        kernel, args, more = join_kernel, (part, got, share), share.shape[0]
    part, wire = call(
        functools.partial(kernel, rows),
        (shape(part.shape, F32), shape((part.shape[0] + more, part.shape[1]), BF)),
        0,
        len(args),
        name="step",
    )(*args)
    return part, exchange(wire, step)


def total_last(part, got, plan, scale):
    rows = part.shape[0] - plan.group
    weight, bias = call(
        functools.partial(last_kernel, rows, plan.group, scale), grad_shapes(plan), 0, 2, name="last"
    )(part, got)
    return as_grads(weight, bias, plan)


def local(volume, weight1, bias1, weight2, bias2, upstream):
    _, group, layers, ny, nz = volume.shape
    chan = weight1.shape[1]
    spaces, groups = lax.axis_size("space"), lax.axis_size("filt")
    plan = Plan(layers, ny, nz, chan, groups, spaces)
    scale = 1.0 / math.sqrt(lax.axis_size("rep") * spaces * layers * ny * nz)

    cells = ny * nz
    conv = 2 * 27 * chan * chan * cells
    slots = VM((16 // ny, ny, chan, 2 * chan), BF)
    dma = pltpu.SemaphoreType.DMA
    padded = plan.padded()
    grad_rows = 27 * group // 2 + group
    grad_scratch = [VM((layers, ny + 2, 3 * group, nz), BF), VM((9 * group, 3 * chan), F32)]

    half = lambda n: (n, ny, chan // 2, nz)

    def early_layers(pieces, pieces2):
        early = call(
            functools.partial(early_kernel, plan, [p[1:] for p in pieces]),
            (shape((layers - 1, ny, chan, nz), BF), shape((layers - 1, ny, chan, nz), F32)),
            len(pieces),
            0,
            [VM(padded, BF), slots, dma((len(pieces),)), dma((groups,))],
            flops=1,
            name="early",
        )(*(p[0] for p in pieces))
        some = layers - 2
        ahead, ahead_output, ahead_sums, ahead_total = call(
            functools.partial(ahead_kernel, plan),
            (
                shape(half(some), BF),
                shape((group, some, ny, nz), BF),
                shape((9 * group, 3 * chan), F32),
                shape((group, nz), F32),
            ),
            3,
            0,
            [
                VM((layers, ny + 2, chan, nz), BF),
                VM((some, ny, chan, nz), BF),
                slots,
                VM(half(some), F32),
                VM((some, ny + 2, 3 * group, nz), BF),
                dma((3,)),
                dma((2,)),
            ],
            flops=1,
            name="ahead",
        )(early[0], *pieces2)
        return early, (ahead, ahead_output, ahead_sums, ahead_total)

    gather = gather_quick if plan.quick else gather_plain
    v_own, v_other, u_own, u_other, early, ahead = gather(
        volume[0], weight1, bias1, upstream[0], weight2, bias2, plan, early_layers
    )
    v_places = [p[1:] for p in v_own + v_other]
    u_places = [p[1:] for p in u_own + u_other]
    v_all = [p[0] for p in v_own + v_other]
    u_all = [p[0] for p in u_own + u_other]

    turned1 = call(
        functools.partial(turn_kernel, plan),
        shape((3, chan, 9 * chan), BF),
        groups,
        0,
        [slots, dma((groups,))],
        moved=2 << 20,
        name="turn",
    )(*v_all[:groups])

    hidden, slope = call(
        functools.partial(first_kernel, plan, v_places),
        (shape(padded, BF), shape((plan.count(2), ny, chan, nz), F32)),
        len(v_all) + len(early),
        0,
        [VM(padded, BF), slots, dma((len(v_all),)), dma((groups,)), dma((2,))],
        flops=1,
        name="first",
    )(*v_all, *early)

    if plan.quick:
        u_all[3] = flip_perm(after(u_all[2], hidden), 1)
        here, there = (0, 1, 4, 5), (2, 3, 6, 7)
        near2, output, part2 = call(
            functools.partial(near_kernel, plan, [u_places[k] for k in here]),
            (
                shape(half(plan.count(1)), BF),
                shape((group, layers, ny, nz), BF),
                shape((grad_rows, 2 * chan), F32),
            ),
            5,
            4,
            [
                VM((plan.count(1), ny, chan, nz), BF),
                slots,
                VM(half(plan.count(1)), F32),
                *grad_scratch,
                dma((4,)),
                dma((2,)),
                dma,
            ],
            flops=1,
            name="near",
        )(*(u_all[k] for k in here), ahead[0], hidden, *ahead[1:])
        delta2, turned2 = call(
            functools.partial(far_kernel, plan, [u_places[k] for k in there]),
            (shape(padded, BF), shape((3, chan, 9 * chan), BF)),
            9,
            1,
            [VM((plan.count(1), ny, chan, nz), BF), slots, dma((4,)), dma((4,)), dma],
            flops=1,
            name="far",
        )(*(u_all[k] for k in there), *u_all[:4], near2, hidden)
    else:
        delta2, output, part2, turned2 = call(
            functools.partial(second_kernel, plan, u_places),
            (
                shape(padded, BF),
                shape((group, layers, ny, nz), BF),
                shape((grad_rows, 2 * chan), F32),
                shape((3, chan, 9 * chan), BF),
            ),
            len(u_all),
            1,
            [
                VM((plan.count(1), ny, chan, nz), BF),
                slots,
                VM((plan.count(1), ny, chan, nz), F32),
                *grad_scratch,
                dma((len(u_all),)),
                dma((groups,)),
            ],
            flops=1,
            name="second",
        )(*u_all, hidden)

    delta1, part1 = call(
        functools.partial(third_kernel, plan, v_places),
        (shape((layers, ny, chan, nz), BF), shape((grad_rows, 2 * chan), F32)),
        len(v_all),
        3,
        [VM(padded, BF), *grad_scratch, dma((len(v_all),))],
        flops=1,
        name="third",
    )(*v_all, slope, delta2, turned2)

    beside = [shape((ny * group, nz), BF)] * plan.sides
    own_grad, *shares = call(
        functools.partial(fourth_kernel, plan),
        (shape((layers, ny, group, nz), F32), *beside),
        1,
        1,
        [VM((layers + 4, ny + 2, chan, nz), BF), dma],
        flops=1,
        name="fourth",
    )(delta1, turned1)

    steps1 = rounds(plan)
    steps2 = steps1[1:] + steps1[:1]
    got1 = exchange(first_wire(part1, plan), steps1[0])
    got2 = exchange(first_wire(after(part2, delta2), plan), steps2[0])
    for step in steps1[1:]:
        part1, got1 = total_step(part1, got1, step, plan)
    for n, step in enumerate(steps2[1:], 2):
        share = shares[0] if plan.pair and n == len(steps2) else None
        part2, got2 = total_step(part2, got2, step, plan, share)
    volume_shape = shape((group, layers, ny, nz), BF)
    finish_scratch = [VM((layers, ny, group, nz), F32), dma]
    if plan.pair:
        w2, b2, volume_grad, output = call(
            functools.partial(close_kernel, plan, part2.shape[0] - group, scale),
            (*grad_shapes(plan), volume_shape, volume_shape),
            1,
            3,
            finish_scratch,
            name="close",
        )(own_grad, part2, got2, output)
        grad1, bias_grad1 = total_last(after(part1, w2), got1, plan, scale)
        grad2, bias_grad2 = as_grads(w2, b2, plan)
    else:
        grad1, bias_grad1 = total_last(part1, got1, plan, scale)
        grad2, bias_grad2 = total_last(part2, got2, plan, scale)
        volume_grad = call(
            functools.partial(finish_kernel, plan), volume_shape, 1, 2, finish_scratch, name="finish"
        )(own_grad, up(shares[1]), down(shares[0]))
    return (output[None], volume_grad[None], grad1, bias_grad1, grad2, bias_grad2)


def solution(mesh):
    field = P("rep", "filt", "space", None, None)
    kernel = P("filt", None, None, None, None)
    return jax.shard_map(
        local,
        mesh=mesh,
        in_specs=(field, kernel, P("filt"), kernel, P("filt"), field),
        out_specs=(field, field, kernel, P("filt"), kernel, P("filt")),
        check_vma=False,
    )
```
